512 devices in a mesh: tm: 256 (over z, y, x), state: 2 (over core).
Axes of the slice: x: 4, y: 4, z: 16, core: 2. Of those that a mesh axis runs over, the one named last changes fastest.
Arguments:
- record: bfloat16 [32768, 4096], P('tm', 'state'), may hold values from -24 to 24
- gain: bfloat16 [2, 256, 4096], P(None, 'state'), may hold values from -0.0625 to 0.0625
- rate: float32 [256, 32768], P('state', 'tm'), as said below
- leak: float32 [256], P('state'), may hold values from 1.5258789e-05 to 0.05
- dilation: int32 [2], replicated, may hold values from 0 to 64, as said below
Outputs:
- smoothed: float32 [256, 32768], P('state', 'tm')
- grad: float32 [4096, 512], P(('state', 'tm'))
The draws below stay inside these ranges and needn't reach their ends.
Inputs may be any that keep to these rules, and one draw needn't show every extreme that they name: `dilation`: delays of the taps; the largest of them equals 64. `rate`: positive rates.
All inputs are finite; a program needn't handle non-finite values.
Results may differ from the reference program's by a relative error of at most 0.0014.
Values may be sent and summed in bfloat16 or wider, within the bound.
No kernel may reach another device: no remote copies, remote signals or barrier semaphores. Data moves between devices by JAX's collectives and lax.ppermute only.
A program may use at most 64 MiB of HBM per device.

```python
import math
import jax
import jax.numpy as jnp
from jax import lax

LATENT_COMPONENTS = 256
Y = 4096
TAPS = 2
DMAX = 64
SAMPLE_COUNT = 32768


def draw_rate(key, part):
    sampler_seeds = jax.random.split(key, 7)
    slow_share = 0.5
    slow = jax.random.uniform(sampler_seeds[0], (LATENT_COMPONENTS, 1)) < slow_share
    slow_rate = jnp.exp(jax.random.uniform(sampler_seeds[1], (LATENT_COMPONENTS, 1), minval=jnp.log(0.2), maxval=jnp.log(1.5))) / SAMPLE_COUNT
    fast_rate = jnp.exp(jax.random.uniform(sampler_seeds[2], (LATENT_COMPONENTS, 1), minval=jnp.log(1.0 / 50.0), maxval=jnp.log(1.0 / 30.0)))
    floor_offset = jnp.where(slow, slow_rate, fast_rate)
    segment_factor = jnp.exp(jax.random.uniform(sampler_seeds[3], (LATENT_COMPONENTS, SAMPLE_COUNT // 8), minval=-0.69, maxval=0.69))
    segment_factor = jnp.repeat(segment_factor, 8, axis=1)
    jitter_disturbance = jax.random.uniform(sampler_seeds[4], (LATENT_COMPONENTS, SAMPLE_COUNT), minval=0.6, maxval=1.4)
    pulse_location = jax.random.uniform(sampler_seeds[5], (1, SAMPLE_COUNT)) < 6.0 / SAMPLE_COUNT
    pulse_height = jnp.where(pulse_location, jax.random.uniform(sampler_seeds[6], (LATENT_COMPONENTS, SAMPLE_COUNT), minval=0.22, maxval=0.7), 0.0)
    return (floor_offset * segment_factor * jitter_disturbance + pulse_height).astype(jnp.float32)


def draw_dilation(key, part):
    sampler_seeds = jax.random.split(key, 2)
    values = jax.random.randint(sampler_seeds[0], (TAPS,), 0, DMAX)
    where_most = jax.random.randint(sampler_seeds[1], (), 0, TAPS)
    return jnp.where(jnp.arange(TAPS) == where_most, DMAX, values).astype(jnp.int32)


def raised(array, rng, source, target, shards_of, factor):
    def block_of(position):
        return (jnp.arange(array.shape[position]) // (array.shape[position] // shards_of)).reshape((-1,) + (1,) * (array.ndim - 1 - position))

    one_side = jax.random.permutation(rng, shards_of)[block_of(target)]
    second = (block_of(target) + shards_of // 2) % shards_of
    return jnp.where((block_of(source) == one_side) | (block_of(source) == second), factor * array, array)


def steps_of(stream_key, extent, cuts, smallest, high):
    def one(position, blocks):
        steps = jax.random.uniform(jax.random.fold_in(jax.random.fold_in(stream_key, 6), position), (blocks,), jnp.float32, smallest / len(cuts), high / len(cuts))
        return jnp.repeat(jnp.exp(steps), extent[position] // blocks).reshape((-1,) + (1,) * (len(extent) - position - 1))

    level = one(*cuts[0])
    for cut in cuts[1:]:
        level = level * one(*cut)
    return level


def scatter_about(own_key, dims, width, reach, shards=(), kind=jnp.bfloat16):
    entries = jax.random.normal(own_key, dims, jnp.float32) * width
    if len(shards) > 0:
        entries = steps_of(own_key, dims, shards, -0.22, 0.18) * entries
    return jnp.clip(entries, min=-reach, max=reach).astype(kind)


def bell_draw_with(rng, shape, deviation, reach, cuts, heavy, kind=jnp.bfloat16):
    drawn = deviation * jax.random.normal(rng, shape, jnp.float32)
    if cuts:
        drawn = drawn * steps_of(rng, shape, cuts, -0.22, 0.18)
    return jnp.clip(raised(drawn, jax.random.fold_in(rng, 3), *heavy), -reach, reach).astype(kind)


def setup_inputs(seed: int = 0) -> dict:
    key_list = jax.random.split(jax.random.key(seed), 6)
    return {
        "record": bell_draw_with(key_list[0], (SAMPLE_COUNT, Y), 1.0, 24.0, ((0, 256), (1, 2)), (0, 1, 256, 6.0)),
        "gain": scatter_about(key_list[1], (TAPS, LATENT_COMPONENTS, Y), (TAPS * Y) ** -0.5, 0.0625, ((1, 2),)),
        "rate": draw_rate(jax.random.fold_in(key_list[5], 71), 0),
        "leak": jnp.clip(jnp.exp(math.log(0.05) - 8.094623 * jax.random.uniform(key_list[3], (LATENT_COMPONENTS,), jnp.float32) ** steps_of(key_list[3], (LATENT_COMPONENTS,), ((0, 2),), -0.2, 0.2)), 1.52587890625e-05, 0.05),
        "dilation": draw_dilation(jax.random.fold_in(key_list[5], 71), 0),
    }


def delayed_rows(padded, shift):
    return lax.dynamic_slice_in_dim(padded, (DMAX - shift).astype(jnp.int32), SAMPLE_COUNT, 0)

def reference(record, gain, rate, leak, dilation):
    padded = jnp.concatenate([jnp.zeros((DMAX, Y), jnp.bfloat16), record], 0)
    drive_in = jnp.zeros((LATENT_COMPONENTS, SAMPLE_COUNT), jnp.float32)
    for k in range(TAPS):
        delayed = delayed_rows(padded, dilation[k])
        drive_in = drive_in + lax.dot_general(gain[k], delayed, (((1,), (1,)), ((), ())), preferred_element_type=jnp.float32)
    decay = jnp.exp(-rate)
    scale = jnp.sqrt(-jnp.expm1(-2.0 * rate))
    drive = scale * drive_in

    def forward(state_now, inputs):
        decay_col, drive_col = inputs
        state_now = decay_col * state_now + drive_col
        return (state_now, state_now)
    _, filtered = lax.scan(forward, jnp.zeros((LATENT_COMPONENTS,), jnp.float32), (decay.T, drive.T))
    filtered = filtered.T
    kappa = 1.0 - leak
    link = kappa[:, None] * decay
    weight = (1.0 - kappa[:, None] * decay * decay) * filtered

    def backward(state_now, inputs):
        link_col, weight_col = inputs
        state_now = link_col * state_now + weight_col
        return (state_now, state_now)
    _, smoothed = lax.scan(backward, jnp.zeros((LATENT_COMPONENTS,), jnp.float32), (link.T, weight.T), reverse=True)
    smoothed = smoothed.T
    shifted = jnp.concatenate([jnp.zeros((LATENT_COMPONENTS, 1), jnp.float32), smoothed[:, :-1]], 1)
    resid = (smoothed - decay * shifted - drive).astype(jnp.bfloat16)
    pieces = []
    for k in range(TAPS):
        delayed = delayed_rows(padded, dilation[k])
        pieces.append(lax.dot_general(delayed, resid, (((0,), (1,)), ((), ())), preferred_element_type=jnp.float32))
    return (smoothed, jnp.concatenate(pieces, 1))
```

```python
import jax
import jax.numpy as jnp
from jax import lax
from jax.experimental import pallas as pl
from jax.experimental.pallas import tpu as pltpu
from jax.sharding import Mesh
from jax.sharding import PartitionSpec as P

TAPS = 2
DMAX = 64
Z = "tm_0"
YX = ("tm_1", "tm_2")
TM = ("tm_0", "tm_1", "tm_2")
STATE_TM = ("state", "tm_0", "tm_1", "tm_2")
F32 = jnp.float32
BF16 = jnp.bfloat16
VMEM = pl.BlockSpec(memory_space=pltpu.VMEM)
SMEM = pl.BlockSpec(memory_space=pltpu.SMEM)
NT = (((1,), (1,)), ((), ()))


def call(body, outs, scratch=(), smem=(0,), n_in=1):
    specs = [SMEM if i in smem else VMEM for i in range(n_in)]
    return pl.pallas_call(
        body,
        out_shape=outs,
        in_specs=specs,
        out_specs=jax.tree.map(lambda _: VMEM, outs),
        scratch_shapes=scratch,
        compiler_params=pltpu.CompilerParams(vmem_limit_bytes=48 << 20),
    )


def later(x, k, fill):
    if k % 8 == 0:
        return jnp.concatenate([jnp.full((k, x.shape[1]), fill, x.dtype), x[:-k]], 0)
    row = lax.broadcasted_iota(jnp.int32, x.shape, 0)
    return jnp.where(row < k, fill, pltpu.roll(x, k, 0))


def earlier(x, k, fill):
    n = x.shape[0]
    if k % 8 == 0:
        return jnp.concatenate([x[k:], jnp.full((k, x.shape[1]), fill, x.dtype)], 0)
    row = lax.broadcasted_iota(jnp.int32, x.shape, 0)
    return jnp.where(row >= n - k, fill, pltpu.roll(x, n - k, 0))


def recur(link, sums, shift):
    k = 1
    while k < link.shape[0]:
        sums = [s + link * shift(s, k, 0.0) for s in sums]
        link = link * shift(link, k, 1.0)
        k *= 2
    return link, sums


def taps_body(where, own, other, gain, out):
    modes = gain.shape[1]
    half = own.shape[1]
    mine = pl.multiple_of(where[2] * half, half)
    theirs = pl.multiple_of((1 - where[2]) * half, half)
    for k in range(TAPS):
        out[:, k * modes : (k + 1) * modes] = lax.dot_general(
            own[...], gain[k, :, pl.ds(mine, half)], NT, preferred_element_type=F32
        ) + lax.dot_general(
            other[...], gain[k, :, pl.ds(theirs, half)], NT, preferred_element_type=F32
        )


def local_body(where, u, tail, decay_ref, scale, leak, keep, summary, ext):
    frames, modes = decay_ref.shape
    ext[:DMAX] = tail[...]
    ext[DMAX:] = u[...]
    drive_in = jnp.zeros((frames, modes), F32)
    for k in range(TAPS):
        rolled = pltpu.roll(ext[:, k * modes : (k + 1) * modes], frames + where[3 + k], 0)
        drive_in += rolled[:frames]
    drive = scale[...] * drive_in
    decay = decay_ref[...]
    prods, (offsets,) = recur(decay, [drive], later)
    kappa = 1.0 - leak[...]
    weight = 1.0 - kappa * decay * decay
    links, (base, slope) = recur(kappa * decay, [weight * offsets, weight * prods], earlier)
    keep[0] = prods
    keep[1] = offsets
    keep[2] = links
    keep[3] = base
    keep[4] = slope
    keep[5] = drive
    summary[...] = jnp.zeros_like(summary)
    rows = [prods[-1:], offsets[-1:], links[:1], base[:1], slope[:1], decay[-1:]]
    for r, row in enumerate(rows):
        for i in range(summary.shape[0]):
            summary[i, r : r + 1] = row


def joined(first, second):
    p1, o1, l1, b1, s1 = first
    p2, o2, l2, b2, s2 = second
    return (p1 * p2, p2 * o1 + o2, l1 * l2, b1 + l1 * (b2 + s2 * o1), s1 + l1 * s2 * p1)


def five(ref, i):
    return tuple(ref[i, r : r + 1] for r in range(5))


def plane_body(every, out):
    n = every.shape[0]
    parts = [five(every, i) for i in range(n)]
    while len(parts) > 1:
        parts = [joined(parts[i], parts[i + 1]) for i in range(0, len(parts), 2)]
    out[...] = jnp.zeros_like(out)
    rows = list(parts[0]) + [every[n - 1, 5:6]]
    for r, row in enumerate(rows):
        for i in range(out.shape[0]):
            out[i, r : r + 1] = row


def ends(every, position, entering, closing, last):
    n = every.shape[0]
    states = []
    state = entering
    before = last
    own_state = jnp.zeros_like(entering)
    own_last = jnp.zeros_like(entering)
    for i in range(n):
        states.append(state)
        own_state = jnp.where(position == i, state, own_state)
        own_last = jnp.where(position == i, before, own_last)
        state = every[i, 0:1] * state + every[i, 1:2]
        before = every[i, 5:6]
    after = closing
    own_after = jnp.zeros_like(entering)
    for i in reversed(range(n)):
        own_after = jnp.where(position == i, after, own_after)
        after = every[i, 2:3] * after + every[i, 3:4] + every[i, 4:5] * states[i]
    return own_state, own_after, own_last


def finish_body(where, plane, planes, keep, decay_ref, leak, smoothed_out, resid_out):
    zero = jnp.zeros((1, decay_ref.shape[1]), F32)
    entering, after, last = ends(planes, where[0], zero, zero, zero)
    entering, after, last = ends(plane, where[1], entering, after, last)
    smoothed = keep[3] + keep[4] * entering + keep[2] * after
    decay = decay_ref[...]
    kappa = 1.0 - leak[...]
    prior = (1.0 - kappa * last * last) * entering + kappa * last * smoothed[:1]
    first = jnp.logical_and(where[0] == 0, where[1] == 0)
    prior = jnp.where(first, 0.0, prior)
    row = lax.broadcasted_iota(jnp.int32, smoothed.shape, 0)
    shifted = jnp.where(row == 0, prior, pltpu.roll(smoothed, 1, 0))
    resid = (smoothed - decay * shifted - keep[5]).astype(BF16)
    smoothed_out[...] = smoothed.T
    for i in range(resid_out.shape[0]):
        resid_out[i] = resid


def gradient_body(where, tail, own, tail_other, other, resid, out, padded):
    blocks, frames, modes = resid.shape
    row = lax.broadcasted_iota(jnp.int32, (frames, 2 * frames), 0)
    column = lax.broadcasted_iota(jnp.int32, (frames, 2 * frames), 1)
    picks = [(column == row + where[3 + k]).astype(F32).astype(BF16) for k in range(TAPS)]
    nothing = jnp.zeros((frames, modes), BF16)
    for b in range(blocks + 1):
        pair = jnp.concatenate(
            [resid[b - 1] if b > 0 else nothing, resid[b] if b < blocks else nothing], 0
        )
        for k in range(TAPS):
            moved = jnp.dot(picks[k], pair, preferred_element_type=F32)
            padded[b * frames : (b + 1) * frames, k * modes : (k + 1) * modes] = moved.astype(BF16)
    rhs = padded[...]
    for which, (before, rows) in enumerate(((tail, own), (tail_other, other))):
        lhs = jnp.concatenate([before[...]] + [rows[i] for i in range(blocks)], 1)
        sums = jnp.dot(lhs, rhs, preferred_element_type=F32)
        half = jnp.where(where[2] == which, 0, 1)
        for i in range(out.shape[0]):
            out[i, half] = sums[i * 8 : (i + 1) * 8]


def swapped(x):
    return lax.ppermute(x, "state", [(0, 1), (1, 0)])


def per_device(record, gain, rate, leak, dilation):
    frames, sensors = record.shape
    modes = rate.shape[0]
    planes = lax.axis_size(Z)
    blocks = lax.axis_size(YX)
    core = lax.axis_index("state")
    where = jnp.concatenate(
        [
            jnp.stack([lax.axis_index(Z), lax.axis_index(YX), core]).astype(jnp.int32),
            dilation,
        ]
    )
    other = swapped(record)
    group = sensors // planes // blocks
    by_sensor = record.T.reshape(planes, blocks, group, frames).swapaxes(0, 1)
    by_sensor = by_sensor.reshape(blocks, planes * group, frames)
    mine = lax.all_to_all(by_sensor, YX, 0, 0, tiled=True)
    tail = lax.ppermute(mine[-1], Z, [(i, i + 1) for i in range(planes - 1)])
    rate_t = rate.T
    decay = jnp.exp(-rate_t)
    scale = jnp.sqrt(-jnp.expm1(-2.0 * rate_t))
    leak_row = leak[None]

    u = call(taps_body, jax.ShapeDtypeStruct((frames, TAPS * modes), F32), n_in=4)(
        where, record, other, gain
    )
    u_tail = lax.ppermute(u[frames - DMAX :], TM, [(i, i + 1) for i in range(planes * blocks - 1)])
    keep, summary = call(
        local_body,
        (
            jax.ShapeDtypeStruct((6, frames, modes), F32),
            jax.ShapeDtypeStruct((blocks, 8, modes), F32),
        ),
        scratch=[pltpu.VMEM((DMAX + frames, TAPS * modes), F32)],
        n_in=6,
    )(where, u, u_tail, decay, scale, leak_row)
    plane = lax.all_to_all(summary, YX, 0, 0, tiled=True)
    plane_summary = call(
        plane_body, jax.ShapeDtypeStruct((planes, 8, modes), F32), smem=(), n_in=1
    )(plane)
    every_plane = lax.all_to_all(plane_summary, Z, 0, 0, tiled=True)
    smoothed, resid = call(
        finish_body,
        (
            jax.ShapeDtypeStruct((modes, frames), F32),
            jax.ShapeDtypeStruct((blocks, frames, modes), BF16),
        ),
        n_in=6,
    )(where, plane, every_plane, keep, decay, leak_row)
    resid_all = lax.all_to_all(resid, YX, 0, 0, tiled=True)
    theirs = swapped(jnp.concatenate([tail[None], mine]))
    partial = call(
        gradient_body,
        jax.ShapeDtypeStruct((planes, 2, group, TAPS * modes), F32),
        scratch=[pltpu.VMEM(((blocks + 1) * frames, TAPS * modes), BF16)],
        n_in=6,
    )(where, tail, mine, theirs[0], theirs[1:], resid_all)
    summed = jnp.sum(lax.all_to_all(partial, Z, 0, 0, tiled=True), axis=0)
    ours = lax.dynamic_index_in_dim(summed, core, 0, keepdims=False)
    given = swapped(lax.dynamic_index_in_dim(summed, 1 - core, 0, keepdims=False))
    ours = ours.reshape(group, TAPS, modes)
    given = given.reshape(group, TAPS, modes)
    low = jnp.where(core == 0, ours, given)
    high = jnp.where(core == 0, given, ours)
    grad = jnp.stack([low, high], 2).reshape(group, TAPS * 2 * modes)
    return (smoothed, grad)


def solution(mesh):
    split = Mesh(
        mesh.devices.reshape(16, 4, 4, mesh.shape["state"]), ("tm_0", "tm_1", "tm_2", "state")
    )
    return jax.shard_map(
        per_device,
        mesh=split,
        in_specs=(P(TM, "state"), P(None, "state", None), P("state", TM), P("state"), P()),
        out_specs=(P("state", TM), P(STATE_TM, None)),
        check_vma=False,
    )
```

```python
import jax
import jax.numpy as jnp
from jax import lax
from jax.experimental import pallas as pl
from jax.experimental.pallas import tpu as pltpu
from jax.sharding import Mesh
from jax.sharding import PartitionSpec as P

TAPS = 2
DMAX = 64
Z = "tm_0"
YX = ("tm_1", "tm_2")
TM = ("tm_0", "tm_1", "tm_2")
STATE_TM = ("state", "tm_0", "tm_1", "tm_2")
F32 = jnp.float32
BF16 = jnp.bfloat16
VMEM = pl.BlockSpec(memory_space=pltpu.VMEM)
SMEM = pl.BlockSpec(memory_space=pltpu.SMEM)
NT = (((1,), (1,)), ((), ()))


def call(body, outs, scratch=(), smem=(0,), n_in=1):
    specs = [SMEM if i in smem else VMEM for i in range(n_in)]
    return pl.pallas_call(
        body,
        out_shape=outs,
        in_specs=specs,
        out_specs=jax.tree.map(lambda _: VMEM, outs),
        scratch_shapes=scratch,
        compiler_params=pltpu.CompilerParams(vmem_limit_bytes=48 << 20),
    )


def later(x, k, fill):
    if k % 8 == 0:
        return jnp.concatenate([jnp.full((k, x.shape[1]), fill, x.dtype), x[:-k]], 0)
    row = lax.broadcasted_iota(jnp.int32, x.shape, 0)
    return jnp.where(row < k, fill, pltpu.roll(x, k, 0))


def earlier(x, k, fill):
    n = x.shape[0]
    if k % 8 == 0:
        return jnp.concatenate([x[k:], jnp.full((k, x.shape[1]), fill, x.dtype)], 0)
    row = lax.broadcasted_iota(jnp.int32, x.shape, 0)
    return jnp.where(row >= n - k, fill, pltpu.roll(x, n - k, 0))


def recur(link, sums, shift):
    k = 1
    while k < link.shape[0]:
        sums = [s + link * shift(s, k, 0.0) for s in sums]
        link = link * shift(link, k, 1.0)
        k *= 2
    return link, sums


def taps_body(where, own, other, gain, out):
    modes = gain.shape[1]
    half = own.shape[1]
    mine = pl.multiple_of(where[2] * half, half)
    theirs = pl.multiple_of((1 - where[2]) * half, half)
    for k in range(TAPS):
        out[:, k * modes : (k + 1) * modes] = lax.dot_general(
            own[...], gain[k, :, pl.ds(mine, half)], NT, preferred_element_type=F32
        ) + lax.dot_general(
            other[...], gain[k, :, pl.ds(theirs, half)], NT, preferred_element_type=F32
        )


def local_body(where, u, tail, decay_ref, scale, leak, keep, summary, ext):
    frames, modes = decay_ref.shape
    ext[:DMAX] = tail[...]
    ext[DMAX:] = u[...]
    drive_in = jnp.zeros((frames, modes), F32)
    for k in range(TAPS):
        rolled = pltpu.roll(ext[:, k * modes : (k + 1) * modes], frames + where[3 + k], 0)
        drive_in += rolled[:frames]
    drive = scale[...] * drive_in
    decay = decay_ref[...]
    prods, (offsets,) = recur(decay, [drive], later)
    kappa = 1.0 - leak[...]
    weight = 1.0 - kappa * decay * decay
    links, (base, slope) = recur(kappa * decay, [weight * offsets, weight * prods], earlier)
    keep[0] = prods
    keep[1] = offsets
    keep[2] = links
    keep[3] = base
    keep[4] = slope
    keep[5] = drive
    summary[...] = jnp.zeros_like(summary)
    rows = [prods[-1:], offsets[-1:], links[:1], base[:1], slope[:1], decay[-1:]]
    for r, row in enumerate(rows):
        for i in range(summary.shape[0]):
            summary[i, r : r + 1] = row


def joined(first, second):
    p1, o1, l1, b1, s1 = first
    p2, o2, l2, b2, s2 = second
    return (p1 * p2, p2 * o1 + o2, l1 * l2, b1 + l1 * (b2 + s2 * o1), s1 + l1 * s2 * p1)


def five(ref, i):
    return tuple(ref[i, r : r + 1] for r in range(5))


def plane_body(every, out):
    n = every.shape[0]
    parts = [five(every, i) for i in range(n)]
    while len(parts) > 1:
        parts = [joined(parts[i], parts[i + 1]) for i in range(0, len(parts), 2)]
    out[...] = jnp.zeros_like(out)
    rows = list(parts[0]) + [every[n - 1, 5:6]]
    for r, row in enumerate(rows):
        for i in range(out.shape[0]):
            out[i, r : r + 1] = row


def ends(every, position, entering, closing, last):
    n = every.shape[0]
    states = []
    state = entering
    before = last
    own_state = jnp.zeros_like(entering)
    own_last = jnp.zeros_like(entering)
    for i in range(n):
        states.append(state)
        own_state = jnp.where(position == i, state, own_state)
        own_last = jnp.where(position == i, before, own_last)
        state = every[i, 0:1] * state + every[i, 1:2]
        before = every[i, 5:6]
    after = closing
    own_after = jnp.zeros_like(entering)
    for i in reversed(range(n)):
        own_after = jnp.where(position == i, after, own_after)
        after = every[i, 2:3] * after + every[i, 3:4] + every[i, 4:5] * states[i]
    return own_state, own_after, own_last


def finish_body(where, plane, planes, keep, decay_ref, leak, smoothed_out, resid_out):
    zero = jnp.zeros((1, decay_ref.shape[1]), F32)
    entering, after, last = ends(planes, where[0], zero, zero, zero)
    entering, after, last = ends(plane, where[1], entering, after, last)
    smoothed = keep[3] + keep[4] * entering + keep[2] * after
    decay = decay_ref[...]
    kappa = 1.0 - leak[...]
    prior = (1.0 - kappa * last * last) * entering + kappa * last * smoothed[:1]
    first = jnp.logical_and(where[0] == 0, where[1] == 0)
    prior = jnp.where(first, 0.0, prior)
    row = lax.broadcasted_iota(jnp.int32, smoothed.shape, 0)
    shifted = jnp.where(row == 0, prior, pltpu.roll(smoothed, 1, 0))
    resid = (smoothed - decay * shifted - keep[5]).astype(BF16)
    smoothed_out[...] = smoothed.T
    for i in range(resid_out.shape[0]):
        resid_out[i] = resid


def gradient_body(where, tails, own, other, resid, out, padded):
    blocks, frames, modes = resid.shape
    row = lax.broadcasted_iota(jnp.int32, (frames, 2 * frames), 0)
    column = lax.broadcasted_iota(jnp.int32, (frames, 2 * frames), 1)
    picks = [(column == row + where[3 + k]).astype(F32).astype(BF16) for k in range(TAPS)]
    nothing = jnp.zeros((frames, modes), BF16)
    for b in range(blocks + 1):
        pair = jnp.concatenate(
            [resid[b - 1] if b > 0 else nothing, resid[b] if b < blocks else nothing], 0
        )
        for k in range(TAPS):
            moved = jnp.dot(picks[k], pair, preferred_element_type=F32)
            padded[b * frames : (b + 1) * frames, k * modes : (k + 1) * modes] = moved.astype(BF16)
    rhs = padded[...]
    for which, rows in enumerate((own, other)):
        lhs = jnp.concatenate([tails[which]] + [rows[i] for i in range(blocks)], 1)
        sums = jnp.dot(lhs, rhs, preferred_element_type=F32)
        half = jnp.where(where[2] == which, 0, 1)
        for i in range(out.shape[0]):
            out[i, half] = sums[i * 8 : (i + 1) * 8]


def total_body(pieces, out):
    modes = out.shape[1] // TAPS // 2
    for core in range(2):
        total = pieces[core]
        for i in range(2 + core, pieces.shape[0], 2):
            total += pieces[i]
        for k in range(TAPS):
            column = (2 * k + core) * modes
            out[:, column : column + modes] = total[:, k * modes : (k + 1) * modes]


def behind(x, first):
    return lax.optimization_barrier((x, first))[0]


def swapped(x):
    return lax.ppermute(x, "state", [(0, 1), (1, 0)])


def per_device(record, gain, rate, leak, dilation):
    frames, sensors = record.shape
    modes = rate.shape[0]
    planes = lax.axis_size(Z)
    blocks = lax.axis_size(YX)
    where = jnp.concatenate(
        [
            jnp.stack([lax.axis_index(Z), lax.axis_index(YX), lax.axis_index("state")]).astype(jnp.int32),
            dilation,
        ]
    )
    other = swapped(record)
    group = sensors // planes // blocks
    by_sensor = record.T.reshape(planes, blocks, group, frames).swapaxes(0, 1)
    by_sensor = by_sensor.reshape(blocks, planes * group, frames)
    mine = lax.all_to_all(by_sensor, YX, 0, 0, tiled=True)
    rate_t = rate.T
    decay = jnp.exp(-rate_t)
    scale = jnp.sqrt(-jnp.expm1(-2.0 * rate_t))
    leak_row = leak[None]

    u = call(taps_body, jax.ShapeDtypeStruct((frames, TAPS * modes), F32), n_in=4)(
        where, record, other, gain
    )
    u_tail = lax.ppermute(u[frames - DMAX :], TM, [(i, i + 1) for i in range(planes * blocks - 1)])
    keep, summary = call(
        local_body,
        (
            jax.ShapeDtypeStruct((6, frames, modes), F32),
            jax.ShapeDtypeStruct((blocks, 8, modes), F32),
        ),
        scratch=[pltpu.VMEM((DMAX + frames, TAPS * modes), F32)],
        n_in=6,
    )(where, u, u_tail, decay, scale, leak_row)
    summary, mine = lax.optimization_barrier((summary, mine))
    theirs = swapped(mine)
    plane = lax.all_to_all(summary, YX, 0, 0, tiled=True)
    plane_summary = call(
        plane_body, jax.ShapeDtypeStruct((planes, 8, modes), F32), smem=(), n_in=1
    )(plane)
    every_plane = lax.all_to_all(plane_summary, Z, 0, 0, tiled=True)
    smoothed, resid = call(
        finish_body,
        (
            jax.ShapeDtypeStruct((modes, frames), F32),
            jax.ShapeDtypeStruct((blocks, frames, modes), BF16),
        ),
        n_in=6,
    )(where, plane, every_plane, keep, decay, leak_row)
    resid_all = lax.all_to_all(resid, YX, 0, 0, tiled=True)
    tails = behind(jnp.stack([mine[-1], theirs[-1]]), resid)
    tails = lax.ppermute(tails, Z, [(i, i + 1) for i in range(planes - 1)])
    partial = call(
        gradient_body,
        jax.ShapeDtypeStruct((planes, 2, group, TAPS * modes), F32),
        scratch=[pltpu.VMEM(((blocks + 1) * frames, TAPS * modes), BF16)],
        n_in=5,
    )(where, tails, mine, theirs, resid_all)
    pieces = partial.reshape(planes * 2, group, TAPS * modes)
    pieces = lax.all_to_all(pieces, (Z, "state"), 0, 0, tiled=True)
    grad = call(
        total_body, jax.ShapeDtypeStruct((group, TAPS * 2 * modes), F32), smem=(), n_in=1
    )(pieces)
    return (smoothed, grad)


def solution(mesh):
    split = Mesh(
        mesh.devices.reshape(16, 4, 4, mesh.shape["state"]), ("tm_0", "tm_1", "tm_2", "state")
    )
    return jax.shard_map(
        per_device,
        mesh=split,
        in_specs=(P(TM, "state"), P(None, "state", None), P("state", TM), P("state"), P()),
        out_specs=(P("state", TM), P(STATE_TM, None)),
        check_vma=False,
    )
```

```python
import jax
import jax.numpy as jnp
from jax import lax
from jax.experimental import pallas as pl
from jax.experimental.pallas import tpu as pltpu
from jax.sharding import Mesh
from jax.sharding import PartitionSpec as P

TAPS = 2
DMAX = 64
Z = "tm_0"
YX = ("tm_1", "tm_2")
TM = ("tm_0", "tm_1", "tm_2")
STATE_TM = ("state", "tm_0", "tm_1", "tm_2")
F32 = jnp.float32
BF16 = jnp.bfloat16
VMEM = pl.BlockSpec(memory_space=pltpu.VMEM)
SMEM = pl.BlockSpec(memory_space=pltpu.SMEM)
NT = (((1,), (1,)), ((), ()))


def call(body, outs, scratch=(), smem=(0,), n_in=1):
    specs = [SMEM if i in smem else VMEM for i in range(n_in)]
    return pl.pallas_call(
        body,
        out_shape=outs,
        in_specs=specs,
        out_specs=jax.tree.map(lambda _: VMEM, outs),
        scratch_shapes=scratch,
        compiler_params=pltpu.CompilerParams(vmem_limit_bytes=48 << 20),
    )


def later(x, k, fill):
    if k % 8 == 0:
        return jnp.concatenate([jnp.full((k, x.shape[1]), fill, x.dtype), x[:-k]], 0)
    row = lax.broadcasted_iota(jnp.int32, x.shape, 0)
    return jnp.where(row < k, fill, pltpu.roll(x, k, 0))


def earlier(x, k, fill):
    n = x.shape[0]
    if k % 8 == 0:
        return jnp.concatenate([x[k:], jnp.full((k, x.shape[1]), fill, x.dtype)], 0)
    row = lax.broadcasted_iota(jnp.int32, x.shape, 0)
    return jnp.where(row >= n - k, fill, pltpu.roll(x, n - k, 0))


def recur(link, sums, shift):
    k = 1
    while k < link.shape[0]:
        sums = [s + link * shift(s, k, 0.0) for s in sums]
        link = link * shift(link, k, 1.0)
        k *= 2
    return link, sums


def taps_body(where, own, other, gain, out):
    modes = gain.shape[1]
    half = own.shape[1]
    mine = pl.multiple_of(where[2] * half, half)
    theirs = pl.multiple_of((1 - where[2]) * half, half)
    for k in range(TAPS):
        out[:, k * modes : (k + 1) * modes] = lax.dot_general(
            own[...], gain[k, :, pl.ds(mine, half)], NT, preferred_element_type=F32
        ) + lax.dot_general(
            other[...], gain[k, :, pl.ds(theirs, half)], NT, preferred_element_type=F32
        )


def local_body(where, u, tail, decay_ref, scale, leak, by_sensor, keep, sent, ext):
    frames, modes = decay_ref.shape
    ext[:DMAX] = tail[...]
    ext[DMAX:] = u[...]
    drive_in = jnp.zeros((frames, modes), F32)
    for k in range(TAPS):
        rolled = pltpu.roll(ext[:, k * modes : (k + 1) * modes], frames + where[3 + k], 0)
        drive_in += rolled[:frames]
    drive = scale[...] * drive_in
    decay = decay_ref[...]
    prods, (offsets,) = recur(decay, [drive], later)
    kappa = 1.0 - leak[...]
    weight = 1.0 - kappa * decay * decay
    links, (base, slope) = recur(kappa * decay, [weight * offsets, weight * prods], earlier)
    keep[0] = prods
    keep[1] = offsets
    keep[2] = links
    keep[3] = base
    keep[4] = slope
    keep[5] = drive
    rows = [prods[-1:], offsets[-1:], links[:1], base[:1], slope[:1], decay[-1:]]
    rest = jnp.concatenate(rows + [jnp.zeros((2, modes), F32)], 0)
    frames_rows = by_sensor.shape[1]
    parts = []
    for _ in range(3):
        part = rest.astype(BF16)
        parts.append(part.astype(F32))
        rest = rest - parts[-1]
    coded = jnp.concatenate(parts, 0).astype(BF16)
    for i in range(sent.shape[0]):
        sent[i, :frames_rows] = by_sensor[i]
        sent[i, frames_rows:] = coded


def decoded(every, out):
    at = every.shape[1] - 24
    for i in range(every.shape[0]):
        rows = every[i, at:].astype(F32)
        out[i] = rows[:8] + rows[8:16] + rows[16:]


def joined(first, second):
    p1, o1, l1, b1, s1 = first
    p2, o2, l2, b2, s2 = second
    return (p1 * p2, p2 * o1 + o2, l1 * l2, b1 + l1 * (b2 + s2 * o1), s1 + l1 * s2 * p1)


def five(ref, i):
    return tuple(ref[i, r : r + 1] for r in range(5))


def plane_body(sent, every, out):
    n = sent.shape[0]
    decoded(sent, every)
    parts = [five(every, i) for i in range(n)]
    while len(parts) > 1:
        parts = [joined(parts[i], parts[i + 1]) for i in range(0, len(parts), 2)]
    out[...] = jnp.zeros_like(out)
    rows = list(parts[0]) + [every[n - 1, 5:6]]
    for r, row in enumerate(rows):
        for i in range(out.shape[0]):
            out[i, r : r + 1] = row


def ends(every, position, entering, closing, last):
    n = every.shape[0]
    states = []
    state = entering
    before = last
    own_state = jnp.zeros_like(entering)
    own_last = jnp.zeros_like(entering)
    for i in range(n):
        states.append(state)
        own_state = jnp.where(position == i, state, own_state)
        own_last = jnp.where(position == i, before, own_last)
        state = every[i, 0:1] * state + every[i, 1:2]
        before = every[i, 5:6]
    after = closing
    own_after = jnp.zeros_like(entering)
    for i in reversed(range(n)):
        own_after = jnp.where(position == i, after, own_after)
        after = every[i, 2:3] * after + every[i, 3:4] + every[i, 4:5] * states[i]
    return own_state, own_after, own_last


def finish_body(where, plane, planes, keep, decay_ref, leak, smoothed_out, resid_out):
    zero = jnp.zeros((1, decay_ref.shape[1]), F32)
    entering, after, last = ends(planes, where[0], zero, zero, zero)
    entering, after, last = ends(plane, where[1], entering, after, last)
    smoothed = keep[3] + keep[4] * entering + keep[2] * after
    decay = decay_ref[...]
    kappa = 1.0 - leak[...]
    prior = (1.0 - kappa * last * last) * entering + kappa * last * smoothed[:1]
    first = jnp.logical_and(where[0] == 0, where[1] == 0)
    prior = jnp.where(first, 0.0, prior)
    row = lax.broadcasted_iota(jnp.int32, smoothed.shape, 0)
    shifted = jnp.where(row == 0, prior, pltpu.roll(smoothed, 1, 0))
    resid = (smoothed - decay * shifted - keep[5]).astype(BF16)
    smoothed_out[...] = smoothed.T
    for i in range(resid_out.shape[0]):
        resid_out[i] = resid


def gradient_body(where, tails, own, other, resid, out, padded):
    blocks, frames, modes = resid.shape
    row = lax.broadcasted_iota(jnp.int32, (frames, 2 * frames), 0)
    column = lax.broadcasted_iota(jnp.int32, (frames, 2 * frames), 1)
    picks = [(column == row + where[3 + k]).astype(F32).astype(BF16) for k in range(TAPS)]
    nothing = jnp.zeros((frames, modes), BF16)
    for b in range(blocks + 1):
        pair = jnp.concatenate(
            [resid[b - 1] if b > 0 else nothing, resid[b] if b < blocks else nothing], 0
        )
        for k in range(TAPS):
            moved = jnp.dot(picks[k], pair, preferred_element_type=F32)
            padded[b * frames : (b + 1) * frames, k * modes : (k + 1) * modes] = moved.astype(BF16)
    rhs = padded[...]
    for which, rows in enumerate((own, other)):
        lhs = jnp.concatenate([tails[which]] + [rows[i, :-24] for i in range(blocks)], 1)
        sums = jnp.dot(lhs, rhs, preferred_element_type=F32)
        half = jnp.where(where[2] == which, 0, 1)
        for i in range(out.shape[0]):
            out[i, half] = sums[i * 8 : (i + 1) * 8]


def total_body(pieces, out):
    modes = out.shape[1] // TAPS // 2
    for core in range(2):
        total = pieces[core]
        for i in range(2 + core, pieces.shape[0], 2):
            total += pieces[i]
        for k in range(TAPS):
            column = (2 * k + core) * modes
            out[:, column : column + modes] = total[:, k * modes : (k + 1) * modes]


def behind(x, first):
    return lax.optimization_barrier((x, first))[0]


def swapped(x):
    return lax.ppermute(x, "state", [(0, 1), (1, 0)])


def per_device(record, gain, rate, leak, dilation):
    frames, sensors = record.shape
    modes = rate.shape[0]
    planes = lax.axis_size(Z)
    blocks = lax.axis_size(YX)
    where = jnp.concatenate(
        [
            jnp.stack([lax.axis_index(Z), lax.axis_index(YX), lax.axis_index("state")]).astype(jnp.int32),
            dilation,
        ]
    )
    other = swapped(record)
    group = sensors // planes // blocks
    rate_t = rate.T
    decay = jnp.exp(-rate_t)
    scale = jnp.sqrt(-jnp.expm1(-2.0 * rate_t))
    leak_row = leak[None]

    u = call(taps_body, jax.ShapeDtypeStruct((frames, TAPS * modes), F32), n_in=4)(
        where, record, other, gain
    )
    u_tail = lax.ppermute(u[frames - DMAX :], TM, [(i, i + 1) for i in range(planes * blocks - 1)])
    by_sensor = behind(record, u).T.reshape(planes, blocks, group, frames).swapaxes(0, 1)
    by_sensor = by_sensor.reshape(blocks, planes * group, frames)
    keep, sent = call(
        local_body,
        (
            jax.ShapeDtypeStruct((6, frames, modes), F32),
            jax.ShapeDtypeStruct((blocks, planes * group + 24, frames), BF16),
        ),
        scratch=[pltpu.VMEM((DMAX + frames, TAPS * modes), F32)],
        n_in=7,
    )(where, u, u_tail, decay, scale, leak_row, by_sensor)
    mine = lax.all_to_all(sent, YX, 0, 0, tiled=True)
    plane, plane_summary = call(
        plane_body,
        (
            jax.ShapeDtypeStruct((blocks, 8, modes), F32),
            jax.ShapeDtypeStruct((planes, 8, modes), F32),
        ),
        smem=(),
        n_in=1,
    )(mine)
    theirs = swapped(mine)
    every_plane = lax.all_to_all(plane_summary, Z, 0, 0, tiled=True)
    smoothed, resid = call(
        finish_body,
        (
            jax.ShapeDtypeStruct((modes, frames), F32),
            jax.ShapeDtypeStruct((blocks, frames, modes), BF16),
        ),
        n_in=6,
    )(where, plane, every_plane, keep, decay, leak_row)
    resid_all = lax.all_to_all(resid, YX, 0, 0, tiled=True)
    tails = behind(jnp.stack([mine[-1, :-24], theirs[-1, :-24]]), resid)
    tails = lax.ppermute(tails, Z, [(i, i + 1) for i in range(planes - 1)])
    partial = call(
        gradient_body,
        jax.ShapeDtypeStruct((planes, 2, group, TAPS * modes), F32),
        scratch=[pltpu.VMEM(((blocks + 1) * frames, TAPS * modes), BF16)],
        n_in=5,
    )(where, tails, mine, theirs, resid_all)
    pieces = partial.reshape(planes * 2, group, TAPS * modes)
    pieces = lax.all_to_all(pieces, (Z, "state"), 0, 0, tiled=True)
    grad = call(
        total_body, jax.ShapeDtypeStruct((group, TAPS * 2 * modes), F32), smem=(), n_in=1
    )(pieces)
    return (smoothed, grad)


def solution(mesh):
    split = Mesh(
        mesh.devices.reshape(16, 4, 4, mesh.shape["state"]), ("tm_0", "tm_1", "tm_2", "state")
    )
    return jax.shard_map(
        per_device,
        mesh=split,
        in_specs=(P(TM, "state"), P(None, "state", None), P("state", TM), P("state"), P()),
        out_specs=(P("state", TM), P(STATE_TM, None)),
        check_vma=False,
    )
```

```python
import jax
import jax.numpy as jnp
from jax import lax
from jax.experimental import pallas as pl
from jax.experimental.pallas import tpu as pltpu
from jax.sharding import Mesh
from jax.sharding import PartitionSpec as P

TAPS = 2
DMAX = 64
Z = "tm_0"
YX = ("tm_1", "tm_2")
TM = ("tm_0", "tm_1", "tm_2")
STATE_TM = ("state", "tm_0", "tm_1", "tm_2")
F32 = jnp.float32
BF16 = jnp.bfloat16
VMEM = pl.BlockSpec(memory_space=pltpu.VMEM)
SMEM = pl.BlockSpec(memory_space=pltpu.SMEM)
NT = (((1,), (1,)), ((), ()))


def call(body, outs, scratch=(), smem=(0,), n_in=1):
    specs = [SMEM if i in smem else VMEM for i in range(n_in)]
    return pl.pallas_call(
        body,
        out_shape=outs,
        in_specs=specs,
        out_specs=jax.tree.map(lambda _: VMEM, outs),
        scratch_shapes=scratch,
        compiler_params=pltpu.CompilerParams(vmem_limit_bytes=48 << 20),
    )


def later(x, k, fill):
    if k % 8 == 0:
        return jnp.concatenate([jnp.full((k, x.shape[1]), fill, x.dtype), x[:-k]], 0)
    row = lax.broadcasted_iota(jnp.int32, x.shape, 0)
    return jnp.where(row < k, fill, pltpu.roll(x, k, 0))


def earlier(x, k, fill):
    n = x.shape[0]
    if k % 8 == 0:
        return jnp.concatenate([x[k:], jnp.full((k, x.shape[1]), fill, x.dtype)], 0)
    row = lax.broadcasted_iota(jnp.int32, x.shape, 0)
    return jnp.where(row >= n - k, fill, pltpu.roll(x, n - k, 0))


def recur(link, sums, shift):
    k = 1
    while k < link.shape[0]:
        sums = [s + link * shift(s, k, 0.0) for s in sums]
        link = link * shift(link, k, 1.0)
        k *= 2
    return link, sums


def own_body(where, own, gain, out):
    modes = gain.shape[1]
    half = own.shape[1]
    at = pl.multiple_of(where[2] * half, half)
    for k in range(TAPS):
        out[:, k * modes : (k + 1) * modes] = lax.dot_general(
            own[...], gain[k, :, pl.ds(at, half)], NT, preferred_element_type=F32
        )


def rest_body(where, other, gain, part, out):
    modes = gain.shape[1]
    half = other.shape[1]
    at = pl.multiple_of((1 - where[2]) * half, half)
    for k in range(TAPS):
        columns = slice(k * modes, (k + 1) * modes)
        out[:, columns] = part[:, columns] + lax.dot_general(
            other[...], gain[k, :, pl.ds(at, half)], NT, preferred_element_type=F32
        )


def local_body(where, u, tail, decay_ref, scale, leak, by_sensor, keep, sent, ext):
    frames, modes = decay_ref.shape
    ext[:DMAX] = tail[...]
    ext[DMAX:] = u[...]
    drive_in = jnp.zeros((frames, modes), F32)
    for k in range(TAPS):
        rolled = pltpu.roll(ext[:, k * modes : (k + 1) * modes], frames + where[3 + k], 0)
        drive_in += rolled[:frames]
    drive = scale[...] * drive_in
    decay = decay_ref[...]
    prods, (offsets,) = recur(decay, [drive], later)
    kappa = 1.0 - leak[...]
    weight = 1.0 - kappa * decay * decay
    links, (base, slope) = recur(kappa * decay, [weight * offsets, weight * prods], earlier)
    keep[0] = prods
    keep[1] = offsets
    keep[2] = links
    keep[3] = base
    keep[4] = slope
    keep[5] = drive
    rows = [prods[-1:], offsets[-1:], links[:1], base[:1], slope[:1], decay[-1:]]
    rest = jnp.concatenate(rows + [jnp.zeros((2, modes), F32)], 0)
    frames_rows = by_sensor.shape[1]
    parts = []
    for _ in range(3):
        part = rest.astype(BF16)
        parts.append(part.astype(F32))
        rest = rest - parts[-1]
    coded = jnp.concatenate(parts, 0).astype(BF16)
    for i in range(sent.shape[0]):
        sent[i, :frames_rows] = by_sensor[i]
        sent[i, frames_rows:] = coded


def decoded(every, out):
    at = every.shape[1] - 24
    for i in range(every.shape[0]):
        rows = every[i, at:].astype(F32)
        out[i] = rows[:8] + rows[8:16] + rows[16:]


def joined(first, second):
    p1, o1, l1, b1, s1 = first
    p2, o2, l2, b2, s2 = second
    return (p1 * p2, p2 * o1 + o2, l1 * l2, b1 + l1 * (b2 + s2 * o1), s1 + l1 * s2 * p1)


def five(ref, i):
    return tuple(ref[i, r : r + 1] for r in range(5))


def plane_body(sent, every, out):
    n = sent.shape[0]
    decoded(sent, every)
    parts = [five(every, i) for i in range(n)]
    while len(parts) > 1:
        parts = [joined(parts[i], parts[i + 1]) for i in range(0, len(parts), 2)]
    out[...] = jnp.zeros_like(out)
    rows = list(parts[0]) + [every[n - 1, 5:6]]
    for r, row in enumerate(rows):
        for i in range(out.shape[0]):
            out[i, r : r + 1] = row


def ends(every, position, entering, closing, last):
    n = every.shape[0]
    states = []
    state = entering
    before = last
    own_state = jnp.zeros_like(entering)
    own_last = jnp.zeros_like(entering)
    for i in range(n):
        states.append(state)
        own_state = jnp.where(position == i, state, own_state)
        own_last = jnp.where(position == i, before, own_last)
        state = every[i, 0:1] * state + every[i, 1:2]
        before = every[i, 5:6]
    after = closing
    own_after = jnp.zeros_like(entering)
    for i in reversed(range(n)):
        own_after = jnp.where(position == i, after, own_after)
        after = every[i, 2:3] * after + every[i, 3:4] + every[i, 4:5] * states[i]
    return own_state, own_after, own_last


def finish_body(where, plane, planes, keep, decay_ref, leak, smoothed_out, resid_out):
    zero = jnp.zeros((1, decay_ref.shape[1]), F32)
    entering, after, last = ends(planes, where[0], zero, zero, zero)
    entering, after, last = ends(plane, where[1], entering, after, last)
    smoothed = keep[3] + keep[4] * entering + keep[2] * after
    decay = decay_ref[...]
    kappa = 1.0 - leak[...]
    prior = (1.0 - kappa * last * last) * entering + kappa * last * smoothed[:1]
    first = jnp.logical_and(where[0] == 0, where[1] == 0)
    prior = jnp.where(first, 0.0, prior)
    row = lax.broadcasted_iota(jnp.int32, smoothed.shape, 0)
    shifted = jnp.where(row == 0, prior, pltpu.roll(smoothed, 1, 0))
    resid = (smoothed - decay * shifted - keep[5]).astype(BF16)
    smoothed_out[...] = smoothed.T
    for i in range(resid_out.shape[0]):
        resid_out[i] = resid


def gradient_body(where, tails, own, other, resid, out, padded):
    blocks, frames, modes = resid.shape
    row = lax.broadcasted_iota(jnp.int32, (frames, 2 * frames), 0)
    column = lax.broadcasted_iota(jnp.int32, (frames, 2 * frames), 1)
    picks = [(column == row + where[3 + k]).astype(F32).astype(BF16) for k in range(TAPS)]
    nothing = jnp.zeros((frames, modes), BF16)
    for b in range(blocks + 1):
        pair = jnp.concatenate(
            [resid[b - 1] if b > 0 else nothing, resid[b] if b < blocks else nothing], 0
        )
        for k in range(TAPS):
            moved = jnp.dot(picks[k], pair, preferred_element_type=F32)
            padded[b * frames : (b + 1) * frames, k * modes : (k + 1) * modes] = moved.astype(BF16)
    rhs = padded[...]
    for which, rows in enumerate((own, other)):
        lhs = jnp.concatenate([tails[which]] + [rows[i, : tails.shape[1]] for i in range(blocks)], 1)
        sums = jnp.dot(lhs, rhs, preferred_element_type=F32)
        half = jnp.where(where[2] == which, 0, 1)
        for i in range(out.shape[0]):
            out[i, half] = sums[i * 8 : (i + 1) * 8]


def total_body(pieces, out):
    modes = out.shape[1] // TAPS // 2
    for core in range(2):
        total = pieces[core]
        for i in range(2 + core, pieces.shape[0], 2):
            total += pieces[i]
        for k in range(TAPS):
            column = (2 * k + core) * modes
            out[:, column : column + modes] = total[:, k * modes : (k + 1) * modes]


def behind(x, first):
    return lax.optimization_barrier((x, first))[0]


def swapped(x):
    return lax.ppermute(x, "state", [(0, 1), (1, 0)])


def per_device(record, gain, rate, leak, dilation):
    frames, sensors = record.shape
    modes = rate.shape[0]
    planes = lax.axis_size(Z)
    blocks = lax.axis_size(YX)
    where = jnp.concatenate(
        [
            jnp.stack([lax.axis_index(Z), lax.axis_index(YX), lax.axis_index("state")]).astype(jnp.int32),
            dilation,
        ]
    )
    other = swapped(record)
    group = sensors // planes // blocks
    rate_t = rate.T
    decay = jnp.exp(-rate_t)
    scale = jnp.sqrt(-jnp.expm1(-2.0 * rate_t))
    leak_row = leak[None]

    both = jax.ShapeDtypeStruct((frames, TAPS * modes), F32)
    part = call(own_body, both, n_in=3)(where, record, gain)
    u = call(rest_body, both, n_in=4)(where, other, gain, part)
    u_tail = lax.ppermute(u[frames - DMAX :], TM, [(i, i + 1) for i in range(planes * blocks - 1)])
    by_sensor = behind(record, u).T.reshape(planes, blocks, group, frames).swapaxes(0, 1)
    by_sensor = by_sensor.reshape(blocks, planes * group, frames)
    keep, sent = call(
        local_body,
        (
            jax.ShapeDtypeStruct((6, frames, modes), F32),
            jax.ShapeDtypeStruct((blocks, planes * group + 24, frames), BF16),
        ),
        scratch=[pltpu.VMEM((DMAX + frames, TAPS * modes), F32)],
        n_in=7,
    )(where, u, u_tail, decay, scale, leak_row, by_sensor)
    mine = lax.all_to_all(sent, YX, 0, 0, tiled=True)
    plane, plane_summary = call(
        plane_body,
        (
            jax.ShapeDtypeStruct((blocks, 8, modes), F32),
            jax.ShapeDtypeStruct((planes, 8, modes), F32),
        ),
        smem=(),
        n_in=1,
    )(mine)
    theirs = swapped(mine[:, :-24])
    every_plane = lax.all_to_all(plane_summary, Z, 0, 0, tiled=True)
    smoothed, resid = call(
        finish_body,
        (
            jax.ShapeDtypeStruct((modes, frames), F32),
            jax.ShapeDtypeStruct((blocks, frames, modes), BF16),
        ),
        n_in=6,
    )(where, plane, every_plane, keep, decay, leak_row)
    resid_all = lax.all_to_all(resid, YX, 0, 0, tiled=True)
    tails = behind(jnp.stack([mine[-1, :-24], theirs[-1]]), resid)
    tails = lax.ppermute(tails, Z, [(i, i + 1) for i in range(planes - 1)])
    partial = call(
        gradient_body,
        jax.ShapeDtypeStruct((planes, 2, group, TAPS * modes), F32),
        scratch=[pltpu.VMEM(((blocks + 1) * frames, TAPS * modes), BF16)],
        n_in=5,
    )(where, tails, mine, theirs, resid_all)
    pieces = partial.reshape(planes * 2, group, TAPS * modes)
    pieces = lax.all_to_all(pieces, (Z, "state"), 0, 0, tiled=True)
    grad = call(
        total_body, jax.ShapeDtypeStruct((group, TAPS * 2 * modes), F32), smem=(), n_in=1
    )(pieces)
    return (smoothed, grad)


def solution(mesh):
    split = Mesh(
        mesh.devices.reshape(16, 4, 4, mesh.shape["state"]), ("tm_0", "tm_1", "tm_2", "state")
    )
    return jax.shard_map(
        per_device,
        mesh=split,
        in_specs=(P(TM, "state"), P(None, "state", None), P("state", TM), P("state"), P()),
        out_specs=(P("state", TM), P(STATE_TM, None)),
        check_vma=False,
    )
```

```python
import jax
import jax.numpy as jnp
from jax import lax
from jax.experimental import pallas as pl
from jax.experimental.pallas import tpu as pltpu
from jax.sharding import Mesh
from jax.sharding import PartitionSpec as P

TAPS = 2
DMAX = 64
Z = "tm_0"
YX = ("tm_1", "tm_2")
TM = ("tm_0", "tm_1", "tm_2")
STATE_TM = ("state", "tm_0", "tm_1", "tm_2")
F32 = jnp.float32
BF16 = jnp.bfloat16
VMEM = pl.BlockSpec(memory_space=pltpu.VMEM)
SMEM = pl.BlockSpec(memory_space=pltpu.SMEM)
WHOLE = pl.BlockSpec(memory_space=pltpu.HBM)
NT = (((1,), (1,)), ((), ()))


def call(body, outs, scratch=(), smem=(0,), whole=(), n_in=1):
    specs = [WHOLE if i in whole else SMEM if i in smem else VMEM for i in range(n_in)]
    return pl.pallas_call(
        body,
        out_shape=outs,
        in_specs=specs,
        out_specs=jax.tree.map(lambda _: VMEM, outs),
        scratch_shapes=scratch,
        compiler_params=pltpu.CompilerParams(vmem_limit_bytes=48 << 20),
    )


def later(x, k, fill):
    if k % 8 == 0:
        return jnp.concatenate([jnp.full((k, x.shape[1]), fill, x.dtype), x[:-k]], 0)
    row = lax.broadcasted_iota(jnp.int32, x.shape, 0)
    return jnp.where(row < k, fill, pltpu.roll(x, k, 0))


def earlier(x, k, fill):
    n = x.shape[0]
    if k % 8 == 0:
        return jnp.concatenate([x[k:], jnp.full((k, x.shape[1]), fill, x.dtype)], 0)
    row = lax.broadcasted_iota(jnp.int32, x.shape, 0)
    return jnp.where(row >= n - k, fill, pltpu.roll(x, n - k, 0))


def recur(link, sums, shift):
    k = 1
    while k < link.shape[0]:
        sums = [s + link * shift(s, k, 0.0) for s in sums]
        link = link * shift(link, k, 1.0)
        k *= 2
    return link, sums


def own_body(record, gain, out, gain_rest, own, gain_own, arrived):
    modes = gain_own.shape[1]
    half = own.shape[1]
    core = lax.axis_index("state")
    mine = pl.multiple_of(core * half, half)
    theirs = pl.multiple_of((1 - core) * half, half)
    copies = [pltpu.make_async_copy(record, own, arrived.at[0])]
    for k in range(TAPS):
        copies.append(
            pltpu.make_async_copy(
                gain.at[k, :, pl.ds(mine, half)], gain_own.at[k], arrived.at[1 + k]
            )
        )
    rest = pltpu.make_async_copy(gain.at[:, :, pl.ds(theirs, half)], gain_rest, arrived.at[1 + TAPS])
    for copy in copies:
        copy.start()
    rest.start()
    copies[0].wait()
    for k in range(TAPS):
        copies[1 + k].wait()
        out[:, k * modes : (k + 1) * modes] = lax.dot_general(
            own[...], gain_own[k], NT, preferred_element_type=F32
        )
    rest.wait()


def rest_body(other, gain, part, out):
    modes = gain.shape[1]
    for k in range(TAPS):
        columns = slice(k * modes, (k + 1) * modes)
        out[:, columns] = part[:, columns] + lax.dot_general(
            other[...], gain[k], NT, preferred_element_type=F32
        )


def local_body(where, u, tail, decay_ref, scale, leak, by_sensor, keep, sent, ext):
    frames, modes = decay_ref.shape
    ext[:DMAX] = tail[...]
    ext[DMAX:] = u[...]
    drive_in = jnp.zeros((frames, modes), F32)
    for k in range(TAPS):
        rolled = pltpu.roll(ext[:, k * modes : (k + 1) * modes], frames + where[3 + k], 0)
        drive_in += rolled[:frames]
    drive = scale[...] * drive_in
    decay = decay_ref[...]
    prods, (offsets,) = recur(decay, [drive], later)
    kappa = 1.0 - leak[...]
    weight = 1.0 - kappa * decay * decay
    links, (base, slope) = recur(kappa * decay, [weight * offsets, weight * prods], earlier)
    keep[0] = prods
    keep[1] = offsets
    keep[2] = links
    keep[3] = base
    keep[4] = slope
    keep[5] = drive
    rows = [prods[-1:], offsets[-1:], links[:1], base[:1], slope[:1], decay[-1:]]
    rest = jnp.concatenate(rows + [jnp.zeros((2, modes), F32)], 0)
    frames_rows = by_sensor.shape[1]
    parts = []
    for _ in range(3):
        part = rest.astype(BF16)
        parts.append(part.astype(F32))
        rest = rest - parts[-1]
    coded = jnp.concatenate(parts, 0).astype(BF16)
    for i in range(sent.shape[0]):
        sent[i, :frames_rows] = by_sensor[i]
        sent[i, frames_rows:] = coded


def decoded(every, out):
    at = every.shape[1] - 24
    for i in range(every.shape[0]):
        rows = every[i, at:].astype(F32)
        out[i] = rows[:8] + rows[8:16] + rows[16:]


def joined(first, second):
    p1, o1, l1, b1, s1 = first
    p2, o2, l2, b2, s2 = second
    return (p1 * p2, p2 * o1 + o2, l1 * l2, b1 + l1 * (b2 + s2 * o1), s1 + l1 * s2 * p1)


def five(ref, i):
    return tuple(ref[i, r : r + 1] for r in range(5))


def plane_body(sent, every, out):
    n = sent.shape[0]
    decoded(sent, every)
    parts = [five(every, i) for i in range(n)]
    while len(parts) > 1:
        parts = [joined(parts[i], parts[i + 1]) for i in range(0, len(parts), 2)]
    out[...] = jnp.zeros_like(out)
    rows = list(parts[0]) + [every[n - 1, 5:6]]
    for r, row in enumerate(rows):
        for i in range(out.shape[0]):
            out[i, r : r + 1] = row


def ends(every, position, entering, closing, last):
    n = every.shape[0]
    states = []
    state = entering
    before = last
    own_state = jnp.zeros_like(entering)
    own_last = jnp.zeros_like(entering)
    for i in range(n):
        states.append(state)
        own_state = jnp.where(position == i, state, own_state)
        own_last = jnp.where(position == i, before, own_last)
        state = every[i, 0:1] * state + every[i, 1:2]
        before = every[i, 5:6]
    after = closing
    own_after = jnp.zeros_like(entering)
    for i in reversed(range(n)):
        own_after = jnp.where(position == i, after, own_after)
        after = every[i, 2:3] * after + every[i, 3:4] + every[i, 4:5] * states[i]
    return own_state, own_after, own_last


def finish_body(where, plane, planes, keep, decay_ref, leak, smoothed_out, resid_out):
    zero = jnp.zeros((1, decay_ref.shape[1]), F32)
    entering, after, last = ends(planes, where[0], zero, zero, zero)
    entering, after, last = ends(plane, where[1], entering, after, last)
    smoothed = keep[3] + keep[4] * entering + keep[2] * after
    decay = decay_ref[...]
    kappa = 1.0 - leak[...]
    prior = (1.0 - kappa * last * last) * entering + kappa * last * smoothed[:1]
    first = jnp.logical_and(where[0] == 0, where[1] == 0)
    prior = jnp.where(first, 0.0, prior)
    row = lax.broadcasted_iota(jnp.int32, smoothed.shape, 0)
    shifted = jnp.where(row == 0, prior, pltpu.roll(smoothed, 1, 0))
    resid = (smoothed - decay * shifted - keep[5]).astype(BF16)
    smoothed_out[...] = smoothed.T
    for i in range(resid_out.shape[0]):
        resid_out[i] = resid


def gradient_body(where, tails, own, other, resid, out, padded):
    blocks, frames, modes = resid.shape
    row = lax.broadcasted_iota(jnp.int32, (frames, 2 * frames), 0)
    column = lax.broadcasted_iota(jnp.int32, (frames, 2 * frames), 1)
    picks = [(column == row + where[3 + k]).astype(F32).astype(BF16) for k in range(TAPS)]
    nothing = jnp.zeros((frames, modes), BF16)
    for b in range(blocks + 1):
        pair = jnp.concatenate(
            [resid[b - 1] if b > 0 else nothing, resid[b] if b < blocks else nothing], 0
        )
        for k in range(TAPS):
            moved = jnp.dot(picks[k], pair, preferred_element_type=F32)
            padded[b * frames : (b + 1) * frames, k * modes : (k + 1) * modes] = moved.astype(BF16)
    rhs = padded[...]
    for which, rows in enumerate((own, other)):
        lhs = jnp.concatenate([tails[which]] + [rows[i, : tails.shape[1]] for i in range(blocks)], 1)
        sums = jnp.dot(lhs, rhs, preferred_element_type=F32)
        half = jnp.where(where[2] == which, 0, 1)
        for i in range(out.shape[0]):
            out[i, half] = sums[i * 8 : (i + 1) * 8]


def total_body(pieces, out):
    modes = out.shape[1] // TAPS // 2
    for core in range(2):
        total = pieces[core]
        for i in range(2 + core, pieces.shape[0], 2):
            total += pieces[i]
        for k in range(TAPS):
            column = (2 * k + core) * modes
            out[:, column : column + modes] = total[:, k * modes : (k + 1) * modes]


def behind(x, first):
    return lax.optimization_barrier((x, first))[0]


def swapped(x):
    return lax.ppermute(x, "state", [(0, 1), (1, 0)])


def per_device(record, gain, rate, leak, dilation):
    frames, sensors = record.shape
    modes = rate.shape[0]
    planes = lax.axis_size(Z)
    blocks = lax.axis_size(YX)
    where = jnp.concatenate(
        [
            jnp.stack([lax.axis_index(Z), lax.axis_index(YX), lax.axis_index("state")]).astype(jnp.int32),
            dilation,
        ]
    )
    other = swapped(record)
    group = sensors // planes // blocks
    both = jax.ShapeDtypeStruct((frames, TAPS * modes), F32)
    half_gain = (TAPS, modes, sensors)
    part, gain_rest = call(
        own_body,
        (both, jax.ShapeDtypeStruct(half_gain, BF16)),
        scratch=[
            pltpu.VMEM((frames, sensors), BF16),
            pltpu.VMEM(half_gain, BF16),
            pltpu.SemaphoreType.DMA((2 + TAPS,)),
        ],
        smem=(),
        whole=(0, 1),
        n_in=2,
    )(*(pltpu.with_memory_space_constraint(x, pltpu.HBM) for x in (record, gain)))
    u = call(rest_body, both, smem=(), n_in=3)(other, gain_rest, part)
    u_tail = lax.ppermute(u[frames - DMAX :], TM, [(i, i + 1) for i in range(planes * blocks - 1)])
    rate_t = behind(rate, u).T
    decay = jnp.exp(-rate_t)
    scale = jnp.sqrt(-jnp.expm1(-2.0 * rate_t))
    leak_row = leak[None]
    by_sensor = behind(record, u).T.reshape(planes, blocks, group, frames).swapaxes(0, 1)
    by_sensor = by_sensor.reshape(blocks, planes * group, frames)
    keep, sent = call(
        local_body,
        (
            jax.ShapeDtypeStruct((6, frames, modes), F32),
            jax.ShapeDtypeStruct((blocks, planes * group + 24, frames), BF16),
        ),
        scratch=[pltpu.VMEM((DMAX + frames, TAPS * modes), F32)],
        n_in=7,
    )(where, u, u_tail, decay, scale, leak_row, by_sensor)
    mine = lax.all_to_all(sent, YX, 0, 0, tiled=True)
    plane, plane_summary = call(
        plane_body,
        (
            jax.ShapeDtypeStruct((blocks, 8, modes), F32),
            jax.ShapeDtypeStruct((planes, 8, modes), F32),
        ),
        smem=(),
        n_in=1,
    )(mine)
    theirs = swapped(mine[:, :-24])
    every_plane = lax.all_to_all(plane_summary, Z, 0, 0, tiled=True)
    smoothed, resid = call(
        finish_body,
        (
            jax.ShapeDtypeStruct((modes, frames), F32),
            jax.ShapeDtypeStruct((blocks, frames, modes), BF16),
        ),
        n_in=6,
    )(where, plane, every_plane, keep, decay, leak_row)
    resid_all = lax.all_to_all(resid, YX, 0, 0, tiled=True)
    tails = behind(jnp.stack([mine[-1, :-24], theirs[-1]]), resid)
    tails = lax.ppermute(tails, Z, [(i, i + 1) for i in range(planes - 1)])
    partial = call(
        gradient_body,
        jax.ShapeDtypeStruct((planes, 2, group, TAPS * modes), F32),
        scratch=[pltpu.VMEM(((blocks + 1) * frames, TAPS * modes), BF16)],
        n_in=5,
    )(where, tails, mine, theirs, resid_all)
    pieces = partial.reshape(planes * 2, group, TAPS * modes)
    pieces = lax.all_to_all(pieces, (Z, "state"), 0, 0, tiled=True)
    grad = call(
        total_body, jax.ShapeDtypeStruct((group, TAPS * 2 * modes), F32), smem=(), n_in=1
    )(pieces)
    return (smoothed, grad)


def solution(mesh):
    split = Mesh(
        mesh.devices.reshape(16, 4, 4, mesh.shape["state"]), ("tm_0", "tm_1", "tm_2", "state")
    )
    return jax.shard_map(
        per_device,
        mesh=split,
        in_specs=(P(TM, "state"), P(None, "state", None), P("state", TM), P("state"), P()),
        out_specs=(P("state", TM), P(STATE_TM, None)),
        check_vma=False,
    )
```

```python
import functools

import jax
import jax.numpy as jnp
from jax import lax
from jax.experimental import pallas as pl
from jax.experimental.pallas import tpu as pltpu
from jax.sharding import Mesh
from jax.sharding import PartitionSpec as P

TAPS = 2
TOP = 32768.0
DMAX = 64
Z = "tm_0"
YX = ("tm_1", "tm_2")
TM = ("tm_0", "tm_1", "tm_2")
STATE_TM = ("state", "tm_0", "tm_1", "tm_2")
F32 = jnp.float32
BF16 = jnp.bfloat16
VMEM = pl.BlockSpec(memory_space=pltpu.VMEM)
SMEM = pl.BlockSpec(memory_space=pltpu.SMEM)
WHOLE = pl.BlockSpec(memory_space=pltpu.HBM)
NT = (((1,), (1,)), ((), ()))


def call(body, outs, scratch=(), smem=(0,), whole=(), n_in=1):
    specs = [WHOLE if i in whole else SMEM if i in smem else VMEM for i in range(n_in)]
    return pl.pallas_call(
        body,
        out_shape=outs,
        in_specs=specs,
        out_specs=jax.tree.map(lambda _: VMEM, outs),
        scratch_shapes=scratch,
        compiler_params=pltpu.CompilerParams(vmem_limit_bytes=48 << 20),
    )


def later(x, k, fill):
    if k % 8 == 0:
        return jnp.concatenate([jnp.full((k, x.shape[1]), fill, x.dtype), x[:-k]], 0)
    row = lax.broadcasted_iota(jnp.int32, x.shape, 0)
    return jnp.where(row < k, fill, pltpu.roll(x, k, 0))


def earlier(x, k, fill):
    n = x.shape[0]
    if k % 8 == 0:
        return jnp.concatenate([x[k:], jnp.full((k, x.shape[1]), fill, x.dtype)], 0)
    row = lax.broadcasted_iota(jnp.int32, x.shape, 0)
    return jnp.where(row >= n - k, fill, pltpu.roll(x, n - k, 0))


def recur(link, sums, shift):
    k = 1
    while k < link.shape[0]:
        sums = [s + link * shift(s, k, 0.0) for s in sums]
        link = link * shift(link, k, 1.0)
        k *= 2
    return link, sums


def own_body(record, gain, out, gain_rest, peak, own, gain_own, arrived):
    modes = gain_own.shape[1]
    half = own.shape[1]
    core = lax.axis_index("state")
    mine = pl.multiple_of(core * half, half)
    theirs = pl.multiple_of((1 - core) * half, half)
    copies = [pltpu.make_async_copy(record, own, arrived.at[0])]
    for k in range(TAPS):
        copies.append(
            pltpu.make_async_copy(
                gain.at[k, :, pl.ds(mine, half)], gain_own.at[k], arrived.at[1 + k]
            )
        )
    rest = pltpu.make_async_copy(gain.at[:, :, pl.ds(theirs, half)], gain_rest, arrived.at[1 + TAPS])
    for copy in copies:
        copy.start()
    rest.start()
    copies[0].wait()
    largest = jnp.max(jnp.abs(own[...].astype(F32)), axis=0, keepdims=True)
    peak[...] = jnp.broadcast_to(jnp.max(largest, axis=1, keepdims=True), peak.shape)
    for k in range(TAPS):
        copies[1 + k].wait()
        out[:, k * modes : (k + 1) * modes] = lax.dot_general(
            own[...], gain_own[k], NT, preferred_element_type=F32
        )
    rest.wait()


def rest_body(other, gain, part, out):
    modes = gain.shape[1]
    for k in range(TAPS):
        columns = slice(k * modes, (k + 1) * modes)
        out[:, columns] = part[:, columns] + lax.dot_general(
            other[...], gain[k], NT, preferred_element_type=F32
        )


def local_body(where, u, tail, decay_ref, scale, leak, by_sensor, peak, keep, sent, ext):
    frames, modes = decay_ref.shape
    ext[:DMAX] = tail[...]
    ext[DMAX:] = u[...]
    drive_in = jnp.zeros((frames, modes), F32)
    for k in range(TAPS):
        rolled = pltpu.roll(ext[:, k * modes : (k + 1) * modes], frames + where[3 + k], 0)
        drive_in += rolled[:frames]
    drive = scale[...] * drive_in
    decay = decay_ref[...]
    prods, (offsets,) = recur(decay, [drive], later)
    kappa = 1.0 - leak[...]
    weight = 1.0 - kappa * decay * decay
    links, (base, slope) = recur(kappa * decay, [weight * offsets, weight * prods], earlier)
    keep[0] = prods
    keep[1] = offsets
    keep[2] = links
    keep[3] = base
    keep[4] = slope
    keep[5] = drive
    rows = [prods[-1:], offsets[-1:], links[:1], base[:1], slope[:1], decay[-1:]]
    rows += [jnp.max(jnp.abs(offsets), axis=0, keepdims=True), peak[:1]]
    rest = jnp.concatenate(rows, 0)
    frames_rows = by_sensor.shape[1]
    parts = []
    for _ in range(3):
        part = rest.astype(BF16)
        parts.append(part.astype(F32))
        rest = rest - parts[-1]
    coded = jnp.concatenate(parts, 0).astype(BF16)
    for i in range(sent.shape[0]):
        sent[i, :frames_rows] = by_sensor[i]
        sent[i, frames_rows:] = coded


def decoded(every, out):
    at = every.shape[1] - 24
    for i in range(every.shape[0]):
        rows = every[i, at:].astype(F32)
        out[i] = rows[:8] + rows[8:16] + rows[16:]


def joined(first, second):
    p1, o1, l1, b1, s1 = first
    p2, o2, l2, b2, s2 = second
    return (p1 * p2, p2 * o1 + o2, l1 * l2, b1 + l1 * (b2 + s2 * o1), s1 + l1 * s2 * p1)


def five(ref, i):
    return tuple(ref[i, r : r + 1] for r in range(5))


def plane_body(sent, every, out):
    n = sent.shape[0]
    decoded(sent, every)
    parts = [five(every, i) for i in range(n)]
    while len(parts) > 1:
        parts = [joined(parts[i], parts[i + 1]) for i in range(0, len(parts), 2)]
    state = jnp.zeros_like(every[0, :1])
    reach = state
    peak = state
    for i in range(n):
        reach = jnp.maximum(reach, every[i, 6:7] + jnp.abs(state))
        peak = jnp.maximum(peak, every[i, 7:8])
        state = every[i, 0:1] * state + every[i, 1:2]
    rows = list(parts[0]) + [every[n - 1, 5:6], reach, peak]
    for r, row in enumerate(rows):
        for i in range(out.shape[0]):
            out[i, r : r + 1] = row


def ends(every, position, entering, closing, last):
    n = every.shape[0]
    states = []
    state = entering
    before = last
    own_state = jnp.zeros_like(entering)
    own_last = jnp.zeros_like(entering)
    for i in range(n):
        states.append(state)
        own_state = jnp.where(position == i, state, own_state)
        own_last = jnp.where(position == i, before, own_last)
        state = every[i, 0:1] * state + every[i, 1:2]
        before = every[i, 5:6]
    after = closing
    afters = [after] * n
    own_after = jnp.zeros_like(entering)
    for i in reversed(range(n)):
        afters[i] = after
        own_after = jnp.where(position == i, after, own_after)
        after = every[i, 2:3] * after + every[i, 3:4] + every[i, 4:5] * states[i]
    return own_state, own_after, own_last, states, afters


def finish_body(where, plane, planes, keep, decay_ref, leak, smoothed_out, resid_out, reach):
    zero = jnp.zeros((1, decay_ref.shape[1]), F32)
    entering, after, last, states, afters = ends(planes, where[0], zero, zero, zero)
    peak = zero
    for i in range(planes.shape[0]):
        bound = 6.0 * (planes[i, 6:7] + jnp.abs(states[i])) + 2.0 * jnp.abs(afters[i])
        reach[0, i : i + 1] = jnp.broadcast_to(jnp.max(bound, axis=1, keepdims=True), zero.shape)
        reach[1, i : i + 1] = jnp.maximum(peak, planes[i, 7:8])
        peak = planes[i, 7:8]
    entering, after, last, _, _ = ends(plane, where[1], entering, after, last)
    smoothed = keep[3] + keep[4] * entering + keep[2] * after
    decay = decay_ref[...]
    kappa = 1.0 - leak[...]
    prior = (1.0 - kappa * last * last) * entering + kappa * last * smoothed[:1]
    first = jnp.logical_and(where[0] == 0, where[1] == 0)
    prior = jnp.where(first, 0.0, prior)
    row = lax.broadcasted_iota(jnp.int32, smoothed.shape, 0)
    shifted = jnp.where(row == 0, prior, pltpu.roll(smoothed, 1, 0))
    resid = (smoothed - decay * shifted - keep[5]).astype(BF16)
    smoothed_out[...] = smoothed.T
    for i in range(resid_out.shape[0]):
        resid_out[i] = resid


def bounds(first, second, span):
    return jnp.maximum(span * first[0] * jnp.maximum(first[1], second[1]), 1e-30)


def gradient_body(where, tails, tails_other, own, other, resid, reach, reach_other, out, padded):
    blocks, frames, modes = resid.shape
    row = lax.broadcasted_iota(jnp.int32, (frames, 2 * frames), 0)
    column = lax.broadcasted_iota(jnp.int32, (frames, 2 * frames), 1)
    picks = [(column == row + where[3 + k]).astype(F32).astype(BF16) for k in range(TAPS)]
    nothing = jnp.zeros((frames, modes), BF16)
    for b in range(blocks + 1):
        pair = jnp.concatenate(
            [resid[b - 1] if b > 0 else nothing, resid[b] if b < blocks else nothing], 0
        )
        for k in range(TAPS):
            moved = jnp.dot(picks[k], pair, preferred_element_type=F32)
            padded[b * frames : (b + 1) * frames, k * modes : (k + 1) * modes] = moved.astype(BF16)
    rhs = padded[...]
    bound = bounds(reach, reach_other, float(blocks * frames))
    plane = lax.broadcasted_iota(jnp.int32, bound.shape, 0)
    factor = jnp.sum(jnp.where(plane == where[0], TOP / bound, 0.0), axis=0, keepdims=True)
    factor = jnp.concatenate([factor] * TAPS, 1)
    for which, (before, rows) in enumerate(((tails, own), (tails_other, other))):
        lhs = jnp.concatenate(
            [before[...]] + [rows[i, : before.shape[0]] for i in range(blocks)], 1
        )
        sums = jnp.dot(lhs, rhs, preferred_element_type=F32) * factor
        half = jnp.where(where[2] == which, 0, 1)
        for i in range(out.shape[0]):
            out[i, half] = sums[i * 8 : (i + 1) * 8]


def total_body(where, pieces, reach, reach_other, out, *, span):
    modes = out.shape[1] // TAPS // 2
    pair = (bounds(reach, reach_other, span) / TOP, bounds(reach_other, reach, span) / TOP)
    for core in range(2):
        factor = jnp.where(where[2] == core, pair[0], pair[1])
        factor = jnp.concatenate([factor] * TAPS, 1)
        total = pieces[core] * factor[:1]
        for i in range(1, factor.shape[0]):
            total += pieces[2 * i + core] * factor[i : i + 1]
        for k in range(TAPS):
            column = (2 * k + core) * modes
            out[:, column : column + modes] = total[:, k * modes : (k + 1) * modes]


def behind(x, first):
    return lax.optimization_barrier((x, first))[0]


def swapped(x):
    return lax.ppermute(x, "state", [(0, 1), (1, 0)])


def per_device(record, gain, rate, leak, dilation):
    frames, sensors = record.shape
    modes = rate.shape[0]
    planes = lax.axis_size(Z)
    blocks = lax.axis_size(YX)
    where = jnp.concatenate(
        [
            jnp.stack([lax.axis_index(Z), lax.axis_index(YX), lax.axis_index("state")]).astype(jnp.int32),
            dilation,
        ]
    )
    other = swapped(record)
    group = sensors // planes // blocks
    both = jax.ShapeDtypeStruct((frames, TAPS * modes), F32)
    half_gain = (TAPS, modes, sensors)
    part, gain_rest, peak = call(
        own_body,
        (
            both,
            jax.ShapeDtypeStruct(half_gain, BF16),
            jax.ShapeDtypeStruct((8, modes), F32),
        ),
        scratch=[
            pltpu.VMEM((frames, sensors), BF16),
            pltpu.VMEM(half_gain, BF16),
            pltpu.SemaphoreType.DMA((2 + TAPS,)),
        ],
        smem=(),
        whole=(0, 1),
        n_in=2,
    )(*(pltpu.with_memory_space_constraint(x, pltpu.HBM) for x in (record, gain)))
    u = call(rest_body, both, smem=(), n_in=3)(other, gain_rest, part)
    u_tail = lax.ppermute(u[frames - DMAX :], TM, [(i, i + 1) for i in range(planes * blocks - 1)])
    rate_t = behind(rate, u).T
    decay = jnp.exp(-rate_t)
    scale = jnp.sqrt(-jnp.expm1(-2.0 * rate_t))
    leak_row = leak[None]
    by_sensor = behind(record, u).T.reshape(planes, blocks, group, frames).swapaxes(0, 1)
    by_sensor = by_sensor.reshape(blocks, planes * group, frames)
    keep, sent = call(
        local_body,
        (
            jax.ShapeDtypeStruct((6, frames, modes), F32),
            jax.ShapeDtypeStruct((blocks, planes * group + 24, frames), BF16),
        ),
        scratch=[pltpu.VMEM((DMAX + frames, TAPS * modes), F32)],
        n_in=8,
    )(where, u, u_tail, decay, scale, leak_row, by_sensor, peak)
    mine = lax.all_to_all(sent, YX, 0, 0, tiled=True)
    plane, plane_summary = call(
        plane_body,
        (
            jax.ShapeDtypeStruct((blocks, 8, modes), F32),
            jax.ShapeDtypeStruct((planes, 8, modes), F32),
        ),
        smem=(),
        n_in=1,
    )(mine)
    ready = behind(mine, plane_summary)[:, :-24]
    theirs = swapped(ready)
    onward = [(2 * i + c, 2 * i + 2 + c) for i in range(planes - 1) for c in range(2)]
    across = [(2 * i + c, 2 * i + 3 - c) for i in range(planes - 1) for c in range(2)]
    tails = lax.ppermute(ready[-1], (Z, "state"), onward)
    tails_other = lax.ppermute(ready[-1], (Z, "state"), across)
    every_plane = lax.all_to_all(plane_summary, Z, 0, 0, tiled=True)
    every_plane = behind(every_plane, (tails, tails_other))
    smoothed, resid, reach = call(
        finish_body,
        (
            jax.ShapeDtypeStruct((modes, frames), F32),
            jax.ShapeDtypeStruct((blocks, frames, modes), BF16),
            jax.ShapeDtypeStruct((2, planes, modes), F32),
        ),
        n_in=6,
    )(where, plane, every_plane, keep, decay, leak_row)
    resid_all = lax.all_to_all(resid, YX, 0, 0, tiled=True)
    reach_other = swapped(reach)
    partial = call(
        gradient_body,
        jax.ShapeDtypeStruct((planes, 2, group, TAPS * modes), F32),
        scratch=[pltpu.VMEM(((blocks + 1) * frames, TAPS * modes), BF16)],
        n_in=8,
    )(where, tails, tails_other, mine, theirs, resid_all, reach, reach_other)
    pieces = partial.reshape(planes * 2, group, TAPS * modes).astype(jnp.float16)
    pieces = lax.all_to_all(pieces, (Z, "state"), 0, 0, tiled=True)
    grad = call(
        functools.partial(total_body, span=float(blocks * frames)),
        jax.ShapeDtypeStruct((group, TAPS * 2 * modes), F32),
        n_in=4,
    )(where, pieces.astype(F32), reach, reach_other)
    return (smoothed, grad)


def solution(mesh):
    split = Mesh(
        mesh.devices.reshape(16, 4, 4, mesh.shape["state"]), ("tm_0", "tm_1", "tm_2", "state")
    )
    return jax.shard_map(
        per_device,
        mesh=split,
        in_specs=(P(TM, "state"), P(None, "state", None), P("state", TM), P("state"), P()),
        out_specs=(P("state", TM), P(STATE_TM, None)),
        check_vma=False,
    )
```

```python
import functools

import jax
import jax.numpy as jnp
from jax import lax
from jax.experimental import pallas as pl
from jax.experimental.pallas import tpu as pltpu
from jax.sharding import Mesh
from jax.sharding import PartitionSpec as P

TAPS = 2
TOP = 32768.0
DMAX = 64
Z = "tm_0"
YX = ("tm_1", "tm_2")
TM = ("tm_0", "tm_1", "tm_2")
STATE_TM = ("state", "tm_0", "tm_1", "tm_2")
F32 = jnp.float32
BF16 = jnp.bfloat16
VMEM = pl.BlockSpec(memory_space=pltpu.VMEM)
SMEM = pl.BlockSpec(memory_space=pltpu.SMEM)
WHOLE = pl.BlockSpec(memory_space=pltpu.HBM)
NT = (((1,), (1,)), ((), ()))


def call(body, outs, scratch=(), smem=(0,), whole=(), n_in=1):
    specs = [WHOLE if i in whole else SMEM if i in smem else VMEM for i in range(n_in)]
    return pl.pallas_call(
        body,
        out_shape=outs,
        in_specs=specs,
        out_specs=jax.tree.map(lambda _: VMEM, outs),
        scratch_shapes=scratch,
        compiler_params=pltpu.CompilerParams(vmem_limit_bytes=48 << 20),
    )


def later(x, k, fill):
    if k % 8 == 0:
        return jnp.concatenate([jnp.full((k, x.shape[1]), fill, x.dtype), x[:-k]], 0)
    row = lax.broadcasted_iota(jnp.int32, x.shape, 0)
    return jnp.where(row < k, fill, pltpu.roll(x, k, 0))


def earlier(x, k, fill):
    n = x.shape[0]
    if k % 8 == 0:
        return jnp.concatenate([x[k:], jnp.full((k, x.shape[1]), fill, x.dtype)], 0)
    row = lax.broadcasted_iota(jnp.int32, x.shape, 0)
    return jnp.where(row >= n - k, fill, pltpu.roll(x, n - k, 0))


def recur(link, sums, shift):
    k = 1
    while k < link.shape[0]:
        sums = [s + link * shift(s, k, 0.0) for s in sums]
        link = link * shift(link, k, 1.0)
        k *= 2
    return link, sums


def own_body(record, gain, out, gain_rest, peak, own, gain_own, arrived):
    modes = gain_own.shape[1]
    half = own.shape[1]
    core = lax.axis_index("state")
    mine = pl.multiple_of(core * half, half)
    theirs = pl.multiple_of((1 - core) * half, half)
    copies = [pltpu.make_async_copy(record, own, arrived.at[0])]
    for k in range(TAPS):
        copies.append(
            pltpu.make_async_copy(
                gain.at[k, :, pl.ds(mine, half)], gain_own.at[k], arrived.at[1 + k]
            )
        )
    rest = pltpu.make_async_copy(gain.at[:, :, pl.ds(theirs, half)], gain_rest, arrived.at[1 + TAPS])
    for copy in copies:
        copy.start()
    rest.start()
    copies[0].wait()
    largest = jnp.max(jnp.abs(own[...].astype(F32)), axis=0, keepdims=True)
    peak[...] = jnp.broadcast_to(jnp.max(largest, axis=1, keepdims=True), peak.shape)
    for k in range(TAPS):
        copies[1 + k].wait()
        out[:, k * modes : (k + 1) * modes] = lax.dot_general(
            own[...], gain_own[k], NT, preferred_element_type=F32
        )
    rest.wait()


def rest_body(other, gain, part, out):
    modes = gain.shape[1]
    for k in range(TAPS):
        columns = slice(k * modes, (k + 1) * modes)
        out[:, columns] = part[:, columns] + lax.dot_general(
            other[...], gain[k], NT, preferred_element_type=F32
        )


def local_body(where, u, tail, decay_ref, scale, leak, by_sensor, peak, keep, sent, ext):
    frames, modes = decay_ref.shape
    ext[:DMAX] = tail[...]
    ext[DMAX:] = u[...]
    drive_in = jnp.zeros((frames, modes), F32)
    for k in range(TAPS):
        rolled = pltpu.roll(ext[:, k * modes : (k + 1) * modes], frames + where[3 + k], 0)
        drive_in += rolled[:frames]
    drive = scale[...] * drive_in
    decay = decay_ref[...]
    prods, (offsets,) = recur(decay, [drive], later)
    kappa = 1.0 - leak[...]
    weight = 1.0 - kappa * decay * decay
    links, (base, slope) = recur(kappa * decay, [weight * offsets, weight * prods], earlier)
    keep[0] = prods
    keep[1] = offsets
    keep[2] = links
    keep[3] = base
    keep[4] = slope
    keep[5] = drive
    rows = [prods[-1:], offsets[-1:], links[:1], base[:1], slope[:1], decay[-1:]]
    rows += [jnp.max(jnp.abs(offsets), axis=0, keepdims=True), peak[:1]]
    rest = jnp.concatenate(rows, 0)
    frames_rows = by_sensor.shape[1]
    parts = []
    for _ in range(3):
        part = rest.astype(BF16)
        parts.append(part.astype(F32))
        rest = rest - parts[-1]
    coded = jnp.concatenate(parts, 0).astype(BF16)
    for i in range(sent.shape[0]):
        sent[i, :frames_rows] = by_sensor[i]
        sent[i, frames_rows:] = coded


def decoded(every, out):
    at = every.shape[1] - 24
    for i in range(every.shape[0]):
        rows = every[i, at:].astype(F32)
        out[i] = rows[:8] + rows[8:16] + rows[16:]


def joined(first, second):
    p1, o1, l1, b1, s1 = first
    p2, o2, l2, b2, s2 = second
    return (p1 * p2, p2 * o1 + o2, l1 * l2, b1 + l1 * (b2 + s2 * o1), s1 + l1 * s2 * p1)


def five(ref, i):
    return tuple(ref[i, r : r + 1] for r in range(5))


def plane_body(sent, every, out):
    n = sent.shape[0]
    decoded(sent, every)
    parts = [five(every, i) for i in range(n)]
    while len(parts) > 1:
        parts = [joined(parts[i], parts[i + 1]) for i in range(0, len(parts), 2)]
    state = jnp.zeros_like(every[0, :1])
    reach = state
    peak = state
    for i in range(n):
        reach = jnp.maximum(reach, every[i, 6:7] + jnp.abs(state))
        peak = jnp.maximum(peak, every[i, 7:8])
        state = every[i, 0:1] * state + every[i, 1:2]
    rows = list(parts[0]) + [every[n - 1, 5:6], reach, peak]
    for r, row in enumerate(rows):
        for i in range(out.shape[0]):
            out[i, r : r + 1] = row


def ends(every, position, entering, closing, last):
    n = every.shape[0]
    states = []
    state = entering
    before = last
    own_state = jnp.zeros_like(entering)
    own_last = jnp.zeros_like(entering)
    for i in range(n):
        states.append(state)
        own_state = jnp.where(position == i, state, own_state)
        own_last = jnp.where(position == i, before, own_last)
        state = every[i, 0:1] * state + every[i, 1:2]
        before = every[i, 5:6]
    after = closing
    afters = [after] * n
    own_after = jnp.zeros_like(entering)
    for i in reversed(range(n)):
        afters[i] = after
        own_after = jnp.where(position == i, after, own_after)
        after = every[i, 2:3] * after + every[i, 3:4] + every[i, 4:5] * states[i]
    return own_state, own_after, own_last, states, afters


def finish_body(where, plane, planes, keep, decay_ref, leak, smoothed_out, resid_out, reach):
    zero = jnp.zeros((1, decay_ref.shape[1]), F32)
    entering, after, last, states, afters = ends(planes, where[0], zero, zero, zero)
    peak = zero
    for i in range(planes.shape[0]):
        bound = 6.0 * (planes[i, 6:7] + jnp.abs(states[i])) + 2.0 * jnp.abs(afters[i])
        reach[0, i : i + 1] = jnp.broadcast_to(jnp.max(bound, axis=1, keepdims=True), zero.shape)
        reach[1, i : i + 1] = jnp.maximum(peak, planes[i, 7:8])
        peak = planes[i, 7:8]
    entering, after, last, _, _ = ends(plane, where[1], entering, after, last)
    smoothed = keep[3] + keep[4] * entering + keep[2] * after
    decay = decay_ref[...]
    kappa = 1.0 - leak[...]
    prior = (1.0 - kappa * last * last) * entering + kappa * last * smoothed[:1]
    first = jnp.logical_and(where[0] == 0, where[1] == 0)
    prior = jnp.where(first, 0.0, prior)
    row = lax.broadcasted_iota(jnp.int32, smoothed.shape, 0)
    shifted = jnp.where(row == 0, prior, pltpu.roll(smoothed, 1, 0))
    resid = (smoothed - decay * shifted - keep[5]).astype(BF16)
    smoothed_out[...] = smoothed.T
    for i in range(resid_out.shape[0]):
        resid_out[i] = resid


def bounds(first, second, span):
    return jnp.maximum(span * first[0] * jnp.maximum(first[1], second[1]), 1e-30)


def gradient_body(where, tails, own, other, resid, reach, reach_other, out, padded):
    blocks, frames, modes = resid.shape
    row = lax.broadcasted_iota(jnp.int32, (frames, 2 * frames), 0)
    column = lax.broadcasted_iota(jnp.int32, (frames, 2 * frames), 1)
    picks = [(column == row + where[3 + k]).astype(F32).astype(BF16) for k in range(TAPS)]
    nothing = jnp.zeros((frames, modes), BF16)
    for b in range(blocks + 1):
        pair = jnp.concatenate(
            [resid[b - 1] if b > 0 else nothing, resid[b] if b < blocks else nothing], 0
        )
        for k in range(TAPS):
            moved = jnp.dot(picks[k], pair, preferred_element_type=F32)
            padded[b * frames : (b + 1) * frames, k * modes : (k + 1) * modes] = moved.astype(BF16)
    rhs = padded[...]
    bound = bounds(reach, reach_other, float(blocks * frames))
    plane = lax.broadcasted_iota(jnp.int32, bound.shape, 0)
    factor = jnp.sum(jnp.where(plane == where[0], TOP / bound, 0.0), axis=0, keepdims=True)
    factor = jnp.concatenate([factor] * TAPS, 1)
    for which, (before, rows) in enumerate(((tails[0], own), (tails[1], other))):
        lhs = jnp.concatenate(
            [before] + [rows[i, : before.shape[0]] for i in range(blocks)], 1
        )
        sums = jnp.dot(lhs, rhs, preferred_element_type=F32) * factor
        half = jnp.where(where[2] == which, 0, 1)
        for i in range(out.shape[0]):
            out[i, half] = sums[i * 8 : (i + 1) * 8]


def total_body(where, pieces, reach, reach_other, out, *, span):
    modes = out.shape[1] // TAPS // 2
    pair = (bounds(reach, reach_other, span) / TOP, bounds(reach_other, reach, span) / TOP)
    for core in range(2):
        factor = jnp.where(where[2] == core, pair[0], pair[1])
        factor = jnp.concatenate([factor] * TAPS, 1)
        total = pieces[core] * factor[:1]
        for i in range(1, factor.shape[0]):
            total += pieces[2 * i + core] * factor[i : i + 1]
        for k in range(TAPS):
            column = (2 * k + core) * modes
            out[:, column : column + modes] = total[:, k * modes : (k + 1) * modes]


def behind(x, first):
    return lax.optimization_barrier((x, first))[0]


def swapped(x):
    return lax.ppermute(x, "state", [(0, 1), (1, 0)])


def per_device(record, gain, rate, leak, dilation):
    frames, sensors = record.shape
    modes = rate.shape[0]
    planes = lax.axis_size(Z)
    blocks = lax.axis_size(YX)
    where = jnp.concatenate(
        [
            jnp.stack([lax.axis_index(Z), lax.axis_index(YX), lax.axis_index("state")]).astype(jnp.int32),
            dilation,
        ]
    )
    other = swapped(record)
    group = sensors // planes // blocks
    both = jax.ShapeDtypeStruct((frames, TAPS * modes), F32)
    half_gain = (TAPS, modes, sensors)
    part, gain_rest, peak = call(
        own_body,
        (
            both,
            jax.ShapeDtypeStruct(half_gain, BF16),
            jax.ShapeDtypeStruct((8, modes), F32),
        ),
        scratch=[
            pltpu.VMEM((frames, sensors), BF16),
            pltpu.VMEM(half_gain, BF16),
            pltpu.SemaphoreType.DMA((2 + TAPS,)),
        ],
        smem=(),
        whole=(0, 1),
        n_in=2,
    )(*(pltpu.with_memory_space_constraint(x, pltpu.HBM) for x in (record, gain)))
    u = call(rest_body, both, smem=(), n_in=3)(other, gain_rest, part)
    u_tail = lax.ppermute(u[frames - DMAX :], TM, [(i, i + 1) for i in range(planes * blocks - 1)])
    rate_t = behind(rate, u).T
    decay = jnp.exp(-rate_t)
    scale = jnp.sqrt(-jnp.expm1(-2.0 * rate_t))
    leak_row = leak[None]
    by_sensor = behind(record, u).T.reshape(planes, blocks, group, frames).swapaxes(0, 1)
    by_sensor = by_sensor.reshape(blocks, planes * group, frames)
    keep, sent = call(
        local_body,
        (
            jax.ShapeDtypeStruct((6, frames, modes), F32),
            jax.ShapeDtypeStruct((blocks, planes * group + 24, frames), BF16),
        ),
        scratch=[pltpu.VMEM((DMAX + frames, TAPS * modes), F32)],
        n_in=8,
    )(where, u, u_tail, decay, scale, leak_row, by_sensor, peak)
    mine = lax.all_to_all(sent, YX, 0, 0, tiled=True)
    plane, plane_summary = call(
        plane_body,
        (
            jax.ShapeDtypeStruct((blocks, 8, modes), F32),
            jax.ShapeDtypeStruct((planes, 8, modes), F32),
        ),
        smem=(),
        n_in=1,
    )(mine)
    theirs = swapped(mine[:, :-24])
    every_plane = lax.all_to_all(plane_summary, Z, 0, 0, tiled=True)
    smoothed, resid, reach = call(
        finish_body,
        (
            jax.ShapeDtypeStruct((modes, frames), F32),
            jax.ShapeDtypeStruct((blocks, frames, modes), BF16),
            jax.ShapeDtypeStruct((2, planes, modes), F32),
        ),
        n_in=6,
    )(where, plane, every_plane, keep, decay, leak_row)
    resid_all = lax.all_to_all(resid, YX, 0, 0, tiled=True)
    tails = behind(jnp.stack([mine[-1, :-24], theirs[-1]]), resid)
    tails = lax.ppermute(tails, Z, [(i, i + 1) for i in range(planes - 1)])
    reach_other = swapped(reach)
    partial = call(
        gradient_body,
        jax.ShapeDtypeStruct((planes, 2, group, TAPS * modes), F32),
        scratch=[pltpu.VMEM(((blocks + 1) * frames, TAPS * modes), BF16)],
        n_in=7,
    )(where, tails, mine, theirs, resid_all, reach, reach_other)
    pieces = partial.reshape(planes * 2, group, TAPS * modes).astype(jnp.float16)
    pieces = lax.all_to_all(pieces, (Z, "state"), 0, 0, tiled=True)
    grad = call(
        functools.partial(total_body, span=float(blocks * frames)),
        jax.ShapeDtypeStruct((group, TAPS * 2 * modes), F32),
        n_in=4,
    )(where, pieces.astype(F32), reach, reach_other)
    return (smoothed, grad)


def solution(mesh):
    split = Mesh(
        mesh.devices.reshape(16, 4, 4, mesh.shape["state"]), ("tm_0", "tm_1", "tm_2", "state")
    )
    return jax.shard_map(
        per_device,
        mesh=split,
        in_specs=(P(TM, "state"), P(None, "state", None), P("state", TM), P("state"), P()),
        out_specs=(P("state", TM), P(STATE_TM, None)),
        check_vma=False,
    )
```

```python
import functools

import jax
import jax.numpy as jnp
from jax import lax
from jax.experimental import pallas as pl
from jax.experimental.pallas import tpu as pltpu
from jax.sharding import Mesh
from jax.sharding import PartitionSpec as P

TAPS = 2
TOP = 32768.0
PIECES = 4
DMAX = 64
Z = "tm_0"
YX = ("tm_1", "tm_2")
TM = ("tm_0", "tm_1", "tm_2")
STATE_TM = ("state", "tm_0", "tm_1", "tm_2")
F32 = jnp.float32
BF16 = jnp.bfloat16
VMEM = pl.BlockSpec(memory_space=pltpu.VMEM)
SMEM = pl.BlockSpec(memory_space=pltpu.SMEM)
WHOLE = pl.BlockSpec(memory_space=pltpu.HBM)
NT = (((1,), (1,)), ((), ()))


def call(body, outs, scratch=(), smem=(0,), whole=(), n_in=1):
    specs = [WHOLE if i in whole else SMEM if i in smem else VMEM for i in range(n_in)]
    return pl.pallas_call(
        body,
        out_shape=outs,
        in_specs=specs,
        out_specs=jax.tree.map(lambda _: VMEM, outs),
        scratch_shapes=scratch,
        compiler_params=pltpu.CompilerParams(vmem_limit_bytes=48 << 20),
    )


def later(x, k, fill):
    if k % 8 == 0:
        return jnp.concatenate([jnp.full((k, x.shape[1]), fill, x.dtype), x[:-k]], 0)
    row = lax.broadcasted_iota(jnp.int32, x.shape, 0)
    return jnp.where(row < k, fill, pltpu.roll(x, k, 0))


def earlier(x, k, fill):
    n = x.shape[0]
    if k % 8 == 0:
        return jnp.concatenate([x[k:], jnp.full((k, x.shape[1]), fill, x.dtype)], 0)
    row = lax.broadcasted_iota(jnp.int32, x.shape, 0)
    return jnp.where(row >= n - k, fill, pltpu.roll(x, n - k, 0))


def recur(link, sums, shift):
    k = 1
    while k < link.shape[0]:
        sums = [s + link * shift(s, k, 0.0) for s in sums]
        link = link * shift(link, k, 1.0)
        k *= 2
    return link, sums


def own_body(record, gain, out, gain_rest, peak, own, gain_own, arrived):
    modes = gain_own.shape[1]
    frames, half = own.shape
    core = lax.axis_index("state")
    mine = pl.multiple_of(core * half, half)
    theirs = pl.multiple_of((1 - core) * half, half)
    record_copies = []
    gain_copies = []
    rest_copies = []
    for piece in range(PIECES):
        rows = pl.ds(piece * (frames // PIECES), frames // PIECES)
        record_copies.append((record.at[rows], own.at[rows]))
    for k in range(TAPS):
        for piece in range(PIECES):
            rows = pl.ds(piece * (modes // PIECES), modes // PIECES)
            gain_copies.append((gain.at[k, rows, pl.ds(mine, half)], gain_own.at[k, rows]))
            rest_copies.append((gain.at[k, rows, pl.ds(theirs, half)], gain_rest.at[k, rows]))
    copies = [
        pltpu.make_async_copy(source, target, arrived.at[n])
        for n, (source, target) in enumerate(record_copies + gain_copies + rest_copies)
    ]
    for copy in copies:
        copy.start()
    for copy in copies[:PIECES]:
        copy.wait()
    largest = jnp.max(jnp.abs(own[...].astype(F32)), axis=0, keepdims=True)
    peak[...] = jnp.broadcast_to(jnp.max(largest, axis=1, keepdims=True), peak.shape)
    for k in range(TAPS):
        for copy in copies[(1 + k) * PIECES : (2 + k) * PIECES]:
            copy.wait()
        out[:, k * modes : (k + 1) * modes] = lax.dot_general(
            own[...], gain_own[k], NT, preferred_element_type=F32
        )
    for copy in copies[(1 + TAPS) * PIECES :]:
        copy.wait()


def rest_body(where, other, gain, part, out, tail):
    modes = gain.shape[1]
    row = lax.broadcasted_iota(jnp.int32, out.shape, 0)
    here = jnp.zeros(out.shape, F32)
    onward = jnp.zeros(out.shape, F32)
    for k in range(TAPS):
        u = part[:, k * modes : (k + 1) * modes] + lax.dot_general(
            other[...], gain[k], NT, preferred_element_type=F32
        )
        delayed = pltpu.roll(u, where[3 + k], 0)
        here += jnp.where(row >= where[3 + k], delayed, 0.0)
        onward += jnp.where(row < where[3 + k], delayed, 0.0)
    out[...] = here
    tail[...] = onward[:DMAX]


def local_body(here, tail, decay_ref, scale, leak, by_sensor, peak, keep, sent):
    frames, modes = decay_ref.shape
    nothing = jnp.zeros((frames - DMAX, modes), F32)
    drive_in = here[...] + jnp.concatenate([tail[...], nothing], 0)
    drive = scale[...] * drive_in
    decay = decay_ref[...]
    prods, (offsets,) = recur(decay, [drive], later)
    kappa = 1.0 - leak[...]
    weight = 1.0 - kappa * decay * decay
    links, (base, slope) = recur(kappa * decay, [weight * offsets, weight * prods], earlier)
    keep[0] = prods
    keep[1] = offsets
    keep[2] = links
    keep[3] = base
    keep[4] = slope
    keep[5] = drive
    rows = [prods[-1:], offsets[-1:], links[:1], base[:1], slope[:1], decay[-1:]]
    rows += [jnp.max(jnp.abs(offsets), axis=0, keepdims=True), peak[:1]]
    rest = jnp.concatenate(rows, 0)
    frames_rows = by_sensor.shape[1]
    parts = []
    for _ in range(3):
        part = rest.astype(BF16)
        parts.append(part.astype(F32))
        rest = rest - parts[-1]
    coded = jnp.concatenate(parts, 0).astype(BF16)
    for i in range(sent.shape[0]):
        sent[i, :frames_rows] = by_sensor[i]
        sent[i, frames_rows:] = coded


def decoded(every, out):
    at = every.shape[1] - 24
    for i in range(every.shape[0]):
        rows = every[i, at:].astype(F32)
        out[i] = rows[:8] + rows[8:16] + rows[16:]


def joined(first, second):
    p1, o1, l1, b1, s1 = first
    p2, o2, l2, b2, s2 = second
    return (p1 * p2, p2 * o1 + o2, l1 * l2, b1 + l1 * (b2 + s2 * o1), s1 + l1 * s2 * p1)


def five(ref, i):
    return tuple(ref[i, r : r + 1] for r in range(5))


def plane_body(sent, every, out):
    n = sent.shape[0]
    decoded(sent, every)
    parts = [five(every, i) for i in range(n)]
    while len(parts) > 1:
        parts = [joined(parts[i], parts[i + 1]) for i in range(0, len(parts), 2)]
    state = jnp.zeros_like(every[0, :1])
    reach = state
    peak = state
    for i in range(n):
        reach = jnp.maximum(reach, every[i, 6:7] + jnp.abs(state))
        peak = jnp.maximum(peak, every[i, 7:8])
        state = every[i, 0:1] * state + every[i, 1:2]
    rows = list(parts[0]) + [every[n - 1, 5:6], reach, peak]
    for r, row in enumerate(rows):
        for i in range(out.shape[0]):
            out[i, r : r + 1] = row


def ends(every, position, entering, closing, last):
    n = every.shape[0]
    states = []
    state = entering
    before = last
    own_state = jnp.zeros_like(entering)
    own_last = jnp.zeros_like(entering)
    for i in range(n):
        states.append(state)
        own_state = jnp.where(position == i, state, own_state)
        own_last = jnp.where(position == i, before, own_last)
        state = every[i, 0:1] * state + every[i, 1:2]
        before = every[i, 5:6]
    after = closing
    afters = [after] * n
    own_after = jnp.zeros_like(entering)
    for i in reversed(range(n)):
        afters[i] = after
        own_after = jnp.where(position == i, after, own_after)
        after = every[i, 2:3] * after + every[i, 3:4] + every[i, 4:5] * states[i]
    return own_state, own_after, own_last, states, afters


def finish_body(where, plane, planes, keep, decay_ref, leak, smoothed_out, resid_out, reach):
    zero = jnp.zeros((1, decay_ref.shape[1]), F32)
    entering, after, last, states, afters = ends(planes, where[0], zero, zero, zero)
    peak = zero
    for i in range(planes.shape[0]):
        bound = 6.0 * (planes[i, 6:7] + jnp.abs(states[i])) + 2.0 * jnp.abs(afters[i])
        reach[0, i : i + 1] = jnp.broadcast_to(jnp.max(bound, axis=1, keepdims=True), zero.shape)
        reach[1, i : i + 1] = jnp.maximum(peak, planes[i, 7:8])
        peak = planes[i, 7:8]
    entering, after, last, _, _ = ends(plane, where[1], entering, after, last)
    smoothed = keep[3] + keep[4] * entering + keep[2] * after
    decay = decay_ref[...]
    kappa = 1.0 - leak[...]
    prior = (1.0 - kappa * last * last) * entering + kappa * last * smoothed[:1]
    first = jnp.logical_and(where[0] == 0, where[1] == 0)
    prior = jnp.where(first, 0.0, prior)
    row = lax.broadcasted_iota(jnp.int32, smoothed.shape, 0)
    shifted = jnp.where(row == 0, prior, pltpu.roll(smoothed, 1, 0))
    resid = (smoothed - decay * shifted - keep[5]).astype(BF16)
    smoothed_out[...] = smoothed.T
    for i in range(resid_out.shape[0]):
        resid_out[i] = resid


def bounds(first, second, span):
    return jnp.maximum(span * first[0] * jnp.maximum(first[1], second[1]), 1e-30)


def gradient_body(where, tails, own, other, resid, reach, reach_other, out, padded):
    blocks, frames, modes = resid.shape
    row = lax.broadcasted_iota(jnp.int32, (frames, 2 * frames), 0)
    column = lax.broadcasted_iota(jnp.int32, (frames, 2 * frames), 1)
    picks = [(column == row + where[3 + k]).astype(F32).astype(BF16) for k in range(TAPS)]
    nothing = jnp.zeros((frames, modes), BF16)
    for b in range(blocks + 1):
        pair = jnp.concatenate(
            [resid[b - 1] if b > 0 else nothing, resid[b] if b < blocks else nothing], 0
        )
        for k in range(TAPS):
            moved = jnp.dot(picks[k], pair, preferred_element_type=F32)
            padded[b * frames : (b + 1) * frames, k * modes : (k + 1) * modes] = moved.astype(BF16)
    rhs = padded[...]
    bound = bounds(reach, reach_other, float(blocks * frames))
    plane = lax.broadcasted_iota(jnp.int32, bound.shape, 0)
    factor = jnp.sum(jnp.where(plane == where[0], TOP / bound, 0.0), axis=0, keepdims=True)
    factor = jnp.concatenate([factor] * TAPS, 1)
    for which, (before, rows) in enumerate(((tails[0], own), (tails[1], other))):
        lhs = jnp.concatenate(
            [before] + [rows[i, : before.shape[0]] for i in range(blocks)], 1
        )
        sums = jnp.dot(lhs, rhs, preferred_element_type=F32) * factor
        half = jnp.where(where[2] == which, 0, 1)
        for i in range(out.shape[0]):
            out[i, half] = sums[i * 8 : (i + 1) * 8]


def total_body(where, pieces, reach, reach_other, out, *, span):
    modes = out.shape[1] // TAPS // 2
    pair = (bounds(reach, reach_other, span) / TOP, bounds(reach_other, reach, span) / TOP)
    for core in range(2):
        factor = jnp.where(where[2] == core, pair[0], pair[1])
        factor = jnp.concatenate([factor] * TAPS, 1)
        total = pieces[core] * factor[:1]
        for i in range(1, factor.shape[0]):
            total += pieces[2 * i + core] * factor[i : i + 1]
        for k in range(TAPS):
            column = (2 * k + core) * modes
            out[:, column : column + modes] = total[:, k * modes : (k + 1) * modes]


def behind(x, first):
    return lax.optimization_barrier((x, first))[0]


def swapped(x):
    return lax.ppermute(x, "state", [(0, 1), (1, 0)])


def per_device(record, gain, rate, leak, dilation):
    frames, sensors = record.shape
    modes = rate.shape[0]
    planes = lax.axis_size(Z)
    blocks = lax.axis_size(YX)
    where = jnp.concatenate(
        [
            jnp.stack([lax.axis_index(Z), lax.axis_index(YX), lax.axis_index("state")]).astype(jnp.int32),
            dilation,
        ]
    )
    other = swapped(record)
    group = sensors // planes // blocks
    both = jax.ShapeDtypeStruct((frames, TAPS * modes), F32)
    half_gain = (TAPS, modes, sensors)
    part, gain_rest, peak = call(
        own_body,
        (
            both,
            jax.ShapeDtypeStruct(half_gain, BF16),
            jax.ShapeDtypeStruct((8, modes), F32),
        ),
        scratch=[
            pltpu.VMEM((frames, sensors), BF16),
            pltpu.VMEM(half_gain, BF16),
            pltpu.SemaphoreType.DMA(((1 + 2 * TAPS) * PIECES,)),
        ],
        smem=(),
        whole=(0, 1),
        n_in=2,
    )(*(pltpu.with_memory_space_constraint(x, pltpu.HBM) for x in (record, gain)))
    here, onward = call(
        rest_body,
        (
            jax.ShapeDtypeStruct((frames, modes), F32),
            jax.ShapeDtypeStruct((DMAX, modes), F32),
        ),
        n_in=4,
    )(where, other, gain_rest, part)
    tail = lax.ppermute(onward, TM, [(i, i + 1) for i in range(planes * blocks - 1)])
    rate_t = behind(rate, here).T
    decay = jnp.exp(-rate_t)
    scale = jnp.sqrt(-jnp.expm1(-2.0 * rate_t))
    leak_row = leak[None]
    by_sensor = behind(record, here).T.reshape(planes, blocks, group, frames).swapaxes(0, 1)
    by_sensor = by_sensor.reshape(blocks, planes * group, frames)
    keep, sent = call(
        local_body,
        (
            jax.ShapeDtypeStruct((6, frames, modes), F32),
            jax.ShapeDtypeStruct((blocks, planes * group + 24, frames), BF16),
        ),
        smem=(),
        n_in=7,
    )(here, tail, decay, scale, leak_row, by_sensor, peak)
    mine = lax.all_to_all(sent, YX, 0, 0, tiled=True)
    plane, plane_summary = call(
        plane_body,
        (
            jax.ShapeDtypeStruct((blocks, 8, modes), F32),
            jax.ShapeDtypeStruct((planes, 8, modes), F32),
        ),
        smem=(),
        n_in=1,
    )(mine)
    theirs = swapped(mine[:, :-24])
    every_plane = lax.all_to_all(plane_summary, Z, 0, 0, tiled=True)
    smoothed, resid, reach = call(
        finish_body,
        (
            jax.ShapeDtypeStruct((modes, frames), F32),
            jax.ShapeDtypeStruct((blocks, frames, modes), BF16),
            jax.ShapeDtypeStruct((2, planes, modes), F32),
        ),
        n_in=6,
    )(where, plane, every_plane, keep, decay, leak_row)
    resid_all = lax.all_to_all(resid, YX, 0, 0, tiled=True)
    tails = behind(jnp.stack([mine[-1, :-24], theirs[-1]]), resid)
    tails = lax.ppermute(tails, Z, [(i, i + 1) for i in range(planes - 1)])
    reach_other = swapped(reach)
    partial = call(
        gradient_body,
        jax.ShapeDtypeStruct((planes, 2, group, TAPS * modes), F32),
        scratch=[pltpu.VMEM(((blocks + 1) * frames, TAPS * modes), BF16)],
        n_in=7,
    )(where, tails, mine, theirs, resid_all, reach, reach_other)
    pieces = partial.reshape(planes * 2, group, TAPS * modes).astype(jnp.float16)
    pieces = lax.all_to_all(pieces, (Z, "state"), 0, 0, tiled=True)
    grad = call(
        functools.partial(total_body, span=float(blocks * frames)),
        jax.ShapeDtypeStruct((group, TAPS * 2 * modes), F32),
        n_in=4,
    )(where, pieces.astype(F32), reach, reach_other)
    return (smoothed, grad)


def solution(mesh):
    split = Mesh(
        mesh.devices.reshape(16, 4, 4, mesh.shape["state"]), ("tm_0", "tm_1", "tm_2", "state")
    )
    return jax.shard_map(
        per_device,
        mesh=split,
        in_specs=(P(TM, "state"), P(None, "state", None), P("state", TM), P("state"), P()),
        out_specs=(P("state", TM), P(STATE_TM, None)),
        check_vma=False,
    )
```

```python
import functools

import jax
import jax.numpy as jnp
from jax import lax
from jax.experimental import pallas as pl
from jax.experimental.pallas import tpu as pltpu
from jax.sharding import Mesh
from jax.sharding import PartitionSpec as P

TAPS = 2
TOP = 32768.0
PIECES = 1
ROWS = 16
DMAX = 64
Z = "tm_0"
YX = ("tm_1", "tm_2")
TM = ("tm_0", "tm_1", "tm_2")
STATE_TM = ("state", "tm_0", "tm_1", "tm_2")
F32 = jnp.float32
BF16 = jnp.bfloat16
VMEM = pl.BlockSpec(memory_space=pltpu.VMEM)
SMEM = pl.BlockSpec(memory_space=pltpu.SMEM)
WHOLE = pl.BlockSpec(memory_space=pltpu.HBM)
NT = (((1,), (1,)), ((), ()))


def call(body, outs, scratch=(), smem=(0,), whole=(), n_in=1):
    specs = [WHOLE if i in whole else SMEM if i in smem else VMEM for i in range(n_in)]
    return pl.pallas_call(
        body,
        out_shape=outs,
        in_specs=specs,
        out_specs=jax.tree.map(lambda _: VMEM, outs),
        scratch_shapes=scratch,
        compiler_params=pltpu.CompilerParams(vmem_limit_bytes=48 << 20),
    )


def later(x, k, fill):
    if k % 8 == 0:
        return jnp.concatenate([jnp.full((k, x.shape[1]), fill, x.dtype), x[:-k]], 0)
    row = lax.broadcasted_iota(jnp.int32, x.shape, 0)
    return jnp.where(row < k, fill, pltpu.roll(x, k, 0))


def earlier(x, k, fill):
    n = x.shape[0]
    if k % 8 == 0:
        return jnp.concatenate([x[k:], jnp.full((k, x.shape[1]), fill, x.dtype)], 0)
    row = lax.broadcasted_iota(jnp.int32, x.shape, 0)
    return jnp.where(row >= n - k, fill, pltpu.roll(x, n - k, 0))


def recur(link, sums, shift):
    k = 1
    while k < link.shape[0]:
        sums = [s + link * shift(s, k, 0.0) for s in sums]
        link = link * shift(link, k, 1.0)
        k *= 2
    return link, sums


def own_body(record, gain, out, gain_rest, peak, own, gain_own, arrived):
    modes = gain_own.shape[1]
    frames, half = own.shape
    core = lax.axis_index("state")
    mine = pl.multiple_of(core * half, half)
    theirs = pl.multiple_of((1 - core) * half, half)
    record_copies = []
    gain_copies = []
    rest_copies = []
    for piece in range(PIECES):
        rows = pl.ds(piece * (frames // PIECES), frames // PIECES)
        record_copies.append((record.at[rows], own.at[rows]))
    for k in range(TAPS):
        for piece in range(PIECES):
            rows = pl.ds(piece * (modes // PIECES), modes // PIECES)
            gain_copies.append((gain.at[k, rows, pl.ds(mine, half)], gain_own.at[k, rows]))
            rest_copies.append((gain.at[k, rows, pl.ds(theirs, half)], gain_rest.at[k, rows]))
    copies = [
        pltpu.make_async_copy(source, target, arrived.at[n])
        for n, (source, target) in enumerate(record_copies + gain_copies + rest_copies)
    ]
    for copy in copies:
        copy.start()
    for copy in copies[:PIECES]:
        copy.wait()
    largest = jnp.max(jnp.abs(own[...].astype(F32)), axis=0, keepdims=True)
    peak[...] = jnp.broadcast_to(jnp.max(largest, axis=1, keepdims=True), peak.shape)
    for k in range(TAPS):
        for copy in copies[(1 + k) * PIECES : (2 + k) * PIECES]:
            copy.wait()
        out[:, k * modes : (k + 1) * modes] = lax.dot_general(
            own[...], gain_own[k], NT, preferred_element_type=F32
        )
    for copy in copies[(1 + TAPS) * PIECES :]:
        copy.wait()


def rest_body(where, other, gain, part, out, tail):
    modes = gain.shape[1]
    row = lax.broadcasted_iota(jnp.int32, out.shape, 0)
    here = jnp.zeros(out.shape, F32)
    onward = jnp.zeros(out.shape, F32)
    for k in range(TAPS):
        u = part[:, k * modes : (k + 1) * modes] + lax.dot_general(
            other[...], gain[k], NT, preferred_element_type=F32
        )
        delayed = pltpu.roll(u, where[3 + k], 0)
        here += jnp.where(row >= where[3 + k], delayed, 0.0)
        onward += jnp.where(row < where[3 + k], delayed, 0.0)
    out[...] = here
    tail[...] = onward[:DMAX]


def response_body(decay_ref, scale_ref, leak, out):
    decay = decay_ref[...]
    scale = scale_ref[...]
    kappa = 1.0 - leak[...]
    weight = 1.0 - kappa * decay * decay
    links, _ = recur(kappa * decay, [], later)
    to_end, (to_start,) = recur(earlier(decay, 1, 1.0), [later(links, 1, 1.0) * weight], earlier)
    out[:DMAX] = (scale * to_end)[:DMAX]
    out[DMAX : 2 * DMAX] = (scale * to_start)[:DMAX]
    largest = jnp.max(scale, axis=0, keepdims=True)
    out[2 * DMAX :] = jnp.broadcast_to(largest, (8, decay.shape[1]))


def recursions(decay, kappa, drive):
    prods, (offsets,) = recur(decay, [drive], later)
    weight = 1.0 - kappa * decay * decay
    links, (base, slope) = recur(kappa * decay, [weight * offsets, weight * prods], earlier)
    return prods, offsets, links, base, slope


def local_body(here, onward, response, decay_ref, scale, leak, by_sensor, peak, sent):
    decay = decay_ref[...]
    modes = decay.shape[1]
    kappa = 1.0 - leak[...]
    prods, offsets, links, base, slope = recursions(decay, kappa, scale[...] * here[...])
    rows = [prods[-1:], offsets[-1:], links[:1], base[:1], slope[:1], decay[-1:]]
    rows += [jnp.max(jnp.abs(offsets), axis=0, keepdims=True), peak[:1]]
    tail = onward[...]
    rows.append(jnp.sum(response[:DMAX] * tail, axis=0, keepdims=True))
    rows.append(jnp.sum(response[DMAX : 2 * DMAX] * tail, axis=0, keepdims=True))
    rows.append(response[2 * DMAX : 2 * DMAX + 1] * jnp.sum(jnp.abs(tail), axis=0, keepdims=True))
    rest = jnp.concatenate(rows + [jnp.zeros((ROWS - len(rows), modes), F32)], 0)
    frames_rows = by_sensor.shape[1]
    parts = []
    for _ in range(3):
        part = rest.astype(BF16)
        parts.append(part.astype(F32))
        rest = rest - parts[-1]
    coded = jnp.concatenate(parts, 0).astype(BF16)
    for i in range(sent.shape[0]):
        sent[i, :frames_rows] = by_sensor[i]
        sent[i, frames_rows:] = coded


def joined(first, second):
    p1, o1, l1, b1, s1 = first
    p2, o2, l2, b2, s2 = second
    return (p1 * p2, p2 * o1 + o2, l1 * l2, b1 + l1 * (b2 + s2 * o1), s1 + l1 * s2 * p1)


def rows_of(ref, i, count):
    return [ref[i, r : r + 1] for r in range(count)]


def plane_body(sent, every, out):
    n = sent.shape[0]
    at = sent.shape[1] - 3 * ROWS
    blocks = []
    for i in range(n):
        coded = sent[i, at:].astype(F32)
        every[i] = coded[:ROWS] + coded[ROWS : 2 * ROWS] + coded[2 * ROWS :]
        block = rows_of(every, i, 11)
        if i > 0:
            before = blocks[-1]
            for to, source in ((1, 8), (3, 9), (6, 10)):
                block[to] = block[to] + before[source]
            every[i, 1:2] = block[1]
            every[i, 3:4] = block[3]
        blocks.append(block)
    parts = [tuple(block[:5]) for block in blocks[1:]]
    while len(parts) > 1:
        pairs = [joined(parts[i], parts[i + 1]) for i in range(0, len(parts) - 1, 2)]
        parts = pairs + parts[len(pairs) * 2 :]
    whole = joined(tuple(blocks[0][:5]), parts[0])
    state = jnp.zeros_like(blocks[0][0])
    reach = state
    peak = state
    for block in blocks:
        reach = jnp.maximum(reach, block[6] + jnp.abs(state))
        peak = jnp.maximum(peak, block[7])
        state = block[0] * state + block[1]
    last = blocks[-1]
    rows = list(whole) + [last[5], reach, peak, last[8], last[9], last[10]]
    rows += [parts[0][0], blocks[0][2] * parts[0][4]]
    rows = jnp.concatenate(rows + [jnp.zeros((ROWS - len(rows), state.shape[1]), F32)], 0)
    for i in range(out.shape[0]):
        out[i] = rows


def ends(every, position, entering, closing, last):
    n = len(every)
    states = []
    state = entering
    before = last
    own_state = jnp.zeros_like(entering)
    own_last = jnp.zeros_like(entering)
    for i in range(n):
        states.append(state)
        own_state = jnp.where(position == i, state, own_state)
        own_last = jnp.where(position == i, before, own_last)
        state = every[i][0] * state + every[i][1]
        before = every[i][5]
    after = closing
    afters = [after] * n
    own_after = jnp.zeros_like(entering)
    for i in reversed(range(n)):
        afters[i] = after
        own_after = jnp.where(position == i, after, own_after)
        after = every[i][2] * after + every[i][3] + every[i][4] * states[i]
    return own_state, own_after, own_last, states, afters


def finish_body(
    where, plane_ref, planes_ref, here, tail, decay_ref, scale, leak, smoothed_out, resid_out, reach
):
    frames, modes = decay_ref.shape
    zero = jnp.zeros((1, modes), F32)
    planes = [rows_of(planes_ref, i, 13) for i in range(planes_ref.shape[0])]
    moved = (zero, zero)
    spread = [zero]
    for i in range(1, len(planes)):
        state, closing, more = planes[i - 1][8:11]
        planes[i][1] = planes[i][1] + planes[i][11] * state
        planes[i][3] = planes[i][3] + closing + planes[i][12] * state
        spread.append(more)
        moved = tuple(
            jnp.where(where[0] == i, new, old) for new, old in zip((state, closing), moved)
        )
    entering, after, last, states, afters = ends(planes, where[0], zero, zero, zero)
    peak = zero
    for i in range(len(planes)):
        bound = 6.0 * (planes[i][6] + spread[i] + jnp.abs(states[i])) + 2.0 * jnp.abs(afters[i])
        reach[0, i : i + 1] = jnp.broadcast_to(jnp.max(bound, axis=1, keepdims=True), zero.shape)
        reach[1, i : i + 1] = jnp.maximum(peak, planes[i][7])
        peak = planes[i][7]
    plane = [rows_of(plane_ref, i, 6) for i in range(plane_ref.shape[0])]
    plane[0][1] = plane[0][1] + moved[0]
    plane[0][3] = plane[0][3] + moved[1]
    entering, after, last, _, _ = ends(plane, where[1], entering, after, last)
    decay = decay_ref[...]
    kappa = 1.0 - leak[...]
    nothing = jnp.zeros((frames - DMAX, modes), F32)
    drive = scale[...] * (here[...] + jnp.concatenate([tail[...], nothing], 0))
    _, _, links, base, slope = recursions(decay, kappa, drive)
    smoothed = base + slope * entering + links * after
    prior = (1.0 - kappa * last * last) * entering + kappa * last * smoothed[:1]
    first = jnp.logical_and(where[0] == 0, where[1] == 0)
    prior = jnp.where(first, 0.0, prior)
    row = lax.broadcasted_iota(jnp.int32, smoothed.shape, 0)
    shifted = jnp.where(row == 0, prior, pltpu.roll(smoothed, 1, 0))
    resid = (smoothed - decay * shifted - drive).astype(BF16)
    smoothed_out[...] = smoothed.T
    for i in range(resid_out.shape[0]):
        resid_out[i] = resid


def bounds(first, second, span):
    return jnp.maximum(span * first[0] * jnp.maximum(first[1], second[1]), 1e-30)


def gradient_body(where, tails, own, other, resid, reach, reach_other, out, padded):
    blocks, frames, modes = resid.shape
    row = lax.broadcasted_iota(jnp.int32, (frames, 2 * frames), 0)
    column = lax.broadcasted_iota(jnp.int32, (frames, 2 * frames), 1)
    picks = [(column == row + where[3 + k]).astype(F32).astype(BF16) for k in range(TAPS)]
    nothing = jnp.zeros((frames, modes), BF16)
    for b in range(blocks + 1):
        pair = jnp.concatenate(
            [resid[b - 1] if b > 0 else nothing, resid[b] if b < blocks else nothing], 0
        )
        for k in range(TAPS):
            moved = jnp.dot(picks[k], pair, preferred_element_type=F32)
            padded[b * frames : (b + 1) * frames, k * modes : (k + 1) * modes] = moved.astype(BF16)
    rhs = padded[...]
    bound = bounds(reach, reach_other, float(blocks * frames))
    plane = lax.broadcasted_iota(jnp.int32, bound.shape, 0)
    factor = jnp.sum(jnp.where(plane == where[0], TOP / bound, 0.0), axis=0, keepdims=True)
    factor = jnp.concatenate([factor] * TAPS, 1)
    for which, (before, rows) in enumerate(((tails[0], own), (tails[1], other))):
        lhs = jnp.concatenate(
            [before] + [rows[i, : before.shape[0]] for i in range(blocks)], 1
        )
        sums = jnp.dot(lhs, rhs, preferred_element_type=F32) * factor
        half = jnp.where(where[2] == which, 0, 1)
        for i in range(out.shape[0]):
            out[i, half] = sums[i * 8 : (i + 1) * 8]


def total_body(where, pieces, reach, reach_other, out, *, span):
    modes = out.shape[1] // TAPS // 2
    pair = (bounds(reach, reach_other, span) / TOP, bounds(reach_other, reach, span) / TOP)
    for core in range(2):
        factor = jnp.where(where[2] == core, pair[0], pair[1])
        factor = jnp.concatenate([factor] * TAPS, 1)
        total = pieces[core] * factor[:1]
        for i in range(1, factor.shape[0]):
            total += pieces[2 * i + core] * factor[i : i + 1]
        for k in range(TAPS):
            column = (2 * k + core) * modes
            out[:, column : column + modes] = total[:, k * modes : (k + 1) * modes]


def behind(x, first):
    return lax.optimization_barrier((x, first))[0]


def swapped(x):
    return lax.ppermute(x, "state", [(0, 1), (1, 0)])


def per_device(record, gain, rate, leak, dilation):
    frames, sensors = record.shape
    modes = rate.shape[0]
    planes = lax.axis_size(Z)
    blocks = lax.axis_size(YX)
    where = jnp.concatenate(
        [
            jnp.stack([lax.axis_index(Z), lax.axis_index(YX), lax.axis_index("state")]).astype(jnp.int32),
            dilation,
        ]
    )
    rate_t = rate.T
    decay = jnp.exp(-rate_t)
    scale = jnp.sqrt(-jnp.expm1(-2.0 * rate_t))
    leak_row = leak[None]
    response = call(
        response_body, jax.ShapeDtypeStruct((2 * DMAX + 8, modes), F32), smem=(), n_in=3
    )(decay, scale, leak_row)
    response_after = lax.ppermute(
        response, TM, [(i + 1, i) for i in range(planes * blocks - 1)]
    )
    other = swapped(record)
    group = sensors // planes // blocks
    both = jax.ShapeDtypeStruct((frames, TAPS * modes), F32)
    half_gain = (TAPS, modes, sensors)
    part, gain_rest, peak = call(
        own_body,
        (
            both,
            jax.ShapeDtypeStruct(half_gain, BF16),
            jax.ShapeDtypeStruct((8, modes), F32),
        ),
        scratch=[
            pltpu.VMEM((frames, sensors), BF16),
            pltpu.VMEM(half_gain, BF16),
            pltpu.SemaphoreType.DMA(((1 + 2 * TAPS) * PIECES,)),
        ],
        smem=(),
        whole=(0, 1),
        n_in=2,
    )(*(pltpu.with_memory_space_constraint(x, pltpu.HBM) for x in (record, gain)))
    here, onward = call(
        rest_body,
        (
            jax.ShapeDtypeStruct((frames, modes), F32),
            jax.ShapeDtypeStruct((DMAX, modes), F32),
        ),
        n_in=4,
    )(where, other, gain_rest, part)
    by_sensor = behind(record, here).T.reshape(planes, blocks, group, frames).swapaxes(0, 1)
    by_sensor = by_sensor.reshape(blocks, planes * group, frames)
    sent = call(
        local_body,
        jax.ShapeDtypeStruct((blocks, planes * group + 3 * ROWS, frames), BF16),
        smem=(),
        n_in=8,
    )(here, onward, response_after, decay, scale, leak_row, by_sensor, peak)
    mine = lax.all_to_all(sent, YX, 0, 0, tiled=True)
    tail = lax.ppermute(
        behind(onward, sent), TM, [(i, i + 1) for i in range(planes * blocks - 1)]
    )
    plane, plane_summary = call(
        plane_body,
        (
            jax.ShapeDtypeStruct((blocks, ROWS, modes), F32),
            jax.ShapeDtypeStruct((planes, ROWS, modes), F32),
        ),
        smem=(),
        n_in=1,
    )(behind(mine, tail))
    theirs = swapped(mine[:, : planes * group])
    every_plane = lax.all_to_all(plane_summary, Z, 0, 0, tiled=True)
    smoothed, resid, reach = call(
        finish_body,
        (
            jax.ShapeDtypeStruct((modes, frames), F32),
            jax.ShapeDtypeStruct((blocks, frames, modes), BF16),
            jax.ShapeDtypeStruct((2, planes, modes), F32),
        ),
        n_in=8,
    )(where, plane, every_plane, here, tail, decay, scale, leak_row)
    resid_all = lax.all_to_all(resid, YX, 0, 0, tiled=True)
    tails = behind(jnp.stack([mine[-1, : planes * group], theirs[-1]]), resid)
    tails = lax.ppermute(tails, Z, [(i, i + 1) for i in range(planes - 1)])
    reach_other = swapped(reach)
    partial = call(
        gradient_body,
        jax.ShapeDtypeStruct((planes, 2, group, TAPS * modes), F32),
        scratch=[pltpu.VMEM(((blocks + 1) * frames, TAPS * modes), BF16)],
        n_in=7,
    )(where, tails, mine, theirs, resid_all, reach, reach_other)
    pieces = partial.reshape(planes * 2, group, TAPS * modes).astype(jnp.float16)
    pieces = lax.all_to_all(pieces, (Z, "state"), 0, 0, tiled=True)
    grad = call(
        functools.partial(total_body, span=float(blocks * frames)),
        jax.ShapeDtypeStruct((group, TAPS * 2 * modes), F32),
        n_in=4,
    )(where, pieces.astype(F32), reach, reach_other)
    return (smoothed, grad)


def solution(mesh):
    split = Mesh(
        mesh.devices.reshape(16, 4, 4, mesh.shape["state"]), ("tm_0", "tm_1", "tm_2", "state")
    )
    return jax.shard_map(
        per_device,
        mesh=split,
        in_specs=(P(TM, "state"), P(None, "state", None), P("state", TM), P("state"), P()),
        out_specs=(P("state", TM), P(STATE_TM, None)),
        check_vma=False,
    )
```

```python
import functools

import jax
import jax.numpy as jnp
from jax import lax
from jax.experimental import pallas as pl
from jax.experimental.pallas import tpu as pltpu
from jax.sharding import Mesh
from jax.sharding import PartitionSpec as P

TAPS = 2
TOP = 32768.0
PIECES = 1
DMAX = 64
Z = "tm_0"
YX = ("tm_1", "tm_2")
TM = ("tm_0", "tm_1", "tm_2")
STATE_TM = ("state", "tm_0", "tm_1", "tm_2")
F32 = jnp.float32
BF16 = jnp.bfloat16
VMEM = pl.BlockSpec(memory_space=pltpu.VMEM)
SMEM = pl.BlockSpec(memory_space=pltpu.SMEM)
WHOLE = pl.BlockSpec(memory_space=pltpu.HBM)
NT = (((1,), (1,)), ((), ()))


def call(body, outs, scratch=(), smem=(0,), whole=(), n_in=1):
    specs = [WHOLE if i in whole else SMEM if i in smem else VMEM for i in range(n_in)]
    return pl.pallas_call(
        body,
        out_shape=outs,
        in_specs=specs,
        out_specs=jax.tree.map(lambda _: VMEM, outs),
        scratch_shapes=scratch,
        compiler_params=pltpu.CompilerParams(vmem_limit_bytes=48 << 20),
    )


def later(x, k, fill):
    if k % 8 == 0:
        return jnp.concatenate([jnp.full((k, x.shape[1]), fill, x.dtype), x[:-k]], 0)
    row = lax.broadcasted_iota(jnp.int32, x.shape, 0)
    return jnp.where(row < k, fill, pltpu.roll(x, k, 0))


def earlier(x, k, fill):
    n = x.shape[0]
    if k % 8 == 0:
        return jnp.concatenate([x[k:], jnp.full((k, x.shape[1]), fill, x.dtype)], 0)
    row = lax.broadcasted_iota(jnp.int32, x.shape, 0)
    return jnp.where(row >= n - k, fill, pltpu.roll(x, n - k, 0))


def recur(link, sums, shift):
    k = 1
    while k < link.shape[0]:
        sums = [s + link * shift(s, k, 0.0) for s in sums]
        link = link * shift(link, k, 1.0)
        k *= 2
    return link, sums


def own_body(record, gain, out, gain_rest, peak, own, gain_own, arrived):
    modes = gain_own.shape[1]
    frames, half = own.shape
    core = lax.axis_index("state")
    mine = pl.multiple_of(core * half, half)
    theirs = pl.multiple_of((1 - core) * half, half)
    record_copies = []
    gain_copies = []
    rest_copies = []
    for piece in range(PIECES):
        rows = pl.ds(piece * (frames // PIECES), frames // PIECES)
        record_copies.append((record.at[rows], own.at[rows]))
    for k in range(TAPS):
        for piece in range(PIECES):
            rows = pl.ds(piece * (modes // PIECES), modes // PIECES)
            gain_copies.append((gain.at[k, rows, pl.ds(mine, half)], gain_own.at[k, rows]))
            rest_copies.append((gain.at[k, rows, pl.ds(theirs, half)], gain_rest.at[k, rows]))
    copies = [
        pltpu.make_async_copy(source, target, arrived.at[n])
        for n, (source, target) in enumerate(record_copies + gain_copies + rest_copies)
    ]
    for copy in copies:
        copy.start()
    for copy in copies[:PIECES]:
        copy.wait()
    largest = jnp.max(jnp.abs(own[...].astype(F32)), axis=0, keepdims=True)
    peak[...] = jnp.broadcast_to(jnp.max(largest, axis=1, keepdims=True), peak.shape)
    for k in range(TAPS):
        for copy in copies[(1 + k) * PIECES : (2 + k) * PIECES]:
            copy.wait()
        out[:, k * modes : (k + 1) * modes] = lax.dot_general(
            own[...], gain_own[k], NT, preferred_element_type=F32
        )
    for copy in copies[(1 + TAPS) * PIECES :]:
        copy.wait()


def rest_body(where, other, gain, part, out, tail):
    modes = gain.shape[1]
    row = lax.broadcasted_iota(jnp.int32, out.shape, 0)
    here = jnp.zeros(out.shape, F32)
    onward = jnp.zeros(out.shape, F32)
    for k in range(TAPS):
        u = part[:, k * modes : (k + 1) * modes] + lax.dot_general(
            other[...], gain[k], NT, preferred_element_type=F32
        )
        delayed = pltpu.roll(u, where[3 + k], 0)
        here += jnp.where(row >= where[3 + k], delayed, 0.0)
        onward += jnp.where(row < where[3 + k], delayed, 0.0)
    out[...] = here
    tail[...] = onward[:DMAX]


def local_body(here, tail, decay_ref, scale, leak, peak, keep, summary):
    frames, modes = decay_ref.shape
    nothing = jnp.zeros((frames - DMAX, modes), F32)
    drive_in = here[...] + jnp.concatenate([tail[...], nothing], 0)
    drive = scale[...] * drive_in
    decay = decay_ref[...]
    prods, (offsets,) = recur(decay, [drive], later)
    kappa = 1.0 - leak[...]
    weight = 1.0 - kappa * decay * decay
    links, (base, slope) = recur(kappa * decay, [weight * offsets, weight * prods], earlier)
    keep[0] = prods
    keep[1] = offsets
    keep[2] = links
    keep[3] = base
    keep[4] = slope
    keep[5] = drive
    rows = [prods[-1:], offsets[-1:], links[:1], base[:1], slope[:1], decay[-1:]]
    rows += [jnp.max(jnp.abs(offsets), axis=0, keepdims=True), peak[:1]]
    rows = jnp.concatenate(rows, 0)
    for i in range(summary.shape[0]):
        summary[i] = rows


def joined(first, second):
    p1, o1, l1, b1, s1 = first
    p2, o2, l2, b2, s2 = second
    return (p1 * p2, p2 * o1 + o2, l1 * l2, b1 + l1 * (b2 + s2 * o1), s1 + l1 * s2 * p1)


def five(ref, i):
    return tuple(ref[i, r : r + 1] for r in range(5))


def plane_body(every, out):
    n = every.shape[0]
    parts = [five(every, i) for i in range(n)]
    while len(parts) > 1:
        parts = [joined(parts[i], parts[i + 1]) for i in range(0, len(parts), 2)]
    state = jnp.zeros_like(every[0, :1])
    reach = state
    peak = state
    for i in range(n):
        reach = jnp.maximum(reach, every[i, 6:7] + jnp.abs(state))
        peak = jnp.maximum(peak, every[i, 7:8])
        state = every[i, 0:1] * state + every[i, 1:2]
    rows = list(parts[0]) + [every[n - 1, 5:6], reach, peak]
    for r, row in enumerate(rows):
        for i in range(out.shape[0]):
            out[i, r : r + 1] = row


def ends(every, position, entering, closing, last):
    n = every.shape[0]
    states = []
    state = entering
    before = last
    own_state = jnp.zeros_like(entering)
    own_last = jnp.zeros_like(entering)
    for i in range(n):
        states.append(state)
        own_state = jnp.where(position == i, state, own_state)
        own_last = jnp.where(position == i, before, own_last)
        state = every[i, 0:1] * state + every[i, 1:2]
        before = every[i, 5:6]
    after = closing
    afters = [after] * n
    own_after = jnp.zeros_like(entering)
    for i in reversed(range(n)):
        afters[i] = after
        own_after = jnp.where(position == i, after, own_after)
        after = every[i, 2:3] * after + every[i, 3:4] + every[i, 4:5] * states[i]
    return own_state, own_after, own_last, states, afters


def finish_body(where, plane, planes, keep, decay_ref, leak, smoothed_out, resid_out, reach):
    zero = jnp.zeros((1, decay_ref.shape[1]), F32)
    entering, after, last, states, afters = ends(planes, where[0], zero, zero, zero)
    peak = zero
    for i in range(planes.shape[0]):
        bound = 6.0 * (planes[i, 6:7] + jnp.abs(states[i])) + 2.0 * jnp.abs(afters[i])
        reach[0, i : i + 1] = jnp.broadcast_to(jnp.max(bound, axis=1, keepdims=True), zero.shape)
        reach[1, i : i + 1] = jnp.maximum(peak, planes[i, 7:8])
        peak = planes[i, 7:8]
    entering, after, last, _, _ = ends(plane, where[1], entering, after, last)
    smoothed = keep[3] + keep[4] * entering + keep[2] * after
    decay = decay_ref[...]
    kappa = 1.0 - leak[...]
    prior = (1.0 - kappa * last * last) * entering + kappa * last * smoothed[:1]
    first = jnp.logical_and(where[0] == 0, where[1] == 0)
    prior = jnp.where(first, 0.0, prior)
    row = lax.broadcasted_iota(jnp.int32, smoothed.shape, 0)
    shifted = jnp.where(row == 0, prior, pltpu.roll(smoothed, 1, 0))
    resid = (smoothed - decay * shifted - keep[5]).astype(BF16)
    smoothed_out[...] = smoothed.T
    for i in range(resid_out.shape[0]):
        resid_out[i] = resid


def bounds(first, second, span):
    return jnp.maximum(span * first[0] * jnp.maximum(first[1], second[1]), 1e-30)


def gradient_body(where, tails, own, other, resid, reach, reach_other, out, padded):
    blocks, frames, modes = resid.shape
    row = lax.broadcasted_iota(jnp.int32, (frames, 2 * frames), 0)
    column = lax.broadcasted_iota(jnp.int32, (frames, 2 * frames), 1)
    picks = [(column == row + where[3 + k]).astype(F32).astype(BF16) for k in range(TAPS)]
    nothing = jnp.zeros((frames, modes), BF16)
    for b in range(blocks + 1):
        pair = jnp.concatenate(
            [resid[b - 1] if b > 0 else nothing, resid[b] if b < blocks else nothing], 0
        )
        for k in range(TAPS):
            moved = jnp.dot(picks[k], pair, preferred_element_type=F32)
            padded[b * frames : (b + 1) * frames, k * modes : (k + 1) * modes] = moved.astype(BF16)
    rhs = padded[...]
    bound = bounds(reach, reach_other, float(blocks * frames))
    plane = lax.broadcasted_iota(jnp.int32, bound.shape, 0)
    factor = jnp.sum(jnp.where(plane == where[0], TOP / bound, 0.0), axis=0, keepdims=True)
    factor = jnp.concatenate([factor] * TAPS, 1)
    for which, (before, rows) in enumerate(((tails[0], own), (tails[1], other))):
        lhs = jnp.concatenate(
            [before] + [rows[i, : before.shape[0]] for i in range(blocks)], 1
        )
        sums = jnp.dot(lhs, rhs, preferred_element_type=F32) * factor
        half = jnp.where(where[2] == which, 0, 1)
        for i in range(out.shape[0]):
            out[i, half] = sums[i * 8 : (i + 1) * 8]


def total_body(where, pieces, reach, reach_other, out, *, span):
    modes = out.shape[1] // TAPS // 2
    pair = (bounds(reach, reach_other, span) / TOP, bounds(reach_other, reach, span) / TOP)
    for core in range(2):
        factor = jnp.where(where[2] == core, pair[0], pair[1])
        factor = jnp.concatenate([factor] * TAPS, 1)
        total = pieces[core] * factor[:1]
        for i in range(1, factor.shape[0]):
            total += pieces[2 * i + core] * factor[i : i + 1]
        for k in range(TAPS):
            column = (2 * k + core) * modes
            out[:, column : column + modes] = total[:, k * modes : (k + 1) * modes]


def behind(x, first):
    return lax.optimization_barrier((x, first))[0]


def swapped(x):
    return lax.ppermute(x, "state", [(0, 1), (1, 0)])


def per_device(record, gain, rate, leak, dilation):
    frames, sensors = record.shape
    modes = rate.shape[0]
    planes = lax.axis_size(Z)
    blocks = lax.axis_size(YX)
    where = jnp.concatenate(
        [
            jnp.stack([lax.axis_index(Z), lax.axis_index(YX), lax.axis_index("state")]).astype(jnp.int32),
            dilation,
        ]
    )
    other = swapped(record)
    group = sensors // planes // blocks
    both = jax.ShapeDtypeStruct((frames, TAPS * modes), F32)
    half_gain = (TAPS, modes, sensors)
    part, gain_rest, peak = call(
        own_body,
        (
            both,
            jax.ShapeDtypeStruct(half_gain, BF16),
            jax.ShapeDtypeStruct((8, modes), F32),
        ),
        scratch=[
            pltpu.VMEM((frames, sensors), BF16),
            pltpu.VMEM(half_gain, BF16),
            pltpu.SemaphoreType.DMA(((1 + 2 * TAPS) * PIECES,)),
        ],
        smem=(),
        whole=(0, 1),
        n_in=2,
    )(*(pltpu.with_memory_space_constraint(x, pltpu.HBM) for x in (record, gain)))
    here, onward = call(
        rest_body,
        (
            jax.ShapeDtypeStruct((frames, modes), F32),
            jax.ShapeDtypeStruct((DMAX, modes), F32),
        ),
        n_in=4,
    )(where, other, gain_rest, part)
    tail = lax.ppermute(onward, TM, [(i, i + 1) for i in range(planes * blocks - 1)])
    rate_t = behind(rate, here).T
    decay = jnp.exp(-rate_t)
    scale = jnp.sqrt(-jnp.expm1(-2.0 * rate_t))
    leak_row = leak[None]
    by_sensor = behind(record, here).T.reshape(planes, blocks, group, frames).swapaxes(0, 1)
    by_sensor = by_sensor.reshape(blocks, planes * group, frames)
    mine = lax.all_to_all(by_sensor, YX, 0, 0, tiled=True)
    keep, summary = call(
        local_body,
        (
            jax.ShapeDtypeStruct((6, frames, modes), F32),
            jax.ShapeDtypeStruct((blocks, 8, modes), F32),
        ),
        smem=(),
        n_in=6,
    )(here, tail, decay, scale, leak_row, peak)
    summary, mine = lax.optimization_barrier((summary, mine))
    plane = lax.all_to_all(summary, YX, 0, 0, tiled=True)
    plane_summary = call(
        plane_body, jax.ShapeDtypeStruct((planes, 8, modes), F32), smem=(), n_in=1
    )(plane)
    theirs = swapped(mine)
    every_plane = lax.all_to_all(plane_summary, Z, 0, 0, tiled=True)
    smoothed, resid, reach = call(
        finish_body,
        (
            jax.ShapeDtypeStruct((modes, frames), F32),
            jax.ShapeDtypeStruct((blocks, frames, modes), BF16),
            jax.ShapeDtypeStruct((2, planes, modes), F32),
        ),
        n_in=6,
    )(where, plane, every_plane, keep, decay, leak_row)
    resid_all = lax.all_to_all(resid, YX, 0, 0, tiled=True)
    tails = behind(jnp.stack([mine[-1], theirs[-1]]), resid)
    tails = lax.ppermute(tails, Z, [(i, i + 1) for i in range(planes - 1)])
    reach_other = swapped(reach)
    partial = call(
        gradient_body,
        jax.ShapeDtypeStruct((planes, 2, group, TAPS * modes), F32),
        scratch=[pltpu.VMEM(((blocks + 1) * frames, TAPS * modes), BF16)],
        n_in=7,
    )(where, tails, mine, theirs, resid_all, reach, reach_other)
    pieces = partial.reshape(planes * 2, group, TAPS * modes).astype(jnp.float16)
    pieces = lax.all_to_all(pieces, (Z, "state"), 0, 0, tiled=True)
    grad = call(
        functools.partial(total_body, span=float(blocks * frames)),
        jax.ShapeDtypeStruct((group, TAPS * 2 * modes), F32),
        n_in=4,
    )(where, pieces.astype(F32), reach, reach_other)
    return (smoothed, grad)


def solution(mesh):
    split = Mesh(
        mesh.devices.reshape(16, 4, 4, mesh.shape["state"]), ("tm_0", "tm_1", "tm_2", "state")
    )
    return jax.shard_map(
        per_device,
        mesh=split,
        in_specs=(P(TM, "state"), P(None, "state", None), P("state", TM), P("state"), P()),
        out_specs=(P("state", TM), P(STATE_TM, None)),
        check_vma=False,
    )
```

```python
import functools

import jax
import jax.numpy as jnp
from jax import lax
from jax.experimental import pallas as pl
from jax.experimental.pallas import tpu as pltpu
from jax.sharding import Mesh
from jax.sharding import PartitionSpec as P

TAPS = 2
TOP = 32768.0
PIECES = 1
DMAX = 64
Z = "tm_0"
YX = ("tm_1", "tm_2")
TM = ("tm_0", "tm_1", "tm_2")
STATE_TM = ("state", "tm_0", "tm_1", "tm_2")
F32 = jnp.float32
BF16 = jnp.bfloat16
VMEM = pl.BlockSpec(memory_space=pltpu.VMEM)
SMEM = pl.BlockSpec(memory_space=pltpu.SMEM)
WHOLE = pl.BlockSpec(memory_space=pltpu.HBM)
NT = (((1,), (1,)), ((), ()))


def call(body, outs, scratch=(), smem=(0,), whole=(), n_in=1):
    specs = [WHOLE if i in whole else SMEM if i in smem else VMEM for i in range(n_in)]
    return pl.pallas_call(
        body,
        out_shape=outs,
        in_specs=specs,
        out_specs=jax.tree.map(lambda _: VMEM, outs),
        scratch_shapes=scratch,
        compiler_params=pltpu.CompilerParams(vmem_limit_bytes=48 << 20),
    )


def later(x, k, fill):
    if k % 8 == 0:
        return jnp.concatenate([jnp.full((k, x.shape[1]), fill, x.dtype), x[:-k]], 0)
    row = lax.broadcasted_iota(jnp.int32, x.shape, 0)
    return jnp.where(row < k, fill, pltpu.roll(x, k, 0))


def earlier(x, k, fill):
    n = x.shape[0]
    if k % 8 == 0:
        return jnp.concatenate([x[k:], jnp.full((k, x.shape[1]), fill, x.dtype)], 0)
    row = lax.broadcasted_iota(jnp.int32, x.shape, 0)
    return jnp.where(row >= n - k, fill, pltpu.roll(x, n - k, 0))


def recur(link, sums, shift):
    k = 1
    while k < link.shape[0]:
        sums = [s + link * shift(s, k, 0.0) for s in sums]
        link = link * shift(link, k, 1.0)
        k *= 2
    return link, sums


def own_body(record, gain, out, gain_rest, peak, own, gain_own, arrived):
    modes = gain_own.shape[1]
    frames, half = own.shape
    core = lax.axis_index("state")
    mine = pl.multiple_of(core * half, half)
    theirs = pl.multiple_of((1 - core) * half, half)
    record_copies = []
    gain_copies = []
    rest_copies = []
    for piece in range(PIECES):
        rows = pl.ds(piece * (frames // PIECES), frames // PIECES)
        record_copies.append((record.at[rows], own.at[rows]))
    for k in range(TAPS):
        for piece in range(PIECES):
            rows = pl.ds(piece * (modes // PIECES), modes // PIECES)
            gain_copies.append((gain.at[k, rows, pl.ds(mine, half)], gain_own.at[k, rows]))
            rest_copies.append((gain.at[k, rows, pl.ds(theirs, half)], gain_rest.at[k, rows]))
    copies = [
        pltpu.make_async_copy(source, target, arrived.at[n])
        for n, (source, target) in enumerate(record_copies + gain_copies + rest_copies)
    ]
    for copy in copies:
        copy.start()
    for copy in copies[:PIECES]:
        copy.wait()
    largest = jnp.max(jnp.abs(own[...].astype(F32)), axis=0, keepdims=True)
    peak[...] = jnp.broadcast_to(jnp.max(largest, axis=1, keepdims=True), peak.shape)
    for k in range(TAPS):
        for copy in copies[(1 + k) * PIECES : (2 + k) * PIECES]:
            copy.wait()
        out[:, k * modes : (k + 1) * modes] = lax.dot_general(
            own[...], gain_own[k], NT, preferred_element_type=F32
        )
    for copy in copies[(1 + TAPS) * PIECES :]:
        copy.wait()


def onward_body(where, other, gain, part, out):
    modes = gain.shape[1]
    at = part.shape[0] - DMAX
    row = lax.broadcasted_iota(jnp.int32, out.shape, 0)
    total = jnp.zeros(out.shape, F32)
    for k in range(TAPS):
        u = part[at:, k * modes : (k + 1) * modes] + lax.dot_general(
            other[at:], gain[k], NT, preferred_element_type=F32
        )
        delayed = pltpu.roll(u, where[3 + k] % DMAX, 0)
        total += jnp.where(row < where[3 + k], delayed, 0.0)
    out[...] = total


def here_body(where, other, gain, part, onward, out):
    modes = gain.shape[1]
    row = lax.broadcasted_iota(jnp.int32, out.shape, 0)
    total = jnp.zeros(out.shape, F32)
    for k in range(TAPS):
        u = part[:, k * modes : (k + 1) * modes] + lax.dot_general(
            other[...], gain[k], NT, preferred_element_type=F32
        )
        delayed = pltpu.roll(u, where[3 + k], 0)
        total += jnp.where(row >= where[3 + k], delayed, 0.0)
    out[...] = total


def local_body(here, tail, decay_ref, scale, leak, by_sensor, peak, keep, sent):
    frames, modes = decay_ref.shape
    nothing = jnp.zeros((frames - DMAX, modes), F32)
    drive_in = here[...] + jnp.concatenate([tail[...], nothing], 0)
    drive = scale[...] * drive_in
    decay = decay_ref[...]
    prods, (offsets,) = recur(decay, [drive], later)
    kappa = 1.0 - leak[...]
    weight = 1.0 - kappa * decay * decay
    links, (base, slope) = recur(kappa * decay, [weight * offsets, weight * prods], earlier)
    keep[0] = prods
    keep[1] = offsets
    keep[2] = links
    keep[3] = base
    keep[4] = slope
    keep[5] = drive
    rows = [prods[-1:], offsets[-1:], links[:1], base[:1], slope[:1], decay[-1:]]
    rows += [jnp.max(jnp.abs(offsets), axis=0, keepdims=True), peak[:1]]
    rest = jnp.concatenate(rows, 0)
    frames_rows = by_sensor.shape[1]
    parts = []
    for _ in range(3):
        part = rest.astype(BF16)
        parts.append(part.astype(F32))
        rest = rest - parts[-1]
    coded = jnp.concatenate(parts, 0).astype(BF16)
    for i in range(sent.shape[0]):
        sent[i, :frames_rows] = by_sensor[i]
        sent[i, frames_rows:] = coded


def decoded(every, out):
    at = every.shape[1] - 24
    for i in range(every.shape[0]):
        rows = every[i, at:].astype(F32)
        out[i] = rows[:8] + rows[8:16] + rows[16:]


def joined(first, second):
    p1, o1, l1, b1, s1 = first
    p2, o2, l2, b2, s2 = second
    return (p1 * p2, p2 * o1 + o2, l1 * l2, b1 + l1 * (b2 + s2 * o1), s1 + l1 * s2 * p1)


def five(ref, i):
    return tuple(ref[i, r : r + 1] for r in range(5))


def plane_body(sent, every, out):
    n = sent.shape[0]
    decoded(sent, every)
    parts = [five(every, i) for i in range(n)]
    while len(parts) > 1:
        parts = [joined(parts[i], parts[i + 1]) for i in range(0, len(parts), 2)]
    state = jnp.zeros_like(every[0, :1])
    reach = state
    peak = state
    for i in range(n):
        reach = jnp.maximum(reach, every[i, 6:7] + jnp.abs(state))
        peak = jnp.maximum(peak, every[i, 7:8])
        state = every[i, 0:1] * state + every[i, 1:2]
    rows = list(parts[0]) + [every[n - 1, 5:6], reach, peak]
    for r, row in enumerate(rows):
        for i in range(out.shape[0]):
            out[i, r : r + 1] = row


def ends(every, position, entering, closing, last):
    n = every.shape[0]
    states = []
    state = entering
    before = last
    own_state = jnp.zeros_like(entering)
    own_last = jnp.zeros_like(entering)
    for i in range(n):
        states.append(state)
        own_state = jnp.where(position == i, state, own_state)
        own_last = jnp.where(position == i, before, own_last)
        state = every[i, 0:1] * state + every[i, 1:2]
        before = every[i, 5:6]
    after = closing
    afters = [after] * n
    own_after = jnp.zeros_like(entering)
    for i in reversed(range(n)):
        afters[i] = after
        own_after = jnp.where(position == i, after, own_after)
        after = every[i, 2:3] * after + every[i, 3:4] + every[i, 4:5] * states[i]
    return own_state, own_after, own_last, states, afters


def finish_body(where, plane, planes, keep, decay_ref, leak, smoothed_out, resid_out, reach):
    zero = jnp.zeros((1, decay_ref.shape[1]), F32)
    entering, after, last, states, afters = ends(planes, where[0], zero, zero, zero)
    peaks = [zero]
    bound = []
    for i in range(planes.shape[0]):
        bound.append(6.0 * (planes[i, 6:7] + jnp.abs(states[i])) + 2.0 * jnp.abs(afters[i]))
        peaks.append(planes[i, 7:8])
    bound = jnp.concatenate(bound, 0)
    reach[0] = jnp.broadcast_to(jnp.max(bound, axis=1, keepdims=True), bound.shape)
    reach[1] = jnp.maximum(jnp.concatenate(peaks[:-1], 0), jnp.concatenate(peaks[1:], 0))
    entering, after, last, _, _ = ends(plane, where[1], entering, after, last)
    smoothed = keep[3] + keep[4] * entering + keep[2] * after
    decay = decay_ref[...]
    kappa = 1.0 - leak[...]
    prior = (1.0 - kappa * last * last) * entering + kappa * last * smoothed[:1]
    first = jnp.logical_and(where[0] == 0, where[1] == 0)
    prior = jnp.where(first, 0.0, prior)
    row = lax.broadcasted_iota(jnp.int32, smoothed.shape, 0)
    shifted = jnp.where(row == 0, prior, pltpu.roll(smoothed, 1, 0))
    resid = (smoothed - decay * shifted - keep[5]).astype(BF16)
    smoothed_out[...] = smoothed.T
    for i in range(resid_out.shape[0]):
        resid_out[i] = resid


def bounds(first, second, span):
    return jnp.maximum(span * first[0] * jnp.maximum(first[1], second[1]), 1e-30)


def gradient_body(where, tails, own, other, resid, reach, reach_other, out, padded):
    blocks, frames, modes = resid.shape
    row = lax.broadcasted_iota(jnp.int32, (frames, 2 * frames), 0)
    column = lax.broadcasted_iota(jnp.int32, (frames, 2 * frames), 1)
    picks = jnp.concatenate(
        [(column == row + where[3 + k]).astype(F32).astype(BF16) for k in range(TAPS)], 0
    )
    nothing = jnp.zeros((frames, modes), BF16)
    for b in range(blocks + 1):
        pair = jnp.concatenate(
            [resid[b - 1] if b > 0 else nothing, resid[b] if b < blocks else nothing], 0
        )
        moved = jnp.dot(picks, pair, preferred_element_type=F32).astype(BF16)
        for k in range(TAPS):
            padded[b * frames : (b + 1) * frames, k * modes : (k + 1) * modes] = moved[
                k * frames : (k + 1) * frames
            ]
    rhs = padded[...]
    bound = bounds(reach, reach_other, float(blocks * frames))
    plane = lax.broadcasted_iota(jnp.int32, bound.shape, 0)
    factor = jnp.sum(jnp.where(plane == where[0], TOP / bound, 0.0), axis=0, keepdims=True)
    factor = jnp.concatenate([factor] * TAPS, 1)
    for which, (before, rows) in enumerate(((tails[0], own), (tails[1], other))):
        lhs = jnp.concatenate(
            [before] + [rows[i, : before.shape[0]] for i in range(blocks)], 1
        )
        sums = jnp.dot(lhs, rhs, preferred_element_type=F32) * factor
        half = jnp.where(where[2] == which, 0, 1)
        for i in range(out.shape[0]):
            out[i, half] = sums[i * 8 : (i + 1) * 8]


def total_body(where, pieces, reach, reach_other, out, *, span):
    modes = out.shape[1] // TAPS // 2
    pair = (bounds(reach, reach_other, span) / TOP, bounds(reach_other, reach, span) / TOP)
    for core in range(2):
        factor = jnp.where(where[2] == core, pair[0], pair[1])
        factor = jnp.concatenate([factor] * TAPS, 1)
        total = pieces[core] * factor[:1]
        for i in range(1, factor.shape[0]):
            total += pieces[2 * i + core] * factor[i : i + 1]
        for k in range(TAPS):
            column = (2 * k + core) * modes
            out[:, column : column + modes] = total[:, k * modes : (k + 1) * modes]


def behind(x, first):
    return lax.optimization_barrier((x, first))[0]


def swapped(x):
    return lax.ppermute(x, "state", [(0, 1), (1, 0)])


def per_device(record, gain, rate, leak, dilation):
    frames, sensors = record.shape
    modes = rate.shape[0]
    planes = lax.axis_size(Z)
    blocks = lax.axis_size(YX)
    where = jnp.concatenate(
        [
            jnp.stack([lax.axis_index(Z), lax.axis_index(YX), lax.axis_index("state")]).astype(jnp.int32),
            dilation,
        ]
    )
    other = swapped(record)
    group = sensors // planes // blocks
    both = jax.ShapeDtypeStruct((frames, TAPS * modes), F32)
    half_gain = (TAPS, modes, sensors)
    part, gain_rest, peak = call(
        own_body,
        (
            both,
            jax.ShapeDtypeStruct(half_gain, BF16),
            jax.ShapeDtypeStruct((8, modes), F32),
        ),
        scratch=[
            pltpu.VMEM((frames, sensors), BF16),
            pltpu.VMEM(half_gain, BF16),
            pltpu.SemaphoreType.DMA(((1 + 2 * TAPS) * PIECES,)),
        ],
        smem=(),
        whole=(0, 1),
        n_in=2,
    )(*(pltpu.with_memory_space_constraint(x, pltpu.HBM) for x in (record, gain)))
    onward = call(onward_body, jax.ShapeDtypeStruct((DMAX, modes), F32), n_in=4)(
        where, other, gain_rest, part
    )
    here = call(here_body, jax.ShapeDtypeStruct((frames, modes), F32), n_in=5)(
        where, other, gain_rest, part, onward
    )
    tail = lax.ppermute(onward, TM, [(i, i + 1) for i in range(planes * blocks - 1)])
    rate_t = behind(rate, here).T
    decay = jnp.exp(-rate_t)
    scale = jnp.sqrt(-jnp.expm1(-2.0 * rate_t))
    leak_row = leak[None]
    by_sensor = behind(record, here).T.reshape(planes, blocks, group, frames).swapaxes(0, 1)
    by_sensor = by_sensor.reshape(blocks, planes * group, frames)
    keep, sent = call(
        local_body,
        (
            jax.ShapeDtypeStruct((6, frames, modes), F32),
            jax.ShapeDtypeStruct((blocks, planes * group + 24, frames), BF16),
        ),
        smem=(),
        n_in=7,
    )(here, tail, decay, scale, leak_row, by_sensor, peak)
    mine = lax.all_to_all(sent, YX, 0, 0, tiled=True)
    plane, plane_summary = call(
        plane_body,
        (
            jax.ShapeDtypeStruct((blocks, 8, modes), F32),
            jax.ShapeDtypeStruct((planes, 8, modes), F32),
        ),
        smem=(),
        n_in=1,
    )(mine)
    theirs = swapped(mine[:, :-24])
    every_plane = lax.all_to_all(plane_summary, Z, 0, 0, tiled=True)
    smoothed, resid, reach = call(
        finish_body,
        (
            jax.ShapeDtypeStruct((modes, frames), F32),
            jax.ShapeDtypeStruct((blocks, frames, modes), BF16),
            jax.ShapeDtypeStruct((2, planes, modes), F32),
        ),
        n_in=6,
    )(where, plane, every_plane, keep, decay, leak_row)
    resid_all = lax.all_to_all(resid, YX, 0, 0, tiled=True)
    tails = behind(jnp.stack([mine[-1, :-24], theirs[-1]]), resid)
    tails = lax.ppermute(tails, Z, [(i, i + 1) for i in range(planes - 1)])
    reach_other = swapped(reach)
    partial = call(
        gradient_body,
        jax.ShapeDtypeStruct((planes, 2, group, TAPS * modes), F32),
        scratch=[pltpu.VMEM(((blocks + 1) * frames, TAPS * modes), BF16)],
        n_in=7,
    )(where, tails, mine, theirs, resid_all, reach, reach_other)
    pieces = partial.reshape(planes * 2, group, TAPS * modes).astype(jnp.float16)
    pieces = lax.all_to_all(pieces, (Z, "state"), 0, 0, tiled=True)
    grad = call(
        functools.partial(total_body, span=float(blocks * frames)),
        jax.ShapeDtypeStruct((group, TAPS * 2 * modes), F32),
        n_in=4,
    )(where, pieces.astype(F32), reach, reach_other)
    return (smoothed, grad)


def solution(mesh):
    split = Mesh(
        mesh.devices.reshape(16, 4, 4, mesh.shape["state"]), ("tm_0", "tm_1", "tm_2", "state")
    )
    return jax.shard_map(
        per_device,
        mesh=split,
        in_specs=(P(TM, "state"), P(None, "state", None), P("state", TM), P("state"), P()),
        out_specs=(P("state", TM), P(STATE_TM, None)),
        check_vma=False,
    )
```

```python
import functools

import jax
import jax.numpy as jnp
from jax import lax
from jax.experimental import pallas as pl
from jax.experimental.pallas import tpu as pltpu
from jax.sharding import Mesh
from jax.sharding import PartitionSpec as P

TAPS = 2
TOP = 32768.0
PIECES = 1
DMAX = 64
Z = "tm_0"
YX = ("tm_1", "tm_2")
TM = ("tm_0", "tm_1", "tm_2")
STATE_TM = ("state", "tm_0", "tm_1", "tm_2")
F32 = jnp.float32
BF16 = jnp.bfloat16
VMEM = pl.BlockSpec(memory_space=pltpu.VMEM)
WHOLE = pl.BlockSpec(memory_space=pltpu.HBM)
NT = (((1,), (1,)), ((), ()))


def call(body, outs, scratch=(), whole=(), n_in=1):
    specs = [WHOLE if i in whole else VMEM for i in range(n_in)]
    return pl.pallas_call(
        body,
        out_shape=outs,
        in_specs=specs,
        out_specs=jax.tree.map(lambda _: VMEM, outs),
        scratch_shapes=scratch,
        compiler_params=pltpu.CompilerParams(vmem_limit_bytes=48 << 20),
    )


def later(x, k, fill):
    if k % 8 == 0:
        return jnp.concatenate([jnp.full((k, x.shape[1]), fill, x.dtype), x[:-k]], 0)
    row = lax.broadcasted_iota(jnp.int32, x.shape, 0)
    return jnp.where(row < k, fill, pltpu.roll(x, k, 0))


def earlier(x, k, fill):
    n = x.shape[0]
    if k % 8 == 0:
        return jnp.concatenate([x[k:], jnp.full((k, x.shape[1]), fill, x.dtype)], 0)
    row = lax.broadcasted_iota(jnp.int32, x.shape, 0)
    return jnp.where(row >= n - k, fill, pltpu.roll(x, n - k, 0))


def recur(link, sums, shift):
    k = 1
    while k < link.shape[0]:
        sums = [s + link * shift(s, k, 0.0) for s in sums]
        link = link * shift(link, k, 1.0)
        k *= 2
    return link, sums


def own_body(record, gain, out, gain_rest, peak, own, gain_own, arrived):
    modes = gain_own.shape[1]
    frames, half = own.shape
    core = lax.axis_index("state")
    mine = pl.multiple_of(core * half, half)
    theirs = pl.multiple_of((1 - core) * half, half)
    record_copies = []
    gain_copies = []
    rest_copies = []
    for piece in range(PIECES):
        rows = pl.ds(piece * (frames // PIECES), frames // PIECES)
        record_copies.append((record.at[rows], own.at[rows]))
    for k in range(TAPS):
        for piece in range(PIECES):
            rows = pl.ds(piece * (modes // PIECES), modes // PIECES)
            gain_copies.append((gain.at[k, rows, pl.ds(mine, half)], gain_own.at[k, rows]))
            rest_copies.append((gain.at[k, rows, pl.ds(theirs, half)], gain_rest.at[k, rows]))
    copies = [
        pltpu.make_async_copy(source, target, arrived.at[n])
        for n, (source, target) in enumerate(record_copies + gain_copies + rest_copies)
    ]
    for copy in copies:
        copy.start()
    for copy in copies[:PIECES]:
        copy.wait()
    largest = jnp.max(jnp.abs(own[...].astype(F32)), axis=0, keepdims=True)
    peak[...] = jnp.broadcast_to(jnp.max(largest, axis=1, keepdims=True), peak.shape)
    for k in range(TAPS):
        for copy in copies[(1 + k) * PIECES : (2 + k) * PIECES]:
            copy.wait()
        out[:, k * modes : (k + 1) * modes] = lax.dot_general(
            own[...], gain_own[k], NT, preferred_element_type=F32
        )
    for copy in copies[(1 + TAPS) * PIECES :]:
        copy.wait()


def moved(delay, rows, ahead, values):
    shape = (rows, values.shape[0])
    row = lax.broadcasted_iota(jnp.int32, shape, 0)
    column = lax.broadcasted_iota(jnp.int32, shape, 1)
    pick = (column + delay[:, : shape[1]] == row + ahead).astype(F32)
    return jnp.dot(
        pick, values, precision=lax.Precision.HIGHEST, preferred_element_type=F32
    )


def onward_body(delays, other, gain, part, out):
    modes = gain.shape[1]
    at = part.shape[0] - DMAX
    total = jnp.zeros(out.shape, F32)
    for k in range(TAPS):
        u = part[at:, k * modes : (k + 1) * modes] + lax.dot_general(
            other[at:], gain[k], NT, preferred_element_type=F32
        )
        total += moved(delays[k : k + 1], DMAX, DMAX, u)
    out[...] = total


def here_body(delays, other, gain, part, onward, out):
    modes = gain.shape[1]
    total = jnp.zeros(out.shape, F32)
    for k in range(TAPS):
        u = part[:, k * modes : (k + 1) * modes] + lax.dot_general(
            other[...], gain[k], NT, preferred_element_type=F32
        )
        total += moved(delays[k : k + 1], u.shape[0], 0, u)
    out[...] = total


def local_body(here, tail, decay_ref, scale, leak, by_sensor, peak, keep, sent):
    frames, modes = decay_ref.shape
    nothing = jnp.zeros((frames - DMAX, modes), F32)
    drive_in = here[...] + jnp.concatenate([tail[...], nothing], 0)
    drive = scale[...] * drive_in
    decay = decay_ref[...]
    prods, (offsets,) = recur(decay, [drive], later)
    kappa = 1.0 - leak[...]
    weight = 1.0 - kappa * decay * decay
    links, (base, slope) = recur(kappa * decay, [weight * offsets, weight * prods], earlier)
    keep[0] = prods
    keep[1] = offsets
    keep[2] = links
    keep[3] = base
    keep[4] = slope
    keep[5] = drive
    rows = [prods[-1:], offsets[-1:], links[:1], base[:1], slope[:1], decay[-1:]]
    rows += [jnp.max(jnp.abs(offsets), axis=0, keepdims=True), peak[:1]]
    rest = jnp.concatenate(rows, 0)
    frames_rows = by_sensor.shape[1]
    parts = []
    for _ in range(3):
        part = rest.astype(BF16)
        parts.append(part.astype(F32))
        rest = rest - parts[-1]
    coded = jnp.concatenate(parts, 0).astype(BF16)
    for i in range(sent.shape[0]):
        sent[i, :frames_rows] = by_sensor[i]
        sent[i, frames_rows:] = coded


def decoded(every, out):
    at = every.shape[1] - 24
    for i in range(every.shape[0]):
        rows = every[i, at:].astype(F32)
        out[i] = rows[:8] + rows[8:16] + rows[16:]


def joined(first, second):
    p1, o1, l1, b1, s1 = first
    p2, o2, l2, b2, s2 = second
    return (p1 * p2, p2 * o1 + o2, l1 * l2, b1 + l1 * (b2 + s2 * o1), s1 + l1 * s2 * p1)


def five(ref, i):
    return tuple(ref[i, r : r + 1] for r in range(5))


def plane_body(sent, every, out):
    n = sent.shape[0]
    decoded(sent, every)
    parts = [five(every, i) for i in range(n)]
    while len(parts) > 1:
        parts = [joined(parts[i], parts[i + 1]) for i in range(0, len(parts), 2)]
    state = jnp.zeros_like(every[0, :1])
    reach = state
    peak = state
    for i in range(n):
        reach = jnp.maximum(reach, every[i, 6:7] + jnp.abs(state))
        peak = jnp.maximum(peak, every[i, 7:8])
        state = every[i, 0:1] * state + every[i, 1:2]
    rows = list(parts[0]) + [every[n - 1, 5:6], reach, peak]
    for r, row in enumerate(rows):
        for i in range(out.shape[0]):
            out[i, r : r + 1] = row


def ends(every, position, entering, closing, last):
    n = every.shape[0]
    states = []
    state = entering
    before = last
    own_state = jnp.zeros_like(entering)
    own_last = jnp.zeros_like(entering)
    for i in range(n):
        states.append(state)
        own_state = jnp.where(position == i, state, own_state)
        own_last = jnp.where(position == i, before, own_last)
        state = every[i, 0:1] * state + every[i, 1:2]
        before = every[i, 5:6]
    after = closing
    afters = [after] * n
    own_after = jnp.zeros_like(entering)
    for i in reversed(range(n)):
        afters[i] = after
        own_after = jnp.where(position == i, after, own_after)
        after = every[i, 2:3] * after + every[i, 3:4] + every[i, 4:5] * states[i]
    return own_state, own_after, own_last, states, afters


def finish_body(plane, planes, keep, decay_ref, leak, smoothed_out, resid_out, reach):
    at_plane = lax.axis_index(Z)
    at_block = lax.axis_index(YX)
    zero = jnp.zeros((1, decay_ref.shape[1]), F32)
    entering, after, last, states, afters = ends(planes, at_plane, zero, zero, zero)
    peaks = [zero]
    bound = []
    for i in range(planes.shape[0]):
        bound.append(6.0 * (planes[i, 6:7] + jnp.abs(states[i])) + 2.0 * jnp.abs(afters[i]))
        peaks.append(planes[i, 7:8])
    bound = jnp.concatenate(bound, 0)
    reach[0] = jnp.broadcast_to(jnp.max(bound, axis=1, keepdims=True), bound.shape)
    reach[1] = jnp.maximum(jnp.concatenate(peaks[:-1], 0), jnp.concatenate(peaks[1:], 0))
    entering, after, last, _, _ = ends(plane, at_block, entering, after, last)
    smoothed = keep[3] + keep[4] * entering + keep[2] * after
    decay = decay_ref[...]
    kappa = 1.0 - leak[...]
    prior = (1.0 - kappa * last * last) * entering + kappa * last * smoothed[:1]
    first = jnp.logical_and(at_plane == 0, at_block == 0)
    prior = jnp.where(first, 0.0, prior)
    row = lax.broadcasted_iota(jnp.int32, smoothed.shape, 0)
    shifted = jnp.where(row == 0, prior, pltpu.roll(smoothed, 1, 0))
    resid = (smoothed - decay * shifted - keep[5]).astype(BF16)
    smoothed_out[...] = smoothed.T
    for i in range(resid_out.shape[0]):
        resid_out[i] = resid


def bounds(first, second, span):
    return jnp.maximum(span * first[0] * jnp.maximum(first[1], second[1]), 1e-30)


def gradient_body(delays, tails, own, other, resid, reach, reach_other, out, padded):
    blocks, frames, modes = resid.shape
    row = lax.broadcasted_iota(jnp.int32, (frames, 2 * frames), 0)
    column = lax.broadcasted_iota(jnp.int32, (frames, 2 * frames), 1)
    picks = jnp.concatenate(
        [(column == row + delays[k : k + 1, : 2 * frames]).astype(F32).astype(BF16) for k in range(TAPS)], 0
    )
    nothing = jnp.zeros((frames, modes), BF16)
    for b in range(blocks + 1):
        pair = jnp.concatenate(
            [resid[b - 1] if b > 0 else nothing, resid[b] if b < blocks else nothing], 0
        )
        moved = jnp.dot(picks, pair, preferred_element_type=F32).astype(BF16)
        for k in range(TAPS):
            padded[b * frames : (b + 1) * frames, k * modes : (k + 1) * modes] = moved[
                k * frames : (k + 1) * frames
            ]
    rhs = padded[...]
    bound = bounds(reach, reach_other, float(blocks * frames))
    plane = lax.broadcasted_iota(jnp.int32, bound.shape, 0)
    factor = jnp.sum(jnp.where(plane == lax.axis_index(Z), TOP / bound, 0.0), axis=0, keepdims=True)
    factor = jnp.concatenate([factor] * TAPS, 1)
    for which, (before, rows) in enumerate(((tails[0], own), (tails[1], other))):
        lhs = jnp.concatenate(
            [before] + [rows[i, : before.shape[0]] for i in range(blocks)], 1
        )
        sums = jnp.dot(lhs, rhs, preferred_element_type=F32) * factor
        half = jnp.where(lax.axis_index("state") == which, 0, 1)
        for i in range(out.shape[0]):
            out[i, half] = sums[i * 8 : (i + 1) * 8]


def total_body(pieces, reach, reach_other, out, *, span):
    modes = out.shape[1] // TAPS // 2
    pair = (bounds(reach, reach_other, span) / TOP, bounds(reach_other, reach, span) / TOP)
    for core in range(2):
        factor = jnp.where(lax.axis_index("state") == core, pair[0], pair[1])
        factor = jnp.concatenate([factor] * TAPS, 1)
        total = pieces[core] * factor[:1]
        for i in range(1, factor.shape[0]):
            total += pieces[2 * i + core] * factor[i : i + 1]
        for k in range(TAPS):
            column = (2 * k + core) * modes
            out[:, column : column + modes] = total[:, k * modes : (k + 1) * modes]


def behind(x, first):
    return lax.optimization_barrier((x, first))[0]


def swapped(x):
    return lax.ppermute(x, "state", [(0, 1), (1, 0)])


def per_device(record, gain, rate, leak, dilation):
    frames, sensors = record.shape
    modes = rate.shape[0]
    planes = lax.axis_size(Z)
    blocks = lax.axis_size(YX)
    delays = jnp.broadcast_to(dilation[:, None], (TAPS, 2 * frames))
    other = swapped(record)
    group = sensors // planes // blocks
    both = jax.ShapeDtypeStruct((frames, TAPS * modes), F32)
    half_gain = (TAPS, modes, sensors)
    part, gain_rest, peak = call(
        own_body,
        (
            both,
            jax.ShapeDtypeStruct(half_gain, BF16),
            jax.ShapeDtypeStruct((8, modes), F32),
        ),
        scratch=[
            pltpu.VMEM((frames, sensors), BF16),
            pltpu.VMEM(half_gain, BF16),
            pltpu.SemaphoreType.DMA(((1 + 2 * TAPS) * PIECES,)),
        ],
        whole=(0, 1),
        n_in=2,
    )(*(pltpu.with_memory_space_constraint(x, pltpu.HBM) for x in (record, gain)))
    onward = call(onward_body, jax.ShapeDtypeStruct((DMAX, modes), F32), n_in=4)(
        delays, other, gain_rest, part
    )
    here = call(here_body, jax.ShapeDtypeStruct((frames, modes), F32), n_in=5)(
        delays, other, gain_rest, part, onward
    )
    tail = lax.ppermute(onward, TM, [(i, i + 1) for i in range(planes * blocks - 1)])
    rate_t = behind(rate, here).T
    decay = jnp.exp(-rate_t)
    scale = jnp.sqrt(-jnp.expm1(-2.0 * rate_t))
    leak_row = leak[None]
    by_sensor = behind(record, here).T.reshape(planes, blocks, group, frames).swapaxes(0, 1)
    by_sensor = by_sensor.reshape(blocks, planes * group, frames)
    keep, sent = call(
        local_body,
        (
            jax.ShapeDtypeStruct((6, frames, modes), F32),
            jax.ShapeDtypeStruct((blocks, planes * group + 24, frames), BF16),
        ),
        n_in=7,
    )(here, tail, decay, scale, leak_row, by_sensor, peak)
    mine = lax.all_to_all(sent, YX, 0, 0, tiled=True)
    plane, plane_summary = call(
        plane_body,
        (
            jax.ShapeDtypeStruct((blocks, 8, modes), F32),
            jax.ShapeDtypeStruct((planes, 8, modes), F32),
        ),
        n_in=1,
    )(mine)
    theirs = swapped(mine[:, :-24])
    every_plane = lax.all_to_all(plane_summary, Z, 0, 0, tiled=True)
    smoothed, resid, reach = call(
        finish_body,
        (
            jax.ShapeDtypeStruct((modes, frames), F32),
            jax.ShapeDtypeStruct((blocks, frames, modes), BF16),
            jax.ShapeDtypeStruct((2, planes, modes), F32),
        ),
        n_in=5,
    )(plane, every_plane, keep, decay, leak_row)
    resid_all = lax.all_to_all(resid, YX, 0, 0, tiled=True)
    tails = behind(jnp.stack([mine[-1, :-24], theirs[-1]]), resid)
    tails = lax.ppermute(tails, Z, [(i, i + 1) for i in range(planes - 1)])
    reach_other = swapped(reach)
    partial = call(
        gradient_body,
        jax.ShapeDtypeStruct((planes, 2, group, TAPS * modes), F32),
        scratch=[pltpu.VMEM(((blocks + 1) * frames, TAPS * modes), BF16)],
        n_in=7,
    )(delays, tails, mine, theirs, resid_all, reach, reach_other)
    pieces = partial.reshape(planes * 2, group, TAPS * modes).astype(jnp.float16)
    pieces = lax.all_to_all(pieces, (Z, "state"), 0, 0, tiled=True)
    grad = call(
        functools.partial(total_body, span=float(blocks * frames)),
        jax.ShapeDtypeStruct((group, TAPS * 2 * modes), F32),
        n_in=3,
    )(pieces.astype(F32), reach, reach_other)
    return (smoothed, grad)


def solution(mesh):
    split = Mesh(
        mesh.devices.reshape(16, 4, 4, mesh.shape["state"]), ("tm_0", "tm_1", "tm_2", "state")
    )
    return jax.shard_map(
        per_device,
        mesh=split,
        in_specs=(P(TM, "state"), P(None, "state", None), P("state", TM), P("state"), P()),
        out_specs=(P("state", TM), P(STATE_TM, None)),
        check_vma=False,
    )
```

```python
import functools

import jax
import jax.numpy as jnp
from jax import lax
from jax.experimental import pallas as pl
from jax.experimental.pallas import tpu as pltpu
from jax.sharding import Mesh
from jax.sharding import PartitionSpec as P

TAPS = 2
TOP = 32768.0
PIECES = 1
DMAX = 64
Z = "tm_0"
YX = ("tm_1", "tm_2")
TM = ("tm_0", "tm_1", "tm_2")
STATE_TM = ("state", "tm_0", "tm_1", "tm_2")
F32 = jnp.float32
BF16 = jnp.bfloat16
VMEM = pl.BlockSpec(memory_space=pltpu.VMEM)
WHOLE = pl.BlockSpec(memory_space=pltpu.HBM)
NT = (((1,), (1,)), ((), ()))


def call(body, outs, scratch=(), whole=(), n_in=1):
    specs = [WHOLE if i in whole else VMEM for i in range(n_in)]
    return pl.pallas_call(
        body,
        out_shape=outs,
        in_specs=specs,
        out_specs=jax.tree.map(lambda _: VMEM, outs),
        scratch_shapes=scratch,
        compiler_params=pltpu.CompilerParams(vmem_limit_bytes=48 << 20),
    )


def later(x, k, fill):
    if k % 8 == 0:
        return jnp.concatenate([jnp.full((k, x.shape[1]), fill, x.dtype), x[:-k]], 0)
    row = lax.broadcasted_iota(jnp.int32, x.shape, 0)
    return jnp.where(row < k, fill, pltpu.roll(x, k, 0))


def earlier(x, k, fill):
    n = x.shape[0]
    if k % 8 == 0:
        return jnp.concatenate([x[k:], jnp.full((k, x.shape[1]), fill, x.dtype)], 0)
    row = lax.broadcasted_iota(jnp.int32, x.shape, 0)
    return jnp.where(row >= n - k, fill, pltpu.roll(x, n - k, 0))


def recur(link, sums, shift):
    k = 1
    while k < link.shape[0]:
        sums = [s + link * shift(s, k, 0.0) for s in sums]
        link = link * shift(link, k, 1.0)
        k *= 2
    return link, sums


def own_body(record, gain, out, gain_rest, peak, own, gain_own, arrived):
    modes = gain_own.shape[1]
    frames, half = own.shape
    core = lax.axis_index("state")
    mine = pl.multiple_of(core * half, half)
    theirs = pl.multiple_of((1 - core) * half, half)
    record_copies = []
    gain_copies = []
    rest_copies = []
    for piece in range(PIECES):
        rows = pl.ds(piece * (frames // PIECES), frames // PIECES)
        record_copies.append((record.at[rows], own.at[rows]))
    for k in range(TAPS):
        for piece in range(PIECES):
            rows = pl.ds(piece * (modes // PIECES), modes // PIECES)
            gain_copies.append((gain.at[k, rows, pl.ds(mine, half)], gain_own.at[k, rows]))
            rest_copies.append((gain.at[k, rows, pl.ds(theirs, half)], gain_rest.at[k, rows]))
    copies = [
        pltpu.make_async_copy(source, target, arrived.at[n])
        for n, (source, target) in enumerate(record_copies + gain_copies + rest_copies)
    ]
    for copy in copies:
        copy.start()
    for copy in copies[:PIECES]:
        copy.wait()
    largest = jnp.max(jnp.abs(own[...].astype(F32)), axis=0, keepdims=True)
    peak[...] = jnp.broadcast_to(jnp.max(largest, axis=1, keepdims=True), peak.shape)
    for k in range(TAPS):
        for copy in copies[(1 + k) * PIECES : (2 + k) * PIECES]:
            copy.wait()
        out[:, k * modes : (k + 1) * modes] = lax.dot_general(
            own[...], gain_own[k], NT, preferred_element_type=F32
        )
    for copy in copies[(1 + TAPS) * PIECES :]:
        copy.wait()


def moved(delay, rows, ahead, values):
    shape = (rows, values.shape[0])
    row = lax.broadcasted_iota(jnp.int32, shape, 0)
    column = lax.broadcasted_iota(jnp.int32, shape, 1)
    pick = (column + delay[:, : shape[1]] == row + ahead).astype(F32)
    return jnp.dot(
        pick, values, precision=lax.Precision.HIGHEST, preferred_element_type=F32
    )


def onward_body(delays, other, gain, part, out):
    modes = gain.shape[1]
    at = part.shape[0] - DMAX
    total = jnp.zeros(out.shape, F32)
    for k in range(TAPS):
        u = part[at:, k * modes : (k + 1) * modes] + lax.dot_general(
            other[at:], gain[k], NT, preferred_element_type=F32
        )
        total += moved(delays[k : k + 1], DMAX, DMAX, u)
    out[...] = total


def here_body(delays, other, gain, part, onward, out):
    modes = gain.shape[1]
    total = jnp.zeros(out.shape, F32)
    for k in range(TAPS):
        u = part[:, k * modes : (k + 1) * modes] + lax.dot_general(
            other[...], gain[k], NT, preferred_element_type=F32
        )
        total += moved(delays[k : k + 1], u.shape[0], 0, u)
    out[...] = total


def local_body(here, tail, decay_ref, scale, leak, by_sensor, peak, keep, sent):
    frames, modes = decay_ref.shape
    nothing = jnp.zeros((frames - DMAX, modes), F32)
    drive_in = here[...] + jnp.concatenate([tail[...], nothing], 0)
    drive = scale[...] * drive_in
    decay = decay_ref[...]
    prods, (offsets,) = recur(decay, [drive], later)
    kappa = 1.0 - leak[...]
    weight = 1.0 - kappa * decay * decay
    links, (base, slope) = recur(kappa * decay, [weight * offsets, weight * prods], earlier)
    keep[0] = prods
    keep[1] = offsets
    keep[2] = links
    keep[3] = base
    keep[4] = slope
    keep[5] = drive
    rows = [prods[-1:], offsets[-1:], links[:1], base[:1], slope[:1], decay[-1:]]
    rows += [jnp.max(jnp.abs(offsets), axis=0, keepdims=True), peak[:1]]
    rest = jnp.concatenate(rows, 0)
    frames_rows = by_sensor.shape[1]
    parts = []
    for _ in range(3):
        part = rest.astype(BF16)
        parts.append(part.astype(F32))
        rest = rest - parts[-1]
    coded = jnp.concatenate(parts, 0).astype(BF16)
    for i in range(sent.shape[0]):
        sent[i, :frames_rows] = by_sensor[i]
        sent[i, frames_rows:] = coded


def decoded(every, out):
    at = every.shape[1] - 24
    for i in range(every.shape[0]):
        rows = every[i, at:].astype(F32)
        out[i] = rows[:8] + rows[8:16] + rows[16:]


def joined(first, second):
    p1, o1, l1, b1, s1 = first
    p2, o2, l2, b2, s2 = second
    return (p1 * p2, p2 * o1 + o2, l1 * l2, b1 + l1 * (b2 + s2 * o1), s1 + l1 * s2 * p1)


def five(ref, i):
    return tuple(ref[i, r : r + 1] for r in range(5))


def plane_body(sent, every, out):
    n = sent.shape[0]
    decoded(sent, every)
    parts = [five(every, i) for i in range(n)]
    while len(parts) > 1:
        parts = [joined(parts[i], parts[i + 1]) for i in range(0, len(parts), 2)]
    state = jnp.zeros_like(every[0, :1])
    reach = state
    peak = state
    for i in range(n):
        reach = jnp.maximum(reach, every[i, 6:7] + jnp.abs(state))
        peak = jnp.maximum(peak, every[i, 7:8])
        state = every[i, 0:1] * state + every[i, 1:2]
    rows = list(parts[0]) + [every[n - 1, 5:6], reach, peak]
    for r, row in enumerate(rows):
        for i in range(out.shape[0]):
            out[i, r : r + 1] = row


def ends(every, position, entering, closing, last):
    n = every.shape[0]
    states = []
    state = entering
    before = last
    own_state = jnp.zeros_like(entering)
    own_last = jnp.zeros_like(entering)
    for i in range(n):
        states.append(state)
        own_state = jnp.where(position == i, state, own_state)
        own_last = jnp.where(position == i, before, own_last)
        state = every[i, 0:1] * state + every[i, 1:2]
        before = every[i, 5:6]
    after = closing
    afters = [after] * n
    own_after = jnp.zeros_like(entering)
    for i in reversed(range(n)):
        afters[i] = after
        own_after = jnp.where(position == i, after, own_after)
        after = every[i, 2:3] * after + every[i, 3:4] + every[i, 4:5] * states[i]
    return own_state, own_after, own_last, states, afters


def finish_body(plane, planes, keep, decay_ref, leak, smoothed_out, resid_out, reach):
    at_plane = lax.axis_index(Z)
    at_block = lax.axis_index(YX)
    zero = jnp.zeros((1, decay_ref.shape[1]), F32)
    entering, after, last, states, afters = ends(planes, at_plane, zero, zero, zero)
    peaks = [zero]
    bound = []
    for i in range(planes.shape[0]):
        bound.append(6.0 * (planes[i, 6:7] + jnp.abs(states[i])) + 2.0 * jnp.abs(afters[i]))
        peaks.append(planes[i, 7:8])
    bound = jnp.concatenate(bound, 0)
    reach[0] = jnp.broadcast_to(jnp.max(bound, axis=1, keepdims=True), bound.shape)
    reach[1] = jnp.maximum(jnp.concatenate(peaks[:-1], 0), jnp.concatenate(peaks[1:], 0))
    entering, after, last, _, _ = ends(plane, at_block, entering, after, last)
    smoothed = keep[3] + keep[4] * entering + keep[2] * after
    decay = decay_ref[...]
    kappa = 1.0 - leak[...]
    prior = (1.0 - kappa * last * last) * entering + kappa * last * smoothed[:1]
    first = jnp.logical_and(at_plane == 0, at_block == 0)
    prior = jnp.where(first, 0.0, prior)
    row = lax.broadcasted_iota(jnp.int32, smoothed.shape, 0)
    shifted = jnp.where(row == 0, prior, pltpu.roll(smoothed, 1, 0))
    resid = (smoothed - decay * shifted - keep[5]).astype(BF16)
    smoothed_out[...] = smoothed
    for i in range(resid_out.shape[0]):
        resid_out[i] = resid


def bounds(first, second, span):
    return jnp.maximum(span * first[0] * jnp.maximum(first[1], second[1]), 1e-30)


def gradient_body(delays, tails, own, other, resid, reach, reach_other, out, padded):
    blocks, frames, modes = resid.shape
    row = lax.broadcasted_iota(jnp.int32, (frames, 2 * frames), 0)
    column = lax.broadcasted_iota(jnp.int32, (frames, 2 * frames), 1)
    picks = jnp.concatenate(
        [(column == row + delays[k : k + 1, : 2 * frames]).astype(F32).astype(BF16) for k in range(TAPS)], 0
    )
    nothing = jnp.zeros((frames, modes), BF16)
    for b in range(blocks + 1):
        pair = jnp.concatenate(
            [resid[b - 1] if b > 0 else nothing, resid[b] if b < blocks else nothing], 0
        )
        moved = jnp.dot(picks, pair, preferred_element_type=F32).astype(BF16)
        for k in range(TAPS):
            padded[b * frames : (b + 1) * frames, k * modes : (k + 1) * modes] = moved[
                k * frames : (k + 1) * frames
            ]
    rhs = padded[...]
    bound = bounds(reach, reach_other, float(blocks * frames))
    plane = lax.broadcasted_iota(jnp.int32, bound.shape, 0)
    factor = jnp.sum(jnp.where(plane == lax.axis_index(Z), TOP / bound, 0.0), axis=0, keepdims=True)
    factor = jnp.concatenate([factor] * TAPS, 1)
    for which, (before, rows) in enumerate(((tails[0], own), (tails[1], other))):
        lhs = jnp.concatenate(
            [before] + [rows[i, : before.shape[0]] for i in range(blocks)], 1
        )
        sums = jnp.dot(lhs, rhs, preferred_element_type=F32) * factor
        half = jnp.where(lax.axis_index("state") == which, 0, 1)
        for i in range(out.shape[0]):
            out[i, half] = sums[i * 8 : (i + 1) * 8]


def total_body(pieces, reach, reach_other, out, *, span):
    modes = out.shape[1] // TAPS // 2
    pair = (bounds(reach, reach_other, span) / TOP, bounds(reach_other, reach, span) / TOP)
    for core in range(2):
        factor = jnp.where(lax.axis_index("state") == core, pair[0], pair[1])
        factor = jnp.concatenate([factor] * TAPS, 1)
        total = pieces[core] * factor[:1]
        for i in range(1, factor.shape[0]):
            total += pieces[2 * i + core] * factor[i : i + 1]
        for k in range(TAPS):
            column = (2 * k + core) * modes
            out[:, column : column + modes] = total[:, k * modes : (k + 1) * modes]


def behind(x, first):
    return lax.optimization_barrier((x, first))[0]


def swapped(x):
    return lax.ppermute(x, "state", [(0, 1), (1, 0)])


def per_device(record, gain, rate, leak, dilation):
    frames, sensors = record.shape
    modes = rate.shape[0]
    planes = lax.axis_size(Z)
    blocks = lax.axis_size(YX)
    delays = jnp.broadcast_to(dilation[:, None], (TAPS, 2 * frames))
    other = swapped(record)
    group = sensors // planes // blocks
    both = jax.ShapeDtypeStruct((frames, TAPS * modes), F32)
    half_gain = (TAPS, modes, sensors)
    part, gain_rest, peak = call(
        own_body,
        (
            both,
            jax.ShapeDtypeStruct(half_gain, BF16),
            jax.ShapeDtypeStruct((8, modes), F32),
        ),
        scratch=[
            pltpu.VMEM((frames, sensors), BF16),
            pltpu.VMEM(half_gain, BF16),
            pltpu.SemaphoreType.DMA(((1 + 2 * TAPS) * PIECES,)),
        ],
        whole=(0, 1),
        n_in=2,
    )(*(pltpu.with_memory_space_constraint(x, pltpu.HBM) for x in (record, gain)))
    onward = call(onward_body, jax.ShapeDtypeStruct((DMAX, modes), F32), n_in=4)(
        delays, other, gain_rest, part
    )
    here = call(here_body, jax.ShapeDtypeStruct((frames, modes), F32), n_in=5)(
        delays, other, gain_rest, part, onward
    )
    tail = lax.ppermute(onward, TM, [(i, i + 1) for i in range(planes * blocks - 1)])
    rate_t = behind(rate, here).T
    decay = jnp.exp(-rate_t)
    scale = jnp.sqrt(-jnp.expm1(-2.0 * rate_t))
    leak_row = leak[None]
    by_sensor = behind(record, here).T.reshape(planes, blocks, group, frames).swapaxes(0, 1)
    by_sensor = by_sensor.reshape(blocks, planes * group, frames)
    keep, sent = call(
        local_body,
        (
            jax.ShapeDtypeStruct((6, frames, modes), F32),
            jax.ShapeDtypeStruct((blocks, planes * group + 24, frames), BF16),
        ),
        n_in=7,
    )(here, tail, decay, scale, leak_row, by_sensor, peak)
    mine = lax.all_to_all(sent, YX, 0, 0, tiled=True)
    plane, plane_summary = call(
        plane_body,
        (
            jax.ShapeDtypeStruct((blocks, 8, modes), F32),
            jax.ShapeDtypeStruct((planes, 8, modes), F32),
        ),
        n_in=1,
    )(mine)
    theirs = swapped(mine[:, :-24])
    every_plane = lax.all_to_all(plane_summary, Z, 0, 0, tiled=True)
    smoothed, resid, reach = call(
        finish_body,
        (
            jax.ShapeDtypeStruct((frames, modes), F32),
            jax.ShapeDtypeStruct((blocks, frames, modes), BF16),
            jax.ShapeDtypeStruct((2, planes, modes), F32),
        ),
        n_in=5,
    )(plane, every_plane, keep, decay, leak_row)
    resid_all = lax.all_to_all(resid, YX, 0, 0, tiled=True)
    tails = behind(jnp.stack([mine[-1, :-24], theirs[-1]]), resid)
    tails = lax.ppermute(tails, Z, [(i, i + 1) for i in range(planes - 1)])
    reach_other = swapped(reach)
    partial = call(
        gradient_body,
        jax.ShapeDtypeStruct((planes, 2, group, TAPS * modes), F32),
        scratch=[pltpu.VMEM(((blocks + 1) * frames, TAPS * modes), BF16)],
        n_in=7,
    )(delays, tails, mine, theirs, resid_all, reach, reach_other)
    pieces = partial.reshape(planes * 2, group, TAPS * modes).astype(jnp.float16)
    pieces = lax.all_to_all(pieces, (Z, "state"), 0, 0, tiled=True)
    grad = call(
        functools.partial(total_body, span=float(blocks * frames)),
        jax.ShapeDtypeStruct((group, TAPS * 2 * modes), F32),
        n_in=3,
    )(pieces.astype(F32), reach, reach_other)
    return (behind(smoothed, partial).T, grad)


def solution(mesh):
    split = Mesh(
        mesh.devices.reshape(16, 4, 4, mesh.shape["state"]), ("tm_0", "tm_1", "tm_2", "state")
    )
    return jax.shard_map(
        per_device,
        mesh=split,
        in_specs=(P(TM, "state"), P(None, "state", None), P("state", TM), P("state"), P()),
        out_specs=(P("state", TM), P(STATE_TM, None)),
        check_vma=False,
    )
```

```python
import functools

import jax
import jax.numpy as jnp
from jax import lax
from jax.experimental import pallas as pl
from jax.experimental.pallas import tpu as pltpu
from jax.sharding import Mesh
from jax.sharding import PartitionSpec as P

TAPS = 2
TOP = 32768.0
PIECES = 1
DMAX = 64
Z = "tm_0"
YX = ("tm_1", "tm_2")
TM = ("tm_0", "tm_1", "tm_2")
STATE_TM = ("state", "tm_0", "tm_1", "tm_2")
F32 = jnp.float32
BF16 = jnp.bfloat16
VMEM = pl.BlockSpec(memory_space=pltpu.VMEM)
WHOLE = pl.BlockSpec(memory_space=pltpu.HBM)
NT = (((1,), (1,)), ((), ()))


def call(body, outs, scratch=(), whole=(), n_in=1):
    specs = [WHOLE if i in whole else VMEM for i in range(n_in)]
    return pl.pallas_call(
        body,
        out_shape=outs,
        in_specs=specs,
        out_specs=jax.tree.map(lambda _: VMEM, outs),
        scratch_shapes=scratch,
        compiler_params=pltpu.CompilerParams(vmem_limit_bytes=48 << 20),
    )


def later(x, k, fill):
    if k % 8 == 0:
        return jnp.concatenate([jnp.full((k, x.shape[1]), fill, x.dtype), x[:-k]], 0)
    row = lax.broadcasted_iota(jnp.int32, x.shape, 0)
    return jnp.where(row < k, fill, pltpu.roll(x, k, 0))


def earlier(x, k, fill):
    n = x.shape[0]
    if k % 8 == 0:
        return jnp.concatenate([x[k:], jnp.full((k, x.shape[1]), fill, x.dtype)], 0)
    row = lax.broadcasted_iota(jnp.int32, x.shape, 0)
    return jnp.where(row >= n - k, fill, pltpu.roll(x, n - k, 0))


def recur(link, sums, shift):
    k = 1
    while k < link.shape[0]:
        sums = [s + link * shift(s, k, 0.0) for s in sums]
        link = link * shift(link, k, 1.0)
        k *= 2
    return link, sums


def product(rows, gain):
    both = gain[...].reshape(TAPS * gain.shape[1], gain.shape[2])
    return lax.dot_general(rows, both, NT, preferred_element_type=F32)


def own_body(record, gain, out, gain_rest, peak, own, gain_own, arrived):
    modes = gain_own.shape[1]
    frames, half = own.shape
    core = lax.axis_index("state")
    mine = pl.multiple_of(core * half, half)
    theirs = pl.multiple_of((1 - core) * half, half)
    record_copies = []
    gain_copies = []
    rest_copies = []
    for piece in range(PIECES):
        rows = pl.ds(piece * (frames // PIECES), frames // PIECES)
        record_copies.append((record.at[rows], own.at[rows]))
    for k in range(TAPS):
        for piece in range(PIECES):
            rows = pl.ds(piece * (modes // PIECES), modes // PIECES)
            gain_copies.append((gain.at[k, rows, pl.ds(mine, half)], gain_own.at[k, rows]))
            rest_copies.append((gain.at[k, rows, pl.ds(theirs, half)], gain_rest.at[k, rows]))
    copies = [
        pltpu.make_async_copy(source, target, arrived.at[n])
        for n, (source, target) in enumerate(record_copies + gain_copies + rest_copies)
    ]
    for copy in copies:
        copy.start()
    for copy in copies[:PIECES]:
        copy.wait()
    largest = jnp.max(jnp.abs(own[...].astype(F32)), axis=0, keepdims=True)
    peak[...] = jnp.broadcast_to(jnp.max(largest, axis=1, keepdims=True), peak.shape)
    for copy in copies[PIECES : (1 + TAPS) * PIECES]:
        copy.wait()
    out[...] = product(own[...], gain_own)
    for copy in copies[(1 + TAPS) * PIECES :]:
        copy.wait()


def moved(delay, rows, ahead, values):
    shape = (rows, values.shape[0])
    row = lax.broadcasted_iota(jnp.int32, shape, 0)
    column = lax.broadcasted_iota(jnp.int32, shape, 1)
    pick = (column + delay[:, : shape[1]] == row + ahead).astype(F32)
    return jnp.dot(
        pick, values, precision=lax.Precision.HIGHEST, preferred_element_type=F32
    )


def onward_body(delays, other, gain, part, out):
    modes = gain.shape[1]
    at = part.shape[0] - DMAX
    u = part[at:] + product(other[at:], gain)
    total = jnp.zeros(out.shape, F32)
    for k in range(TAPS):
        total += moved(delays[k : k + 1], DMAX, DMAX, u[:, k * modes : (k + 1) * modes])
    out[...] = total


def here_body(delays, other, gain, part, onward, out):
    modes = gain.shape[1]
    u = part[...] + product(other[...], gain)
    total = jnp.zeros(out.shape, F32)
    for k in range(TAPS):
        total += moved(delays[k : k + 1], u.shape[0], 0, u[:, k * modes : (k + 1) * modes])
    out[...] = total


def local_body(here, tail, decay_ref, scale, leak, by_sensor, peak, keep, sent):
    frames, modes = decay_ref.shape
    nothing = jnp.zeros((frames - DMAX, modes), F32)
    drive_in = here[...] + jnp.concatenate([tail[...], nothing], 0)
    drive = scale[...] * drive_in
    decay = decay_ref[...]
    prods, (offsets,) = recur(decay, [drive], later)
    kappa = 1.0 - leak[...]
    weight = 1.0 - kappa * decay * decay
    links, (base, slope) = recur(kappa * decay, [weight * offsets, weight * prods], earlier)
    keep[0] = prods
    keep[1] = offsets
    keep[2] = links
    keep[3] = base
    keep[4] = slope
    keep[5] = drive
    rows = [prods[-1:], offsets[-1:], links[:1], base[:1], slope[:1], decay[-1:]]
    rows += [jnp.max(jnp.abs(offsets), axis=0, keepdims=True), peak[:1]]
    rest = jnp.concatenate(rows, 0)
    frames_rows = by_sensor.shape[1]
    parts = []
    for _ in range(3):
        part = rest.astype(BF16)
        parts.append(part.astype(F32))
        rest = rest - parts[-1]
    coded = jnp.concatenate(parts, 0).astype(BF16)
    for i in range(sent.shape[0]):
        sent[i, :frames_rows] = by_sensor[i]
        sent[i, frames_rows:] = coded


def decoded(every, out):
    at = every.shape[1] - 24
    for i in range(every.shape[0]):
        rows = every[i, at:].astype(F32)
        out[i] = rows[:8] + rows[8:16] + rows[16:]


def joined(first, second):
    p1, o1, l1, b1, s1 = first
    p2, o2, l2, b2, s2 = second
    return (p1 * p2, p2 * o1 + o2, l1 * l2, b1 + l1 * (b2 + s2 * o1), s1 + l1 * s2 * p1)


def five(ref, i):
    return tuple(ref[i, r : r + 1] for r in range(5))


def plane_body(sent, every, out):
    n = sent.shape[0]
    decoded(sent, every)
    parts = [five(every, i) for i in range(n)]
    while len(parts) > 1:
        parts = [joined(parts[i], parts[i + 1]) for i in range(0, len(parts), 2)]
    state = jnp.zeros_like(every[0, :1])
    reach = state
    peak = state
    for i in range(n):
        reach = jnp.maximum(reach, every[i, 6:7] + jnp.abs(state))
        peak = jnp.maximum(peak, every[i, 7:8])
        state = every[i, 0:1] * state + every[i, 1:2]
    rows = list(parts[0]) + [every[n - 1, 5:6], reach, peak]
    for r, row in enumerate(rows):
        for i in range(out.shape[0]):
            out[i, r : r + 1] = row


def ends(every, position, entering, closing, last):
    n = every.shape[0]
    states = []
    state = entering
    before = last
    own_state = jnp.zeros_like(entering)
    own_last = jnp.zeros_like(entering)
    for i in range(n):
        states.append(state)
        own_state = jnp.where(position == i, state, own_state)
        own_last = jnp.where(position == i, before, own_last)
        state = every[i, 0:1] * state + every[i, 1:2]
        before = every[i, 5:6]
    after = closing
    afters = [after] * n
    own_after = jnp.zeros_like(entering)
    for i in reversed(range(n)):
        afters[i] = after
        own_after = jnp.where(position == i, after, own_after)
        after = every[i, 2:3] * after + every[i, 3:4] + every[i, 4:5] * states[i]
    return own_state, own_after, own_last, states, afters


def finish_body(plane, planes, keep, decay_ref, leak, smoothed_out, resid_out, reach):
    at_plane = lax.axis_index(Z)
    at_block = lax.axis_index(YX)
    zero = jnp.zeros((1, decay_ref.shape[1]), F32)
    entering, after, last, states, afters = ends(planes, at_plane, zero, zero, zero)
    peaks = [zero]
    bound = []
    for i in range(planes.shape[0]):
        bound.append(6.0 * (planes[i, 6:7] + jnp.abs(states[i])) + 2.0 * jnp.abs(afters[i]))
        peaks.append(planes[i, 7:8])
    bound = jnp.concatenate(bound, 0)
    reach[0] = jnp.broadcast_to(jnp.max(bound, axis=1, keepdims=True), bound.shape)
    reach[1] = jnp.maximum(jnp.concatenate(peaks[:-1], 0), jnp.concatenate(peaks[1:], 0))
    entering, after, last, _, _ = ends(plane, at_block, entering, after, last)
    smoothed = keep[3] + keep[4] * entering + keep[2] * after
    decay = decay_ref[...]
    kappa = 1.0 - leak[...]
    prior = (1.0 - kappa * last * last) * entering + kappa * last * smoothed[:1]
    first = jnp.logical_and(at_plane == 0, at_block == 0)
    prior = jnp.where(first, 0.0, prior)
    row = lax.broadcasted_iota(jnp.int32, smoothed.shape, 0)
    shifted = jnp.where(row == 0, prior, pltpu.roll(smoothed, 1, 0))
    resid = (smoothed - decay * shifted - keep[5]).astype(BF16)
    smoothed_out[...] = smoothed.T
    for i in range(resid_out.shape[0]):
        resid_out[i] = resid


def bounds(first, second, span):
    return jnp.maximum(span * first[0] * jnp.maximum(first[1], second[1]), 1e-30)


def gradient_body(delays, tails, own, other, resid, reach, reach_other, out, padded):
    blocks, frames, modes = resid.shape
    row = lax.broadcasted_iota(jnp.int32, (frames, 2 * frames), 0)
    column = lax.broadcasted_iota(jnp.int32, (frames, 2 * frames), 1)
    picks = jnp.concatenate(
        [(column == row + delays[k : k + 1, : 2 * frames]).astype(F32).astype(BF16) for k in range(TAPS)], 0
    )
    nothing = jnp.zeros((frames, modes), BF16)
    for b in range(blocks + 1):
        pair = jnp.concatenate(
            [resid[b - 1] if b > 0 else nothing, resid[b] if b < blocks else nothing], 0
        )
        moved = jnp.dot(picks, pair, preferred_element_type=F32).astype(BF16)
        for k in range(TAPS):
            padded[b * frames : (b + 1) * frames, k * modes : (k + 1) * modes] = moved[
                k * frames : (k + 1) * frames
            ]
    rhs = padded[...]
    bound = bounds(reach, reach_other, float(blocks * frames))
    plane = lax.broadcasted_iota(jnp.int32, bound.shape, 0)
    factor = jnp.sum(jnp.where(plane == lax.axis_index(Z), TOP / bound, 0.0), axis=0, keepdims=True)
    factor = jnp.concatenate([factor] * TAPS, 1)
    lhs = [
        jnp.concatenate([tails[which]] + [rows[i, : tails.shape[1]] for i in range(blocks)], 1)
        for which, rows in enumerate((own, other))
    ]
    sums = jnp.dot(jnp.concatenate(lhs, 0), rhs, preferred_element_type=F32) * factor
    for which in range(2):
        half = jnp.where(lax.axis_index("state") == which, 0, 1)
        for i in range(out.shape[0]):
            row = which * tails.shape[1] + i * 8
            out[i, half] = sums[row : row + 8]


def total_body(pieces, reach, reach_other, out, *, span):
    modes = out.shape[1] // TAPS // 2
    pair = (bounds(reach, reach_other, span) / TOP, bounds(reach_other, reach, span) / TOP)
    for core in range(2):
        factor = jnp.where(lax.axis_index("state") == core, pair[0], pair[1])
        factor = jnp.concatenate([factor] * TAPS, 1)
        total = pieces[core] * factor[:1]
        for i in range(1, factor.shape[0]):
            total += pieces[2 * i + core] * factor[i : i + 1]
        for k in range(TAPS):
            column = (2 * k + core) * modes
            out[:, column : column + modes] = total[:, k * modes : (k + 1) * modes]


def behind(x, first):
    return lax.optimization_barrier((x, first))[0]


def swapped(x):
    return lax.ppermute(x, "state", [(0, 1), (1, 0)])


def per_device(record, gain, rate, leak, dilation):
    frames, sensors = record.shape
    modes = rate.shape[0]
    planes = lax.axis_size(Z)
    blocks = lax.axis_size(YX)
    delays = jnp.broadcast_to(dilation[:, None], (TAPS, 2 * frames))
    other = swapped(record)
    group = sensors // planes // blocks
    both = jax.ShapeDtypeStruct((frames, TAPS * modes), F32)
    half_gain = (TAPS, modes, sensors)
    part, gain_rest, peak = call(
        own_body,
        (
            both,
            jax.ShapeDtypeStruct(half_gain, BF16),
            jax.ShapeDtypeStruct((8, modes), F32),
        ),
        scratch=[
            pltpu.VMEM((frames, sensors), BF16),
            pltpu.VMEM(half_gain, BF16),
            pltpu.SemaphoreType.DMA(((1 + 2 * TAPS) * PIECES,)),
        ],
        whole=(0, 1),
        n_in=2,
    )(*(pltpu.with_memory_space_constraint(x, pltpu.HBM) for x in (record, gain)))
    onward = call(onward_body, jax.ShapeDtypeStruct((DMAX, modes), F32), n_in=4)(
        delays, other, gain_rest, part
    )
    here = call(here_body, jax.ShapeDtypeStruct((frames, modes), F32), n_in=5)(
        delays, other, gain_rest, part, onward
    )
    tail = lax.ppermute(onward, TM, [(i, i + 1) for i in range(planes * blocks - 1)])
    rate_t = behind(rate, here).T
    decay = jnp.exp(-rate_t)
    scale = jnp.sqrt(-jnp.expm1(-2.0 * rate_t))
    leak_row = leak[None]
    by_sensor = behind(record, here).T.reshape(planes, blocks, group, frames).swapaxes(0, 1)
    by_sensor = by_sensor.reshape(blocks, planes * group, frames)
    keep, sent = call(
        local_body,
        (
            jax.ShapeDtypeStruct((6, frames, modes), F32),
            jax.ShapeDtypeStruct((blocks, planes * group + 24, frames), BF16),
        ),
        n_in=7,
    )(here, tail, decay, scale, leak_row, by_sensor, peak)
    mine = lax.all_to_all(sent, YX, 0, 0, tiled=True)
    plane, plane_summary = call(
        plane_body,
        (
            jax.ShapeDtypeStruct((blocks, 8, modes), F32),
            jax.ShapeDtypeStruct((planes, 8, modes), F32),
        ),
        n_in=1,
    )(mine)
    theirs = swapped(mine[:, :-24])
    every_plane = lax.all_to_all(plane_summary, Z, 0, 0, tiled=True)
    smoothed, resid, reach = call(
        finish_body,
        (
            jax.ShapeDtypeStruct((modes, frames), F32),
            jax.ShapeDtypeStruct((blocks, frames, modes), BF16),
            jax.ShapeDtypeStruct((2, planes, modes), F32),
        ),
        n_in=5,
    )(plane, every_plane, keep, decay, leak_row)
    resid_all = lax.all_to_all(resid, YX, 0, 0, tiled=True)
    tails = behind(jnp.stack([mine[-1, :-24], theirs[-1]]), resid)
    tails = lax.ppermute(tails, Z, [(i, i + 1) for i in range(planes - 1)])
    reach_other = swapped(reach)
    partial = call(
        gradient_body,
        jax.ShapeDtypeStruct((planes, 2, group, TAPS * modes), F32),
        scratch=[pltpu.VMEM(((blocks + 1) * frames, TAPS * modes), BF16)],
        n_in=7,
    )(delays, tails, mine, theirs, resid_all, reach, reach_other)
    pieces = partial.reshape(planes * 2, group, TAPS * modes).astype(jnp.float16)
    pieces = lax.all_to_all(pieces, (Z, "state"), 0, 0, tiled=True)
    grad = call(
        functools.partial(total_body, span=float(blocks * frames)),
        jax.ShapeDtypeStruct((group, TAPS * 2 * modes), F32),
        n_in=3,
    )(pieces.astype(F32), reach, reach_other)
    return (smoothed, grad)


def solution(mesh):
    split = Mesh(
        mesh.devices.reshape(16, 4, 4, mesh.shape["state"]), ("tm_0", "tm_1", "tm_2", "state")
    )
    return jax.shard_map(
        per_device,
        mesh=split,
        in_specs=(P(TM, "state"), P(None, "state", None), P("state", TM), P("state"), P()),
        out_specs=(P("state", TM), P(STATE_TM, None)),
        check_vma=False,
    )
```

```python
import functools

import jax
import jax.numpy as jnp
from jax import lax
from jax.experimental import pallas as pl
from jax.experimental.pallas import tpu as pltpu
from jax.sharding import Mesh
from jax.sharding import PartitionSpec as P

TAPS = 2
TOP = 32768.0
PIECES = 1
DMAX = 64
Z = "tm_0"
YX = ("tm_1", "tm_2")
TM = ("tm_0", "tm_1", "tm_2")
STATE_TM = ("state", "tm_0", "tm_1", "tm_2")
F32 = jnp.float32
BF16 = jnp.bfloat16
VMEM = pl.BlockSpec(memory_space=pltpu.VMEM)
WHOLE = pl.BlockSpec(memory_space=pltpu.HBM)
NT = (((1,), (1,)), ((), ()))


def call(body, outs, scratch=(), whole=(), n_in=1):
    specs = [WHOLE if i in whole else VMEM for i in range(n_in)]
    return pl.pallas_call(
        body,
        out_shape=outs,
        in_specs=specs,
        out_specs=jax.tree.map(lambda _: VMEM, outs),
        scratch_shapes=scratch,
        compiler_params=pltpu.CompilerParams(vmem_limit_bytes=48 << 20),
    )


def later(x, k, fill):
    if k % 8 == 0:
        return jnp.concatenate([jnp.full((k, x.shape[1]), fill, x.dtype), x[:-k]], 0)
    row = lax.broadcasted_iota(jnp.int32, x.shape, 0)
    return jnp.where(row < k, fill, pltpu.roll(x, k, 0))


def earlier(x, k, fill):
    n = x.shape[0]
    if k % 8 == 0:
        return jnp.concatenate([x[k:], jnp.full((k, x.shape[1]), fill, x.dtype)], 0)
    row = lax.broadcasted_iota(jnp.int32, x.shape, 0)
    return jnp.where(row >= n - k, fill, pltpu.roll(x, n - k, 0))


def recur(link, sums, shift):
    k = 1
    while k < link.shape[0]:
        sums = [s + link * shift(s, k, 0.0) for s in sums]
        link = link * shift(link, k, 1.0)
        k *= 2
    return link, sums


def product(rows, gain):
    both = gain[...].reshape(TAPS * gain.shape[1], gain.shape[2])
    return lax.dot_general(rows, both, NT, preferred_element_type=F32)


def own_body(record, gain, out, gain_rest, peak, own, gain_own, arrived):
    modes = gain_own.shape[1]
    frames, half = own.shape
    core = lax.axis_index("state")
    mine = pl.multiple_of(core * half, half)
    theirs = pl.multiple_of((1 - core) * half, half)
    record_copies = []
    gain_copies = []
    rest_copies = []
    for piece in range(PIECES):
        rows = pl.ds(piece * (frames // PIECES), frames // PIECES)
        record_copies.append((record.at[rows], own.at[rows]))
    for k in range(TAPS):
        for piece in range(PIECES):
            rows = pl.ds(piece * (modes // PIECES), modes // PIECES)
            gain_copies.append((gain.at[k, rows, pl.ds(mine, half)], gain_own.at[k, rows]))
            rest_copies.append((gain.at[k, rows, pl.ds(theirs, half)], gain_rest.at[k, rows]))
    copies = [
        pltpu.make_async_copy(source, target, arrived.at[n])
        for n, (source, target) in enumerate(record_copies + gain_copies + rest_copies)
    ]
    for copy in copies:
        copy.start()
    for copy in copies[:PIECES]:
        copy.wait()
    largest = jnp.max(jnp.abs(own[...].astype(F32)), axis=0, keepdims=True)
    peak[...] = jnp.broadcast_to(jnp.max(largest, axis=1, keepdims=True), peak.shape)
    for copy in copies[PIECES : (1 + TAPS) * PIECES]:
        copy.wait()
    out[...] = product(own[...], gain_own)
    for copy in copies[(1 + TAPS) * PIECES :]:
        copy.wait()


def moved(delay, rows, ahead, values):
    shape = (rows, values.shape[0])
    row = lax.broadcasted_iota(jnp.int32, shape, 0)
    column = lax.broadcasted_iota(jnp.int32, shape, 1)
    pick = (column + delay[:, : shape[1]] == row + ahead).astype(F32)
    return jnp.dot(
        pick, values, precision=lax.Precision.HIGHEST, preferred_element_type=F32
    )


def onward_body(delays, other, gain, part, out):
    modes = gain.shape[1]
    at = part.shape[0] - DMAX
    u = part[at:] + product(other[at:], gain)
    total = jnp.zeros(out.shape, F32)
    for k in range(TAPS):
        total += moved(delays[k : k + 1], DMAX, DMAX, u[:, k * modes : (k + 1) * modes])
    out[...] = total


def here_body(delays, other, gain, part, onward, out):
    modes = gain.shape[1]
    u = part[...] + product(other[...], gain)
    total = jnp.zeros(out.shape, F32)
    for k in range(TAPS):
        total += moved(delays[k : k + 1], u.shape[0], 0, u[:, k * modes : (k + 1) * modes])
    out[...] = total


def local_body(here, tail, decay_ref, scale, leak, by_sensor, peak, keep, sent):
    frames, modes = decay_ref.shape
    nothing = jnp.zeros((frames - DMAX, modes), F32)
    drive_in = here[...] + jnp.concatenate([tail[...], nothing], 0)
    drive = scale[...] * drive_in
    decay = decay_ref[...]
    prods, (offsets,) = recur(decay, [drive], later)
    kappa = 1.0 - leak[...]
    weight = 1.0 - kappa * decay * decay
    links, (base, slope) = recur(kappa * decay, [weight * offsets, weight * prods], earlier)
    keep[0] = prods
    keep[1] = offsets
    keep[2] = links
    keep[3] = base
    keep[4] = slope
    keep[5] = drive
    rows = [prods[-1:], offsets[-1:], links[:1], base[:1], slope[:1], decay[-1:]]
    rows += [jnp.max(jnp.abs(offsets), axis=0, keepdims=True), peak[:1]]
    rest = jnp.concatenate(rows, 0)
    frames_rows = by_sensor.shape[1]
    parts = []
    for _ in range(3):
        part = rest.astype(BF16)
        parts.append(part.astype(F32))
        rest = rest - parts[-1]
    coded = jnp.concatenate(parts, 0).astype(BF16)
    for i in range(sent.shape[0]):
        sent[i, :frames_rows] = by_sensor[i]
        sent[i, frames_rows:] = coded


def decoded(every, out):
    at = every.shape[1] - 24
    for i in range(every.shape[0]):
        rows = every[i, at:].astype(F32)
        out[i] = rows[:8] + rows[8:16] + rows[16:]


def joined(first, second):
    p1, o1, l1, b1, s1 = first
    p2, o2, l2, b2, s2 = second
    return (p1 * p2, p2 * o1 + o2, l1 * l2, b1 + l1 * (b2 + s2 * o1), s1 + l1 * s2 * p1)


def five(ref, i):
    return tuple(ref[i, r : r + 1] for r in range(5))


def plane_body(sent, every, out):
    n = sent.shape[0]
    decoded(sent, every)
    parts = [five(every, i) for i in range(n)]
    while len(parts) > 1:
        parts = [joined(parts[i], parts[i + 1]) for i in range(0, len(parts), 2)]
    state = jnp.zeros_like(every[0, :1])
    reach = state
    peak = state
    for i in range(n):
        reach = jnp.maximum(reach, every[i, 6:7] + jnp.abs(state))
        peak = jnp.maximum(peak, every[i, 7:8])
        state = every[i, 0:1] * state + every[i, 1:2]
    rows = list(parts[0]) + [every[n - 1, 5:6], reach, peak]
    for r, row in enumerate(rows):
        for i in range(out.shape[0]):
            out[i, r : r + 1] = row


def ends(every, position, entering, closing, last):
    n = every.shape[0]
    states = []
    state = entering
    before = last
    own_state = jnp.zeros_like(entering)
    own_last = jnp.zeros_like(entering)
    for i in range(n):
        states.append(state)
        own_state = jnp.where(position == i, state, own_state)
        own_last = jnp.where(position == i, before, own_last)
        state = every[i, 0:1] * state + every[i, 1:2]
        before = every[i, 5:6]
    after = closing
    afters = [after] * n
    own_after = jnp.zeros_like(entering)
    for i in reversed(range(n)):
        afters[i] = after
        own_after = jnp.where(position == i, after, own_after)
        after = every[i, 2:3] * after + every[i, 3:4] + every[i, 4:5] * states[i]
    return own_state, own_after, own_last, states, afters


def finish_body(plane, planes, keep, decay_ref, leak, smoothed_out, resid_out, reach):
    at_plane = lax.axis_index(Z)
    at_block = lax.axis_index(YX)
    zero = jnp.zeros((1, decay_ref.shape[1]), F32)
    entering, after, last, states, afters = ends(planes, at_plane, zero, zero, zero)
    peaks = [zero]
    bound = []
    for i in range(planes.shape[0]):
        bound.append(6.0 * (planes[i, 6:7] + jnp.abs(states[i])) + 2.0 * jnp.abs(afters[i]))
        peaks.append(planes[i, 7:8])
    bound = jnp.concatenate(bound, 0)
    reach[0] = jnp.broadcast_to(jnp.max(bound, axis=1, keepdims=True), bound.shape)
    reach[1] = jnp.maximum(jnp.concatenate(peaks[:-1], 0), jnp.concatenate(peaks[1:], 0))
    entering, after, last, _, _ = ends(plane, at_block, entering, after, last)
    smoothed = keep[3] + keep[4] * entering + keep[2] * after
    decay = decay_ref[...]
    kappa = 1.0 - leak[...]
    prior = (1.0 - kappa * last * last) * entering + kappa * last * smoothed[:1]
    first = jnp.logical_and(at_plane == 0, at_block == 0)
    prior = jnp.where(first, 0.0, prior)
    row = lax.broadcasted_iota(jnp.int32, smoothed.shape, 0)
    shifted = jnp.where(row == 0, prior, pltpu.roll(smoothed, 1, 0))
    resid = (smoothed - decay * shifted - keep[5]).astype(BF16)
    smoothed_out[...] = smoothed.T
    for i in range(resid_out.shape[0]):
        resid_out[i] = resid


def bounds(first, second, span):
    return jnp.maximum(span * first[0] * jnp.maximum(first[1], second[1]), 1e-30)


def gradient_body(delays, tails, own, other, resid, reach, reach_other, out, padded):
    blocks, frames, modes = resid.shape
    row = lax.broadcasted_iota(jnp.int32, (frames, 2 * frames), 0)
    column = lax.broadcasted_iota(jnp.int32, (frames, 2 * frames), 1)
    picks = jnp.concatenate(
        [(column == row + delays[k : k + 1, : 2 * frames]).astype(F32).astype(BF16) for k in range(TAPS)], 0
    )
    nothing = jnp.zeros((frames, modes), BF16)
    for b in range(blocks + 1):
        pair = jnp.concatenate(
            [resid[b - 1] if b > 0 else nothing, resid[b] if b < blocks else nothing], 0
        )
        moved = jnp.dot(picks, pair, preferred_element_type=F32).astype(BF16)
        for k in range(TAPS):
            padded[b * frames : (b + 1) * frames, k * modes : (k + 1) * modes] = moved[
                k * frames : (k + 1) * frames
            ]
    rhs = padded[...]
    bound = bounds(reach, reach_other, float(blocks * frames))
    plane = lax.broadcasted_iota(jnp.int32, bound.shape, 0)
    factor = jnp.sum(jnp.where(plane == lax.axis_index(Z), TOP / bound, 0.0), axis=0, keepdims=True)
    factor = jnp.concatenate([factor] * TAPS, 1)
    for which, (before, rows) in enumerate(((tails[0], own), (tails[1], other))):
        lhs = jnp.concatenate(
            [before] + [rows[i, : before.shape[0]] for i in range(blocks)], 1
        )
        sums = jnp.dot(lhs, rhs, preferred_element_type=F32) * factor
        half = jnp.where(lax.axis_index("state") == which, 0, 1)
        for i in range(out.shape[1]):
            out[half, i] = sums[i * 8 : (i + 1) * 8]


def total_body(pieces, reach, reach_other, out, *, span):
    modes = out.shape[1] // TAPS // 2
    pair = (bounds(reach, reach_other, span) / TOP, bounds(reach_other, reach, span) / TOP)
    for core in range(2):
        factor = jnp.where(lax.axis_index("state") == core, pair[0], pair[1])
        factor = jnp.concatenate([factor] * TAPS, 1)
        planes = factor.shape[0]
        total = pieces[core * planes] * factor[:1]
        for i in range(1, planes):
            total += pieces[core * planes + i] * factor[i : i + 1]
        for k in range(TAPS):
            column = (2 * k + core) * modes
            out[:, column : column + modes] = total[:, k * modes : (k + 1) * modes]


def behind(x, first):
    return lax.optimization_barrier((x, first))[0]


def swapped(x):
    return lax.ppermute(x, "state", [(0, 1), (1, 0)])


def per_device(record, gain, rate, leak, dilation):
    frames, sensors = record.shape
    modes = rate.shape[0]
    planes = lax.axis_size(Z)
    blocks = lax.axis_size(YX)
    delays = jnp.broadcast_to(dilation[:, None], (TAPS, 2 * frames))
    other = swapped(record)
    group = sensors // planes // blocks
    both = jax.ShapeDtypeStruct((frames, TAPS * modes), F32)
    half_gain = (TAPS, modes, sensors)
    part, gain_rest, peak = call(
        own_body,
        (
            both,
            jax.ShapeDtypeStruct(half_gain, BF16),
            jax.ShapeDtypeStruct((8, modes), F32),
        ),
        scratch=[
            pltpu.VMEM((frames, sensors), BF16),
            pltpu.VMEM(half_gain, BF16),
            pltpu.SemaphoreType.DMA(((1 + 2 * TAPS) * PIECES,)),
        ],
        whole=(0, 1),
        n_in=2,
    )(*(pltpu.with_memory_space_constraint(x, pltpu.HBM) for x in (record, gain)))
    onward = call(onward_body, jax.ShapeDtypeStruct((DMAX, modes), F32), n_in=4)(
        delays, other, gain_rest, part
    )
    here = call(here_body, jax.ShapeDtypeStruct((frames, modes), F32), n_in=5)(
        delays, other, gain_rest, part, onward
    )
    tail = lax.ppermute(onward, TM, [(i, i + 1) for i in range(planes * blocks - 1)])
    rate_t = behind(rate, here).T
    decay = jnp.exp(-rate_t)
    scale = jnp.sqrt(-jnp.expm1(-2.0 * rate_t))
    leak_row = leak[None]
    by_sensor = behind(record, here).T.reshape(planes, blocks, group, frames).swapaxes(0, 1)
    by_sensor = by_sensor.reshape(blocks, planes * group, frames)
    keep, sent = call(
        local_body,
        (
            jax.ShapeDtypeStruct((6, frames, modes), F32),
            jax.ShapeDtypeStruct((blocks, planes * group + 24, frames), BF16),
        ),
        n_in=7,
    )(here, tail, decay, scale, leak_row, by_sensor, peak)
    mine = lax.all_to_all(sent, YX, 0, 0, tiled=True)
    plane, plane_summary = call(
        plane_body,
        (
            jax.ShapeDtypeStruct((blocks, 8, modes), F32),
            jax.ShapeDtypeStruct((planes, 8, modes), F32),
        ),
        n_in=1,
    )(mine)
    theirs = swapped(mine[:, :-24])
    every_plane = lax.all_to_all(plane_summary, Z, 0, 0, tiled=True)
    smoothed, resid, reach = call(
        finish_body,
        (
            jax.ShapeDtypeStruct((modes, frames), F32),
            jax.ShapeDtypeStruct((blocks, frames, modes), BF16),
            jax.ShapeDtypeStruct((2, planes, modes), F32),
        ),
        n_in=5,
    )(plane, every_plane, keep, decay, leak_row)
    resid_all = lax.all_to_all(resid, YX, 0, 0, tiled=True)
    tails = behind(jnp.stack([mine[-1, :-24], theirs[-1]]), resid)
    tails = lax.ppermute(tails, Z, [(i, i + 1) for i in range(planes - 1)])
    reach_other = swapped(reach)
    partial = call(
        gradient_body,
        jax.ShapeDtypeStruct((2, planes, group, TAPS * modes), F32),
        scratch=[pltpu.VMEM(((blocks + 1) * frames, TAPS * modes), BF16)],
        n_in=7,
    )(delays, tails, mine, theirs, resid_all, reach, reach_other)
    pieces = partial.reshape(planes * 2, group, TAPS * modes).astype(jnp.float16)
    pieces = lax.all_to_all(pieces, ("state", Z), 0, 0, tiled=True)
    grad = call(
        functools.partial(total_body, span=float(blocks * frames)),
        jax.ShapeDtypeStruct((group, TAPS * 2 * modes), F32),
        n_in=3,
    )(pieces.astype(F32), reach, reach_other)
    return (smoothed, grad)


def solution(mesh):
    split = Mesh(
        mesh.devices.reshape(16, 4, 4, mesh.shape["state"]), ("tm_0", "tm_1", "tm_2", "state")
    )
    return jax.shard_map(
        per_device,
        mesh=split,
        in_specs=(P(TM, "state"), P(None, "state", None), P("state", TM), P("state"), P()),
        out_specs=(P("state", TM), P(STATE_TM, None)),
        check_vma=False,
    )
```

```python
import functools

import jax
import jax.numpy as jnp
from jax import lax
from jax.experimental import pallas as pl
from jax.experimental.pallas import tpu as pltpu
from jax.sharding import Mesh
from jax.sharding import PartitionSpec as P

TAPS = 2
TOP = 32768.0
PIECES = 1
DMAX = 64
Z = "tm_0"
YX = ("tm_1", "tm_2")
TM = ("tm_0", "tm_1", "tm_2")
STATE_TM = ("state", "tm_0", "tm_1", "tm_2")
F32 = jnp.float32
BF16 = jnp.bfloat16
VMEM = pl.BlockSpec(memory_space=pltpu.VMEM)
WHOLE = pl.BlockSpec(memory_space=pltpu.HBM)
NT = (((1,), (1,)), ((), ()))


def call(body, outs, scratch=(), whole=(), n_in=1):
    specs = [WHOLE if i in whole else VMEM for i in range(n_in)]
    return pl.pallas_call(
        body,
        out_shape=outs,
        in_specs=specs,
        out_specs=jax.tree.map(lambda _: VMEM, outs),
        scratch_shapes=scratch,
        compiler_params=pltpu.CompilerParams(vmem_limit_bytes=48 << 20),
    )


def later(x, k, fill):
    if k % 8 == 0:
        return jnp.concatenate([jnp.full((k, x.shape[1]), fill, x.dtype), x[:-k]], 0)
    row = lax.broadcasted_iota(jnp.int32, x.shape, 0)
    return jnp.where(row < k, fill, pltpu.roll(x, k, 0))


def earlier(x, k, fill):
    n = x.shape[0]
    if k % 8 == 0:
        return jnp.concatenate([x[k:], jnp.full((k, x.shape[1]), fill, x.dtype)], 0)
    row = lax.broadcasted_iota(jnp.int32, x.shape, 0)
    return jnp.where(row >= n - k, fill, pltpu.roll(x, n - k, 0))


def recur(link, sums, shift):
    k = 1
    while k < link.shape[0]:
        sums = [s + link * shift(s, k, 0.0) for s in sums]
        link = link * shift(link, k, 1.0)
        k *= 2
    return link, sums


def product(rows, gain):
    both = gain[...].reshape(TAPS * gain.shape[1], gain.shape[2])
    return lax.dot_general(rows, both, NT, preferred_element_type=F32)


def own_body(record, gain, out, gain_rest, peak, own, gain_own, arrived):
    modes = gain_own.shape[1]
    frames, half = own.shape
    core = lax.axis_index("state")
    mine = pl.multiple_of(core * half, half)
    theirs = pl.multiple_of((1 - core) * half, half)
    record_copies = []
    gain_copies = []
    rest_copies = []
    for piece in range(PIECES):
        rows = pl.ds(piece * (frames // PIECES), frames // PIECES)
        record_copies.append((record.at[rows], own.at[rows]))
    for k in range(TAPS):
        for piece in range(PIECES):
            rows = pl.ds(piece * (modes // PIECES), modes // PIECES)
            gain_copies.append((gain.at[k, rows, pl.ds(mine, half)], gain_own.at[k, rows]))
            rest_copies.append((gain.at[k, rows, pl.ds(theirs, half)], gain_rest.at[k, rows]))
    copies = [
        pltpu.make_async_copy(source, target, arrived.at[n])
        for n, (source, target) in enumerate(record_copies + gain_copies + rest_copies)
    ]
    for copy in copies:
        copy.start()
    for copy in copies[:PIECES]:
        copy.wait()
    largest = jnp.max(jnp.abs(own[...].astype(F32)), axis=0, keepdims=True)
    peak[...] = jnp.broadcast_to(jnp.max(largest, axis=1, keepdims=True), peak.shape)
    for copy in copies[PIECES : (1 + TAPS) * PIECES]:
        copy.wait()
    out[...] = product(own[...], gain_own)
    for copy in copies[(1 + TAPS) * PIECES :]:
        copy.wait()


def moved(delay, rows, ahead, values):
    shape = (rows, values.shape[0])
    row = lax.broadcasted_iota(jnp.int32, shape, 0)
    column = lax.broadcasted_iota(jnp.int32, shape, 1)
    pick = (column + delay[:, : shape[1]] == row + ahead).astype(F32)
    return jnp.dot(
        pick, values, precision=lax.Precision.HIGHEST, preferred_element_type=F32
    )


def onward_body(delays, other, gain, part, out):
    modes = gain.shape[1]
    at = part.shape[0] - DMAX
    u = part[at:] + product(other[at:], gain)
    total = jnp.zeros(out.shape, F32)
    for k in range(TAPS):
        total += moved(delays[k : k + 1], DMAX, DMAX, u[:, k * modes : (k + 1) * modes])
    out[...] = total


def here_body(delays, other, gain, part, onward, out):
    modes = gain.shape[1]
    u = part[...] + product(other[...], gain)
    total = jnp.zeros(out.shape, F32)
    for k in range(TAPS):
        total += moved(delays[k : k + 1], u.shape[0], 0, u[:, k * modes : (k + 1) * modes])
    out[...] = total


def local_body(here, tail, decay_ref, scale, leak, by_sensor, peak, keep, sent):
    frames, modes = decay_ref.shape
    nothing = jnp.zeros((frames - DMAX, modes), F32)
    drive_in = here[...] + jnp.concatenate([tail[...], nothing], 0)
    drive = scale[...] * drive_in
    decay = decay_ref[...]
    prods, (offsets,) = recur(decay, [drive], later)
    kappa = 1.0 - leak[...]
    weight = 1.0 - kappa * decay * decay
    links, (base, slope) = recur(kappa * decay, [weight * offsets, weight * prods], earlier)
    keep[0] = prods
    keep[1] = offsets
    keep[2] = links
    keep[3] = base
    keep[4] = slope
    keep[5] = drive
    rows = [prods[-1:], offsets[-1:], links[:1], base[:1], slope[:1], decay[-1:]]
    rows += [jnp.max(jnp.abs(offsets), axis=0, keepdims=True), peak[:1]]
    rest = jnp.concatenate(rows, 0)
    frames_rows = by_sensor.shape[1]
    parts = []
    for _ in range(3):
        part = rest.astype(BF16)
        parts.append(part.astype(F32))
        rest = rest - parts[-1]
    coded = jnp.concatenate(parts, 0).astype(BF16)
    for i in range(sent.shape[0]):
        sent[i, :frames_rows] = by_sensor[i]
        sent[i, frames_rows:] = coded


def decoded(every, out):
    at = every.shape[1] - 24
    for i in range(every.shape[0]):
        rows = every[i, at:].astype(F32)
        out[i] = rows[:8] + rows[8:16] + rows[16:]


def joined(first, second):
    p1, o1, l1, b1, s1 = first
    p2, o2, l2, b2, s2 = second
    return (p1 * p2, p2 * o1 + o2, l1 * l2, b1 + l1 * (b2 + s2 * o1), s1 + l1 * s2 * p1)


def five(ref, i):
    return tuple(ref[i, r : r + 1] for r in range(5))


def plane_body(sent, every, out):
    n = sent.shape[0]
    decoded(sent, every)
    parts = [five(every, i) for i in range(n)]
    while len(parts) > 1:
        parts = [joined(parts[i], parts[i + 1]) for i in range(0, len(parts), 2)]
    reach = every[0, 6:7]
    peak = every[0, 7:8]
    spread = jnp.abs(every[0, 1:2])
    for i in range(1, n):
        reach = jnp.maximum(reach, every[i, 6:7])
        peak = jnp.maximum(peak, every[i, 7:8])
        spread += jnp.abs(every[i, 1:2])
    reach += spread
    rows = list(parts[0]) + [every[n - 1, 5:6], reach, peak]
    for r, row in enumerate(rows):
        for i in range(out.shape[0]):
            out[i, r : r + 1] = row


def ends(every, position, entering, closing, last):
    n = every.shape[0]
    states = []
    state = entering
    before = last
    own_state = jnp.zeros_like(entering)
    own_last = jnp.zeros_like(entering)
    for i in range(n):
        states.append(state)
        own_state = jnp.where(position == i, state, own_state)
        own_last = jnp.where(position == i, before, own_last)
        state = every[i, 0:1] * state + every[i, 1:2]
        before = every[i, 5:6]
    after = closing
    afters = [after] * n
    own_after = jnp.zeros_like(entering)
    for i in reversed(range(n)):
        afters[i] = after
        own_after = jnp.where(position == i, after, own_after)
        after = every[i, 2:3] * after + every[i, 3:4] + every[i, 4:5] * states[i]
    return own_state, own_after, own_last, states, afters


def finish_body(plane, planes, keep, decay_ref, leak, smoothed_out, resid_out):
    at_plane = lax.axis_index(Z)
    at_block = lax.axis_index(YX)
    zero = jnp.zeros((1, decay_ref.shape[1]), F32)
    entering, after, last, _, _ = ends(planes, at_plane, zero, zero, zero)
    entering, after, last, _, _ = ends(plane, at_block, entering, after, last)
    smoothed = keep[3] + keep[4] * entering + keep[2] * after
    decay = decay_ref[...]
    kappa = 1.0 - leak[...]
    prior = (1.0 - kappa * last * last) * entering + kappa * last * smoothed[:1]
    first = jnp.logical_and(at_plane == 0, at_block == 0)
    prior = jnp.where(first, 0.0, prior)
    row = lax.broadcasted_iota(jnp.int32, smoothed.shape, 0)
    shifted = jnp.where(row == 0, prior, pltpu.roll(smoothed, 1, 0))
    resid = (smoothed - decay * shifted - keep[5]).astype(BF16)
    smoothed_out[...] = smoothed.T
    for i in range(resid_out.shape[0]):
        resid_out[i] = resid


def reach_body(planes, resid, reach):
    zero = jnp.zeros((1, planes.shape[2]), F32)
    _, _, _, states, afters = ends(planes, 0, zero, zero, zero)
    peaks = [zero]
    bound = []
    for i in range(planes.shape[0]):
        bound.append(6.0 * (planes[i, 6:7] + jnp.abs(states[i])) + 2.0 * jnp.abs(afters[i]))
        peaks.append(planes[i, 7:8])
    bound = jnp.concatenate(bound, 0)
    reach[0] = jnp.broadcast_to(jnp.max(bound, axis=1, keepdims=True), bound.shape)
    reach[1] = jnp.maximum(jnp.concatenate(peaks[:-1], 0), jnp.concatenate(peaks[1:], 0))


def bounds(first, second, span):
    return jnp.maximum(span * first[0] * jnp.maximum(first[1], second[1]), 1e-30)


def gradient_body(delays, tails, own, other, resid, reach, reach_other, out, padded):
    blocks, frames, modes = resid.shape
    row = lax.broadcasted_iota(jnp.int32, (frames, 2 * frames), 0)
    column = lax.broadcasted_iota(jnp.int32, (frames, 2 * frames), 1)
    picks = jnp.concatenate(
        [(column == row + delays[k : k + 1, : 2 * frames]).astype(F32).astype(BF16) for k in range(TAPS)], 0
    )
    nothing = jnp.zeros((frames, modes), BF16)
    for b in range(blocks + 1):
        pair = jnp.concatenate(
            [resid[b - 1] if b > 0 else nothing, resid[b] if b < blocks else nothing], 0
        )
        moved = jnp.dot(picks, pair, preferred_element_type=F32).astype(BF16)
        for k in range(TAPS):
            padded[b * frames : (b + 1) * frames, k * modes : (k + 1) * modes] = moved[
                k * frames : (k + 1) * frames
            ]
    rhs = padded[...]
    bound = bounds(reach, reach_other, float(blocks * frames))
    plane = lax.broadcasted_iota(jnp.int32, bound.shape, 0)
    factor = jnp.sum(jnp.where(plane == lax.axis_index(Z), TOP / bound, 0.0), axis=0, keepdims=True)
    factor = jnp.concatenate([factor] * TAPS, 1)
    for which, (before, rows) in enumerate(((tails[0], own), (tails[1], other))):
        lhs = jnp.concatenate(
            [before] + [rows[i, : before.shape[0]] for i in range(blocks)], 1
        )
        sums = jnp.dot(lhs, rhs, preferred_element_type=F32) * factor
        half = jnp.where(lax.axis_index("state") == which, 0, 1)
        for i in range(out.shape[1]):
            out[half, i] = sums[i * 8 : (i + 1) * 8]


def total_body(pieces, reach, reach_other, out, *, span):
    modes = out.shape[1] // TAPS // 2
    pair = (bounds(reach, reach_other, span) / TOP, bounds(reach_other, reach, span) / TOP)
    for core in range(2):
        factor = jnp.where(lax.axis_index("state") == core, pair[0], pair[1])
        factor = jnp.concatenate([factor] * TAPS, 1)
        planes = factor.shape[0]
        total = pieces[core * planes] * factor[:1]
        for i in range(1, planes):
            total += pieces[core * planes + i] * factor[i : i + 1]
        for k in range(TAPS):
            column = (2 * k + core) * modes
            out[:, column : column + modes] = total[:, k * modes : (k + 1) * modes]


def behind(x, first):
    return lax.optimization_barrier((x, first))[0]


def swapped(x):
    return lax.ppermute(x, "state", [(0, 1), (1, 0)])


def per_device(record, gain, rate, leak, dilation):
    frames, sensors = record.shape
    modes = rate.shape[0]
    planes = lax.axis_size(Z)
    blocks = lax.axis_size(YX)
    delays = jnp.broadcast_to(dilation[:, None], (TAPS, 2 * frames))
    other = swapped(record)
    group = sensors // planes // blocks
    both = jax.ShapeDtypeStruct((frames, TAPS * modes), F32)
    half_gain = (TAPS, modes, sensors)
    part, gain_rest, peak = call(
        own_body,
        (
            both,
            jax.ShapeDtypeStruct(half_gain, BF16),
            jax.ShapeDtypeStruct((8, modes), F32),
        ),
        scratch=[
            pltpu.VMEM((frames, sensors), BF16),
            pltpu.VMEM(half_gain, BF16),
            pltpu.SemaphoreType.DMA(((1 + 2 * TAPS) * PIECES,)),
        ],
        whole=(0, 1),
        n_in=2,
    )(*(pltpu.with_memory_space_constraint(x, pltpu.HBM) for x in (record, gain)))
    onward = call(onward_body, jax.ShapeDtypeStruct((DMAX, modes), F32), n_in=4)(
        delays, other, gain_rest, part
    )
    here = call(here_body, jax.ShapeDtypeStruct((frames, modes), F32), n_in=5)(
        delays, other, gain_rest, part, onward
    )
    tail = lax.ppermute(onward, TM, [(i, i + 1) for i in range(planes * blocks - 1)])
    rate_t = behind(rate, here).T
    decay = jnp.exp(-rate_t)
    scale = jnp.sqrt(-jnp.expm1(-2.0 * rate_t))
    leak_row = leak[None]
    by_sensor = behind(record, here).T.reshape(planes, blocks, group, frames).swapaxes(0, 1)
    by_sensor = by_sensor.reshape(blocks, planes * group, frames)
    keep, sent = call(
        local_body,
        (
            jax.ShapeDtypeStruct((6, frames, modes), F32),
            jax.ShapeDtypeStruct((blocks, planes * group + 24, frames), BF16),
        ),
        n_in=7,
    )(here, tail, decay, scale, leak_row, by_sensor, peak)
    mine = lax.all_to_all(sent, YX, 0, 0, tiled=True)
    plane, plane_summary = call(
        plane_body,
        (
            jax.ShapeDtypeStruct((blocks, 8, modes), F32),
            jax.ShapeDtypeStruct((planes, 8, modes), F32),
        ),
        n_in=1,
    )(mine)
    theirs = swapped(mine[:, :-24])
    every_plane = lax.all_to_all(plane_summary, Z, 0, 0, tiled=True)
    smoothed, resid = call(
        finish_body,
        (
            jax.ShapeDtypeStruct((modes, frames), F32),
            jax.ShapeDtypeStruct((blocks, frames, modes), BF16),
        ),
        n_in=5,
    )(plane, every_plane, keep, decay, leak_row)
    resid_all = lax.all_to_all(resid, YX, 0, 0, tiled=True)
    tails = behind(jnp.stack([mine[-1, :-24], theirs[-1]]), resid)
    tails = lax.ppermute(tails, Z, [(i, i + 1) for i in range(planes - 1)])
    reach = call(reach_body, jax.ShapeDtypeStruct((2, planes, modes), F32), whole=(1,), n_in=2)(
        every_plane, resid
    )
    reach_other = swapped(reach)
    partial = call(
        gradient_body,
        jax.ShapeDtypeStruct((2, planes, group, TAPS * modes), F32),
        scratch=[pltpu.VMEM(((blocks + 1) * frames, TAPS * modes), BF16)],
        n_in=7,
    )(delays, tails, mine, theirs, resid_all, reach, reach_other)
    pieces = partial.reshape(planes * 2, group, TAPS * modes).astype(jnp.float16)
    pieces = lax.all_to_all(pieces, ("state", Z), 0, 0, tiled=True)
    grad = call(
        functools.partial(total_body, span=float(blocks * frames)),
        jax.ShapeDtypeStruct((group, TAPS * 2 * modes), F32),
        n_in=3,
    )(pieces.astype(F32), reach, reach_other)
    return (smoothed, grad)


def solution(mesh):
    split = Mesh(
        mesh.devices.reshape(16, 4, 4, mesh.shape["state"]), ("tm_0", "tm_1", "tm_2", "state")
    )
    return jax.shard_map(
        per_device,
        mesh=split,
        in_specs=(P(TM, "state"), P(None, "state", None), P("state", TM), P("state"), P()),
        out_specs=(P("state", TM), P(STATE_TM, None)),
        check_vma=False,
    )
```

```python
import functools

import jax
import jax.numpy as jnp
from jax import lax
from jax.experimental import pallas as pl
from jax.experimental.pallas import tpu as pltpu
from jax.sharding import Mesh
from jax.sharding import PartitionSpec as P

TAPS = 2
TOP = 32768.0
PIECES = 1
DMAX = 64
Z = "tm_0"
YX = ("tm_1", "tm_2")
TM = ("tm_0", "tm_1", "tm_2")
STATE_TM = ("state", "tm_0", "tm_1", "tm_2")
F32 = jnp.float32
BF16 = jnp.bfloat16
VMEM = pl.BlockSpec(memory_space=pltpu.VMEM)
WHOLE = pl.BlockSpec(memory_space=pltpu.HBM)
NT = (((1,), (1,)), ((), ()))


def call(body, outs, scratch=(), whole=(), n_in=1):
    specs = [WHOLE if i in whole else VMEM for i in range(n_in)]
    return pl.pallas_call(
        body,
        out_shape=outs,
        in_specs=specs,
        out_specs=jax.tree.map(lambda _: VMEM, outs),
        scratch_shapes=scratch,
        compiler_params=pltpu.CompilerParams(vmem_limit_bytes=48 << 20),
    )


def later(x, k, fill):
    if k % 8 == 0:
        return jnp.concatenate([jnp.full((k, x.shape[1]), fill, x.dtype), x[:-k]], 0)
    row = lax.broadcasted_iota(jnp.int32, x.shape, 0)
    return jnp.where(row < k, fill, pltpu.roll(x, k, 0))


def earlier(x, k, fill):
    n = x.shape[0]
    if k % 8 == 0:
        return jnp.concatenate([x[k:], jnp.full((k, x.shape[1]), fill, x.dtype)], 0)
    row = lax.broadcasted_iota(jnp.int32, x.shape, 0)
    return jnp.where(row >= n - k, fill, pltpu.roll(x, n - k, 0))


def recur(link, sums, shift):
    k = 1
    while k < link.shape[0]:
        sums = [s + link * shift(s, k, 0.0) for s in sums]
        link = link * shift(link, k, 1.0)
        k *= 2
    return link, sums


def product(rows, gain):
    both = gain[...].reshape(TAPS * gain.shape[1], gain.shape[2])
    return lax.dot_general(rows, both, NT, preferred_element_type=F32)


def own_body(record, gain, out, gain_rest, peak, own, gain_own, arrived):
    modes = gain_own.shape[1]
    frames, half = own.shape
    core = lax.axis_index("state")
    mine = pl.multiple_of(core * half, half)
    theirs = pl.multiple_of((1 - core) * half, half)
    record_copies = []
    gain_copies = []
    rest_copies = []
    for piece in range(PIECES):
        rows = pl.ds(piece * (frames // PIECES), frames // PIECES)
        record_copies.append((record.at[rows], own.at[rows]))
    for k in range(TAPS):
        for piece in range(PIECES):
            rows = pl.ds(piece * (modes // PIECES), modes // PIECES)
            gain_copies.append((gain.at[k, rows, pl.ds(mine, half)], gain_own.at[k, rows]))
            rest_copies.append((gain.at[k, rows, pl.ds(theirs, half)], gain_rest.at[k, rows]))
    copies = [
        pltpu.make_async_copy(source, target, arrived.at[n])
        for n, (source, target) in enumerate(record_copies + gain_copies + rest_copies)
    ]
    for copy in copies:
        copy.start()
    for copy in copies[:PIECES]:
        copy.wait()
    largest = jnp.max(jnp.abs(own[...].astype(F32)), axis=0, keepdims=True)
    peak[...] = jnp.broadcast_to(jnp.max(largest, axis=1, keepdims=True), peak.shape)
    for copy in copies[PIECES : (1 + TAPS) * PIECES]:
        copy.wait()
    out[...] = product(own[...], gain_own)
    for copy in copies[(1 + TAPS) * PIECES :]:
        copy.wait()


def moved(delay, rows, ahead, values):
    shape = (rows, values.shape[0])
    row = lax.broadcasted_iota(jnp.int32, shape, 0)
    column = lax.broadcasted_iota(jnp.int32, shape, 1)
    pick = (column + delay[:, : shape[1]] == row + ahead).astype(F32).astype(BF16)
    parts = []
    for _ in range(3):
        parts.append(values.astype(BF16))
        values = values - parts[-1].astype(F32)
    sums = jnp.dot(pick, jnp.concatenate(parts, 1), preferred_element_type=F32)
    wide = values.shape[1]
    return sums[:, :wide] + sums[:, wide : 2 * wide] + sums[:, 2 * wide :]


def onward_body(delays, other, gain, part, out):
    modes = gain.shape[1]
    at = part.shape[0] - DMAX
    u = part[at:] + product(other[at:], gain)
    total = jnp.zeros(out.shape, F32)
    for k in range(TAPS):
        total += moved(delays[k : k + 1], DMAX, DMAX, u[:, k * modes : (k + 1) * modes])
    out[...] = total


def here_body(delays, other, gain, part, onward, out):
    modes = gain.shape[1]
    u = part[...] + product(other[...], gain)
    total = jnp.zeros(out.shape, F32)
    for k in range(TAPS):
        total += moved(delays[k : k + 1], u.shape[0], 0, u[:, k * modes : (k + 1) * modes])
    out[...] = total


def local_body(here, tail, decay_ref, scale, leak, by_sensor, peak, keep, sent):
    frames, modes = decay_ref.shape
    nothing = jnp.zeros((frames - DMAX, modes), F32)
    drive_in = here[...] + jnp.concatenate([tail[...], nothing], 0)
    drive = scale[...] * drive_in
    decay = decay_ref[...]
    prods, (offsets,) = recur(decay, [drive], later)
    kappa = 1.0 - leak[...]
    weight = 1.0 - kappa * decay * decay
    links, (base, slope) = recur(kappa * decay, [weight * offsets, weight * prods], earlier)
    keep[0] = prods
    keep[1] = offsets
    keep[2] = links
    keep[3] = base
    keep[4] = slope
    keep[5] = drive
    rows = [prods[-1:], offsets[-1:], links[:1], base[:1], slope[:1], decay[-1:]]
    rows += [jnp.max(jnp.abs(offsets), axis=0, keepdims=True), peak[:1]]
    rest = jnp.concatenate(rows, 0)
    frames_rows = by_sensor.shape[1]
    parts = []
    for _ in range(3):
        part = rest.astype(BF16)
        parts.append(part.astype(F32))
        rest = rest - parts[-1]
    coded = jnp.concatenate(parts, 0).astype(BF16)
    for i in range(sent.shape[0]):
        sent[i, :frames_rows] = by_sensor[i]
        sent[i, frames_rows:] = coded


def decoded(every, out):
    at = every.shape[1] - 24
    for i in range(every.shape[0]):
        rows = every[i, at:].astype(F32)
        out[i] = rows[:8] + rows[8:16] + rows[16:]


def joined(first, second):
    p1, o1, l1, b1, s1 = first
    p2, o2, l2, b2, s2 = second
    return (p1 * p2, p2 * o1 + o2, l1 * l2, b1 + l1 * (b2 + s2 * o1), s1 + l1 * s2 * p1)


def five(ref, i):
    return tuple(ref[i, r : r + 1] for r in range(5))


def plane_body(sent, every, out):
    n = sent.shape[0]
    decoded(sent, every)
    parts = [five(every, i) for i in range(n)]
    while len(parts) > 1:
        parts = [joined(parts[i], parts[i + 1]) for i in range(0, len(parts), 2)]
    state = jnp.zeros_like(every[0, :1])
    reach = state
    peak = state
    for i in range(n):
        reach = jnp.maximum(reach, every[i, 6:7] + jnp.abs(state))
        peak = jnp.maximum(peak, every[i, 7:8])
        state = every[i, 0:1] * state + every[i, 1:2]
    rows = list(parts[0]) + [every[n - 1, 5:6], reach, peak]
    for r, row in enumerate(rows):
        for i in range(out.shape[0]):
            out[i, r : r + 1] = row


def ends(every, position, entering, closing, last):
    n = every.shape[0]
    states = []
    state = entering
    before = last
    own_state = jnp.zeros_like(entering)
    own_last = jnp.zeros_like(entering)
    for i in range(n):
        states.append(state)
        own_state = jnp.where(position == i, state, own_state)
        own_last = jnp.where(position == i, before, own_last)
        state = every[i, 0:1] * state + every[i, 1:2]
        before = every[i, 5:6]
    after = closing
    afters = [after] * n
    own_after = jnp.zeros_like(entering)
    for i in reversed(range(n)):
        afters[i] = after
        own_after = jnp.where(position == i, after, own_after)
        after = every[i, 2:3] * after + every[i, 3:4] + every[i, 4:5] * states[i]
    return own_state, own_after, own_last, states, afters


def finish_body(plane, planes, keep, decay_ref, leak, smoothed_out, resid_out, reach):
    at_plane = lax.axis_index(Z)
    at_block = lax.axis_index(YX)
    zero = jnp.zeros((1, decay_ref.shape[1]), F32)
    entering, after, last, states, afters = ends(planes, at_plane, zero, zero, zero)
    peaks = [zero]
    bound = []
    for i in range(planes.shape[0]):
        bound.append(6.0 * (planes[i, 6:7] + jnp.abs(states[i])) + 2.0 * jnp.abs(afters[i]))
        peaks.append(planes[i, 7:8])
    bound = jnp.concatenate(bound, 0)
    reach[0] = jnp.broadcast_to(jnp.max(bound, axis=1, keepdims=True), bound.shape)
    reach[1] = jnp.maximum(jnp.concatenate(peaks[:-1], 0), jnp.concatenate(peaks[1:], 0))
    entering, after, last, _, _ = ends(plane, at_block, entering, after, last)
    smoothed = keep[3] + keep[4] * entering + keep[2] * after
    decay = decay_ref[...]
    kappa = 1.0 - leak[...]
    prior = (1.0 - kappa * last * last) * entering + kappa * last * smoothed[:1]
    first = jnp.logical_and(at_plane == 0, at_block == 0)
    prior = jnp.where(first, 0.0, prior)
    row = lax.broadcasted_iota(jnp.int32, smoothed.shape, 0)
    shifted = jnp.where(row == 0, prior, pltpu.roll(smoothed, 1, 0))
    resid = (smoothed - decay * shifted - keep[5]).astype(BF16)
    smoothed_out[...] = smoothed.T
    for i in range(resid_out.shape[0]):
        resid_out[i] = resid


def bounds(first, second, span):
    return jnp.maximum(span * first[0] * jnp.maximum(first[1], second[1]), 1e-30)


def gradient_body(delays, tails, own, other, resid, reach, reach_other, out, padded):
    blocks, frames, modes = resid.shape
    row = lax.broadcasted_iota(jnp.int32, (frames, 2 * frames), 0)
    column = lax.broadcasted_iota(jnp.int32, (frames, 2 * frames), 1)
    picks = jnp.concatenate(
        [(column == row + delays[k : k + 1, : 2 * frames]).astype(F32).astype(BF16) for k in range(TAPS)], 0
    )
    nothing = jnp.zeros((frames, modes), BF16)
    for b in range(blocks + 1):
        pair = jnp.concatenate(
            [resid[b - 1] if b > 0 else nothing, resid[b] if b < blocks else nothing], 0
        )
        moved = jnp.dot(picks, pair, preferred_element_type=F32).astype(BF16)
        for k in range(TAPS):
            padded[b * frames : (b + 1) * frames, k * modes : (k + 1) * modes] = moved[
                k * frames : (k + 1) * frames
            ]
    rhs = padded[...]
    bound = bounds(reach, reach_other, float(blocks * frames))
    plane = lax.broadcasted_iota(jnp.int32, bound.shape, 0)
    factor = jnp.sum(jnp.where(plane == lax.axis_index(Z), TOP / bound, 0.0), axis=0, keepdims=True)
    factor = jnp.concatenate([factor] * TAPS, 1)
    for which, (before, rows) in enumerate(((tails[0], own), (tails[1], other))):
        lhs = jnp.concatenate(
            [before] + [rows[i, : before.shape[0]] for i in range(blocks)], 1
        )
        sums = jnp.dot(lhs, rhs, preferred_element_type=F32) * factor
        half = jnp.where(lax.axis_index("state") == which, 0, 1)
        for i in range(out.shape[1]):
            out[half, i] = sums[i * 8 : (i + 1) * 8]


def total_body(pieces, reach, reach_other, out, *, span):
    modes = out.shape[1] // TAPS // 2
    pair = (bounds(reach, reach_other, span) / TOP, bounds(reach_other, reach, span) / TOP)
    for core in range(2):
        factor = jnp.where(lax.axis_index("state") == core, pair[0], pair[1])
        factor = jnp.concatenate([factor] * TAPS, 1)
        planes = factor.shape[0]
        total = pieces[core * planes] * factor[:1]
        for i in range(1, planes):
            total += pieces[core * planes + i] * factor[i : i + 1]
        for k in range(TAPS):
            column = (2 * k + core) * modes
            out[:, column : column + modes] = total[:, k * modes : (k + 1) * modes]


def behind(x, first):
    return lax.optimization_barrier((x, first))[0]


def swapped(x):
    return lax.ppermute(x, "state", [(0, 1), (1, 0)])


def per_device(record, gain, rate, leak, dilation):
    frames, sensors = record.shape
    modes = rate.shape[0]
    planes = lax.axis_size(Z)
    blocks = lax.axis_size(YX)
    delays = jnp.broadcast_to(dilation[:, None], (TAPS, 2 * frames))
    other = swapped(record)
    group = sensors // planes // blocks
    both = jax.ShapeDtypeStruct((frames, TAPS * modes), F32)
    half_gain = (TAPS, modes, sensors)
    part, gain_rest, peak = call(
        own_body,
        (
            both,
            jax.ShapeDtypeStruct(half_gain, BF16),
            jax.ShapeDtypeStruct((8, modes), F32),
        ),
        scratch=[
            pltpu.VMEM((frames, sensors), BF16),
            pltpu.VMEM(half_gain, BF16),
            pltpu.SemaphoreType.DMA(((1 + 2 * TAPS) * PIECES,)),
        ],
        whole=(0, 1),
        n_in=2,
    )(*(pltpu.with_memory_space_constraint(x, pltpu.HBM) for x in (record, gain)))
    onward = call(onward_body, jax.ShapeDtypeStruct((DMAX, modes), F32), n_in=4)(
        delays, other, gain_rest, part
    )
    here = call(here_body, jax.ShapeDtypeStruct((frames, modes), F32), n_in=5)(
        delays, other, gain_rest, part, onward
    )
    tail = lax.ppermute(onward, TM, [(i, i + 1) for i in range(planes * blocks - 1)])
    rate_t = behind(rate, here).T
    decay = jnp.exp(-rate_t)
    scale = jnp.sqrt(-jnp.expm1(-2.0 * rate_t))
    leak_row = leak[None]
    by_sensor = behind(record, here).T.reshape(planes, blocks, group, frames).swapaxes(0, 1)
    by_sensor = by_sensor.reshape(blocks, planes * group, frames)
    keep, sent = call(
        local_body,
        (
            jax.ShapeDtypeStruct((6, frames, modes), F32),
            jax.ShapeDtypeStruct((blocks, planes * group + 24, frames), BF16),
        ),
        n_in=7,
    )(here, tail, decay, scale, leak_row, by_sensor, peak)
    mine = lax.all_to_all(sent, YX, 0, 0, tiled=True)
    plane, plane_summary = call(
        plane_body,
        (
            jax.ShapeDtypeStruct((blocks, 8, modes), F32),
            jax.ShapeDtypeStruct((planes, 8, modes), F32),
        ),
        n_in=1,
    )(mine)
    theirs = swapped(mine[:, :-24])
    every_plane = lax.all_to_all(plane_summary, Z, 0, 0, tiled=True)
    smoothed, resid, reach = call(
        finish_body,
        (
            jax.ShapeDtypeStruct((modes, frames), F32),
            jax.ShapeDtypeStruct((blocks, frames, modes), BF16),
            jax.ShapeDtypeStruct((2, planes, modes), F32),
        ),
        n_in=5,
    )(plane, every_plane, keep, decay, leak_row)
    resid_all = lax.all_to_all(resid, YX, 0, 0, tiled=True)
    tails = behind(jnp.stack([mine[-1, :-24], theirs[-1]]), resid)
    tails = lax.ppermute(tails, Z, [(i, i + 1) for i in range(planes - 1)])
    reach_other = swapped(reach)
    partial = call(
        gradient_body,
        jax.ShapeDtypeStruct((2, planes, group, TAPS * modes), F32),
        scratch=[pltpu.VMEM(((blocks + 1) * frames, TAPS * modes), BF16)],
        n_in=7,
    )(delays, tails, mine, theirs, resid_all, reach, reach_other)
    pieces = partial.reshape(planes * 2, group, TAPS * modes).astype(jnp.float16)
    pieces = lax.all_to_all(pieces, ("state", Z), 0, 0, tiled=True)
    grad = call(
        functools.partial(total_body, span=float(blocks * frames)),
        jax.ShapeDtypeStruct((group, TAPS * 2 * modes), F32),
        n_in=3,
    )(pieces.astype(F32), reach, reach_other)
    return (smoothed, grad)


def solution(mesh):
    split = Mesh(
        mesh.devices.reshape(16, 4, 4, mesh.shape["state"]), ("tm_0", "tm_1", "tm_2", "state")
    )
    return jax.shard_map(
        per_device,
        mesh=split,
        in_specs=(P(TM, "state"), P(None, "state", None), P("state", TM), P("state"), P()),
        out_specs=(P("state", TM), P(STATE_TM, None)),
        check_vma=False,
    )
```
